32 devices in a mesh: row: 16 (over z, y, core), col: 2 (over x).
Axes of the slice: x: 2, y: 2, z: 4, core: 2. Of those that a mesh axis runs over, the one named last changes fastest.
Arguments:
- layer_input: bfloat16 [16384, 1152], P(('row', 'col')), may hold values from -6 to 6
- attn_gain: bfloat16 [1152], replicated, may hold values from 0.099609375 to 1.8984375
- mlp_gain: bfloat16 [1152], replicated, may hold values from 0.099609375 to 1.8984375
- query_weight: bfloat16 [1152, 1152], P('row', 'col'), may hold values from -0.1875 to 0.1875
- key_weight: bfloat16 [1152, 384], P('row', 'col'), may hold values from -0.1875 to 0.1875
- value_weight: bfloat16 [1152, 384], P('row', 'col'), may hold values from -0.1875 to 0.1875
- out_weight: bfloat16 [1152, 1152], P('col', 'row'), may hold values from -4 to 4
- gate_weight: bfloat16 [1152, 3072], P('row', 'col'), may hold values from -0.1875 to 0.1875
- up_weight: bfloat16 [1152, 3072], P('row', 'col'), may hold values from -0.1875 to 0.1875
- down_weight: bfloat16 [3072, 1152], P('col', 'row'), may hold values from -0.109375 to 0.109375
- seq_ids: int32 [16384], P('row'), may hold values from 0 to 31, as said below
- block_ends: int32 [16384], P('row'), may hold values from 255 to 16383, as said below
- grad_output: bfloat16 [16384, 1152], P(('row', 'col')), may hold values from -6 to 6
Outputs:
- layer_output: bfloat16 [16384, 1152], P(('row', 'col'))
- grad_input: bfloat16 [16384, 1152], P(('row', 'col'))
- grad_attn_gain: float32 [1152], replicated
- grad_mlp_gain: float32 [1152], replicated
- grad_query: float32 [1152, 1152], P('row', 'col')
- grad_key: float32 [1152, 384], P('row', 'col')
- grad_value: float32 [1152, 384], P('row', 'col')
- grad_out_weight: float32 [1152, 1152], P('col', 'row')
- grad_gate: float32 [1152, 3072], P('row', 'col')
- grad_up: float32 [1152, 3072], P('row', 'col')
- grad_down: float32 [3072, 1152], P('col', 'row')
The draws below stay inside these ranges and needn't reach their ends.
Inputs may be any that keep to these rules, and one draw needn't show every extreme that they name: `seq_ids`: ids never fall; span number s of the aligned spans of 1024 tokens holds exactly two sequences, with ids 2 * s and 2 * s + 1, each of 256 tokens or more. `block_ends`: values never fall; an attention block is a run of 1 to 256 tokens inside one sequence, and the first block of every sequence has exactly 256 tokens.
All inputs are finite; a program needn't handle non-finite values.
Results may differ from the reference program's by a relative error of at most 0.014.
The reference program's roundings to bfloat16 on the way count: a program that leaves them out, or rounds other values in their place, can miss the bound.
Values may be sent and summed in bfloat16 or wider, within the bound.
A program may use at most 192 MiB of HBM per device.

```python
import math
import jax
import jax.numpy as jnp
from jax import lax

D = 1152
QUERY_HEADS = 18
KEY_VALUE_HEADS = 6
HEAD_SIZE_DIM = 64
FF = 3072
TOK_ROW = 1024
BLOCK = 256
QW = 1152
KW = 384
TOKENS = 16384


cut_odds = 128


def sequence_layout(key):
    span_count = TOKENS // TOK_ROW
    cut_points = jax.random.randint(jax.random.fold_in(key, 11), (span_count,), TOK_ROW // 4, 3 * TOK_ROW // 4 + 1)
    offsets = jnp.arange(TOK_ROW, dtype=jnp.int32)
    second = (offsets[None, :] >= cut_points[:, None]).astype(jnp.int32)
    return (2 * jnp.arange(span_count, dtype=jnp.int32)[:, None] + second).reshape(TOKENS).astype(jnp.int32)


def draw_seq_ids(key, part):
    return sequence_layout(key)


def draw_block_ends(key, part):
    sequence = sequence_layout(key)
    token_index = jnp.arange(TOKENS, dtype=jnp.int32)
    earlier = jnp.concatenate([sequence[:1] - 1, sequence[:-1]])
    is_first = sequence != earlier
    seq_start = lax.cummax(jnp.where(is_first, token_index, 0), axis=0)
    position = token_index - seq_start
    extra_cut = jax.random.randint(jax.random.fold_in(key, 12), (TOKENS,), 0, cut_odds) == 0
    starts = is_first | (position % BLOCK == 0) | extra_cut & (position >= BLOCK)
    is_last = jnp.concatenate([starts[1:], jnp.ones((1,), dtype=jnp.bool_)])
    return lax.cummin(jnp.where(is_last, token_index, TOKENS), axis=0, reverse=True).astype(jnp.int32)


def raised(entries, rng, source, target, shards_of, factor):
    owner, partner = [(jnp.arange(entries.shape[axis_at]) // (entries.shape[axis_at] // shards_of)).reshape([-1 if axis == axis_at else 1 for axis in range(entries.ndim)]) for axis_at in (source, target)]
    chosen = jax.random.permutation(rng, shards_of)[partner]
    strong = (owner == chosen) | (owner == (partner + shards_of // 2) % shards_of)
    return jnp.where(strong, factor * entries, entries)


def steps_of(rng, shape, shards, smallest, top_value):
    gain = 1.0
    for dim, parts in shards:
        draws = jax.random.uniform(jax.random.fold_in(jax.random.fold_in(rng, 6), dim), (parts,), jnp.float32, smallest / len(shards), top_value / len(shards))
        gain = gain * jnp.repeat(jnp.exp(draws), shape[dim] // parts).reshape((-1,) + (1,) * (len(shape) - 1 - dim))
    return gain


def normal_values(key, shape, scale, reach, split=(), kind=jnp.bfloat16):
    result = scale * jax.random.normal(key, shape, jnp.float32)
    if split:
        result = result * steps_of(key, shape, split, -0.22, 0.18)
    return jnp.clip(result, -reach, reach).astype(kind)


def heavy_noise(own_key, shape, scale, most, cuts, heavy, held_as=jnp.bfloat16):
    array = scale * jax.random.normal(own_key, shape, jnp.float32)
    if cuts:
        array = array * steps_of(own_key, shape, cuts, -0.22, 0.18)
    return jnp.clip(raised(array, jax.random.fold_in(own_key, 3), *heavy), -most, most).astype(held_as)


def setup_inputs(seed: int = 0) -> dict:
    key_of = jax.random.split(jax.random.key(seed), 14)
    layer_input = heavy_noise(key_of[0], (TOKENS, D), 1.0, 6.0, ((0, 32),), (0, 1, 32, 2.75))
    attn_gain = jnp.clip(1.0 + 0.18 * jax.random.normal(key_of[1], (D,), jnp.float32), 0.099609375, 1.8984375).astype(jnp.bfloat16)
    mlp_gain = jnp.clip(1.0 + 0.18 * jax.random.normal(key_of[2], (D,), jnp.float32), 0.099609375, 1.8984375).astype(jnp.bfloat16)
    query_weight = normal_values(key_of[3], (D, QW), D ** -0.5, 0.1875, ((0, 16), (1, 2)))
    key_weight = normal_values(key_of[4], (D, KW), D ** -0.5, 0.1875, ((0, 16), (1, 2)))
    value_weight = normal_values(key_of[5], (D, KW), D ** -0.5, 0.1875, ((0, 16), (1, 2)))
    out_weight = normal_values(key_of[6], (QW, D), 2 ** -0.5, 4.0, ((0, 2), (1, 16)))
    gate_weight = normal_values(key_of[7], (D, FF), D ** -0.5, 0.1875, ((0, 16), (1, 2)))
    up_weight = normal_values(key_of[8], (D, FF), D ** -0.5, 0.1875, ((0, 16), (1, 2)))
    down_weight = normal_values(key_of[9], (FF, D), FF ** -0.5, 0.109375, ((0, 2), (1, 16)))
    seq_ids = draw_seq_ids(jax.random.fold_in(key_of[13], 71), 0)
    block_ends = draw_block_ends(jax.random.fold_in(key_of[13], 71), 0)
    grad_output = heavy_noise(key_of[12], (TOKENS, D), 1.0, 6.0, ((0, 32),), (0, 1, 32, 2.75))
    return dict(layer_input=layer_input, attn_gain=attn_gain, mlp_gain=mlp_gain, query_weight=query_weight, key_weight=key_weight, value_weight=value_weight, out_weight=out_weight, gate_weight=gate_weight, up_weight=up_weight, down_weight=down_weight, seq_ids=seq_ids, block_ends=block_ends, grad_output=grad_output)


eps = 1e-05
rope_base = 10000.0
neg_fill = -1e+30

@jax.custom_vjp
def lower_precision(v):
    return lax.optimization_barrier(v.astype(jnp.bfloat16)).astype(jnp.float32)

@jax.custom_vjp
def lower_backward(v):
    return v

def low_keep(v):
    return (lower_precision(v), None)

def low_pass(kept, grad):
    return (grad,)

def back_keep(v):
    return (v, None)

def back_low(kept, grad):
    return (lower_precision(grad),)
lower_precision.defvjp(low_keep, low_pass)
lower_backward.defvjp(back_keep, back_low)

def product(operand_a, operand_b):
    return jnp.dot(operand_a, operand_b, precision=lax.Precision.HIGHEST, preferred_element_type=jnp.float32)

def rms_scale(values):
    return lax.rsqrt(lax.optimization_barrier(jnp.mean(values * values, axis=-1, keepdims=True)) + eps)

def rotate_half(values, head_size):
    lane_index = jnp.arange(values.shape[-1], dtype=jnp.int32) % head_size
    forward_roll = jnp.roll(values, -(head_size // 2), axis=-1)
    backward_roll = jnp.roll(values, head_size // 2, axis=-1)
    return jnp.where(lane_index < head_size // 2, -forward_roll, backward_roll)

def rope_tables(position, table_width, head_size):
    lane_index = (jnp.arange(table_width, dtype=jnp.int32) % (head_size // 2)).astype(jnp.float32)
    frequency = jnp.exp(lane_index * (-2.0 * math.log(rope_base) / head_size))
    angles = position[:, None] * frequency[None, :]
    return (jnp.cos(angles), jnp.sin(angles))

def positions(seq_ids):
    token_index = jnp.arange(seq_ids.shape[0], dtype=jnp.int32)
    earlier = jnp.concatenate([seq_ids[:1] - 1, seq_ids[:-1]])
    seq_start = lax.cummax(jnp.where(seq_ids != earlier, token_index, 0), axis=0)
    return (token_index - seq_start).astype(jnp.float32)

def group_attention(grouped_query_head, key_group, value_group, allowed):
    total_row_count = grouped_query_head.shape[0]
    query_head_rows = grouped_query_head.reshape(total_row_count, QUERY_HEADS // KEY_VALUE_HEADS, HEAD_SIZE_DIM)
    scores = lower_backward(jnp.einsum('qhd,kd->hqk', query_head_rows, key_group, precision=lax.Precision.HIGHEST))
    scores = jnp.where(allowed[None], scores, neg_fill)
    row_top = lax.optimization_barrier(jnp.max(scores, axis=2, keepdims=True))
    powers = jnp.exp(scores - row_top)
    attn_probs = powers / lax.optimization_barrier(jnp.sum(powers, axis=2, keepdims=True))
    weighted_values = jnp.einsum('hqk,kd->qhd', lower_precision(attn_probs), value_group, precision=lax.Precision.HIGHEST)
    return weighted_values.reshape(total_row_count, grouped_query_head.shape[1])

def layer(inputs, attn_gain, mlp_gain, query_weight, key_weight, value_weight, out_weight, gate_weight, up_weight, down_weight, seq_ids, block_ends):
    attn_in = lower_precision(inputs * rms_scale(inputs) * attn_gain)
    query_unrotated = lower_backward(lower_precision(product(attn_in, query_weight)))
    key_raw = lower_backward(lower_precision(product(attn_in, key_weight)))
    value_projected = lower_backward(lower_precision(product(attn_in, value_weight)))
    position = positions(seq_ids)
    query_cos, query_sin = rope_tables(position, query_unrotated.shape[1], HEAD_SIZE_DIM)
    key_cos, key_sin = rope_tables(position, key_raw.shape[1], HEAD_SIZE_DIM)
    query_rotated = lower_precision((query_unrotated * query_cos + rotate_half(query_unrotated, HEAD_SIZE_DIM) * query_sin) * HEAD_SIZE_DIM ** (-0.5))
    key_rotated = lower_precision(key_raw * key_cos + rotate_half(key_raw, HEAD_SIZE_DIM) * key_sin)
    allowed = (seq_ids[:, None] == seq_ids[None, :]) & (block_ends[None, :] <= block_ends[:, None])
    total_row_count = inputs.shape[0]
    group_head_width = query_unrotated.shape[1] // KEY_VALUE_HEADS
    grouped_queries = jnp.transpose(query_rotated.reshape(total_row_count, KEY_VALUE_HEADS, group_head_width), (1, 0, 2))
    grouped_keys = jnp.transpose(key_rotated.reshape(total_row_count, KEY_VALUE_HEADS, HEAD_SIZE_DIM), (1, 0, 2))
    grouped_values = jnp.transpose(value_projected.reshape(total_row_count, KEY_VALUE_HEADS, HEAD_SIZE_DIM), (1, 0, 2))
    checked = jax.checkpoint(group_attention)
    weighted_values = lax.map(lambda scan_items: checked(scan_items[0], scan_items[1], scan_items[2], allowed), (grouped_queries, grouped_keys, grouped_values))
    weighted_values = lower_backward(lower_precision(jnp.transpose(weighted_values, (1, 0, 2)).reshape(total_row_count, KEY_VALUE_HEADS * group_head_width)))
    attn_branch = lower_backward(product(weighted_values, out_weight))
    residual = inputs + attn_branch
    mlp_in = lower_precision(residual * rms_scale(residual) * mlp_gain)
    gate_act = lower_backward(product(mlp_in, gate_weight))
    up_act = lower_backward(product(mlp_in, up_weight))
    hidden = lower_precision(jax.nn.silu(gate_act) * up_act)
    return residual + product(hidden, down_weight)

def reference(layer_input, attn_gain, mlp_gain, query_weight, key_weight, value_weight, out_weight, gate_weight, up_weight, down_weight, seq_ids, block_ends, grad_output):
    span_count = layer_input.shape[0] // TOK_ROW
    model_width = layer_input.shape[1]
    params = tuple((weight_arg.astype(jnp.float32) for weight_arg in (attn_gain, mlp_gain, query_weight, key_weight, value_weight, out_weight, gate_weight, up_weight, down_weight)))
    inputs = layer_input.astype(jnp.float32).reshape(span_count, TOK_ROW, model_width)
    cotangent = grad_output.astype(jnp.float32).reshape(span_count, TOK_ROW, model_width)
    seq_spans = seq_ids.reshape(span_count, TOK_ROW)
    end_spans = block_ends.reshape(span_count, TOK_ROW)

    def one_span(running, scan_items):
        span_input, span_grad, span_seq, span_end = scan_items

        def forward(values, *weights):
            return layer(values, *weights, span_seq, span_end)
        output, pullback = jax.vjp(forward, span_input, *params)
        grads = pullback(span_grad)
        running = tuple((earlier_sum + addend for earlier_sum, addend in zip(running, grads[1:])))
        return (running, (output, grads[0]))
    start_sums = tuple((jnp.zeros(weight_arg.shape, jnp.float32) for weight_arg in params))
    totals, (outputs, grad_inputs) = lax.scan(one_span, start_sums, (inputs, cotangent, seq_spans, end_spans))
    layer_output = outputs.reshape(layer_input.shape).astype(jnp.bfloat16)
    grad_input = grad_inputs.reshape(layer_input.shape).astype(jnp.bfloat16)
    return (layer_output, grad_input, totals[0], totals[1], totals[2], totals[3], totals[4], totals[5], totals[6], totals[7], totals[8])
```

```python
import math

import jax
import jax.numpy as jnp
from jax import lax
from jax.experimental import pallas as pl
from jax.experimental.pallas import tpu as pltpu
from jax.sharding import PartitionSpec as P

HEAD = 64
LANES = 128
eps = 1e-05
rope_base = 10000.0
neg_fill = -1e30
f32 = jnp.float32
bf16 = jnp.bfloat16
VMEM_BYTES = 60 * 1024 * 1024


def dot_nn(a, b):
    return lax.dot_general(a, b, (((1,), (0,)), ((), ())), preferred_element_type=f32)


def dot_nt(a, b):
    return lax.dot_general(a, b, (((1,), (1,)), ((), ())), preferred_element_type=f32)


def halves(values):
    rows, cols = values.shape
    return jnp.transpose(values.reshape(rows, 2, cols // 2), (1, 0, 2))


def whole(values):
    two, rows, cols = values.shape
    return jnp.transpose(values, (1, 0, 2)).reshape(rows, two * cols)


def gather_any(weights):
    query, key, value, out, gate, up, down = weights

    def both(weight, row_axis):
        part = lax.all_gather(weight, "row", axis=row_axis, tiled=True)
        return lax.all_gather(part, "col", axis=1 - row_axis, tiled=True)

    mix = [halves(both(key, 0)), halves(both(value, 0)), halves(both(query, 0)), halves(both(out, 1).T)]
    return [
        jnp.concatenate(mix, axis=2),
        halves(both(gate, 0)),
        halves(both(up, 0)),
        halves(both(down, 1).T),
    ]


def scatter_any(grads, gains):
    first, gate, up, down = [grad.astype(f32) for grad in grads]
    kv = first.shape[2] // 8
    key, value, query, out = (
        whole(first[:, :, :kv]),
        whole(first[:, :, kv : 2 * kv]),
        whole(first[:, :, 2 * kv : 5 * kv]),
        whole(first[:, :, 5 * kv :]).T,
    )

    def both(grad, row_axis):
        part = lax.psum_scatter(grad, "row", scatter_dimension=row_axis, tiled=True)
        return lax.psum_scatter(part, "col", scatter_dimension=1 - row_axis, tiled=True)

    return (
        lax.psum(gains, ("row", "col")),
        (
            both(query, 0),
            both(key, 0),
            both(value, 0),
            both(out, 1),
            both(whole(gate), 0),
            both(whole(up), 0),
            both(whole(down).T, 1),
        ),
    )


PACKS = 4
MESH = pl.DeviceIdType.MESH


class Place:
    def __init__(self):
        row, x = lax.axis_index("row"), lax.axis_index("col")
        z, y, c = row // 4, (row // 2) % 2, row % 2
        self.x, self.z, self.y, self.c = x, z, y, c
        self.xa, self.ya = jnp.where(c == 0, 1 - x, x), jnp.where(c == 0, y, 1 - y)
        self.xb, self.yb = jnp.where(c == 0, x, 1 - x), jnp.where(c == 0, 1 - y, y)
        self.others = [(z + k) % 4 for k in (1, 2, 3)]
        self.line = [self.device(x, other, y, c) for other in self.others]
        self.near = self.device(self.xa, z, self.ya, c)
        self.far = self.device(self.xb, z, self.yb, c)
        self.twin = self.device(x, z, y, 1 - c)

    @staticmethod
    def device(x, z, y, c):
        return ((z * 2 + y) * 2 + c, x)

    def greet(self):
        barrier = pltpu.get_barrier_semaphore()
        for peer in self.line + [self.near, self.far, self.twin]:
            pl.semaphore_signal(barrier, inc=1, device_id=peer, device_id_type=MESH)
        pl.semaphore_wait(barrier, 6)


def remote(src, dst, send, recv, device):
    return pltpu.make_async_remote_copy(
        src_ref=src, dst_ref=dst, send_sem=send, recv_sem=recv, device_id=device, device_id_type=MESH
    )


GATHER_PLAN = [(p, h * 768, 768, (0, 0, 0, 1, 0, 0, 0, 1)[2 * p + h]) for p in range(PACKS) for h in range(2)]
SCATTER_PLAN = [(p, h * 768, 768) for p in range(PACKS) for h in range(2)]


def gather_kernel(plan, ahead, own_ref, out_ref, copied, sent, came):
    at = Place()
    at.greet()
    x, y, z, c = at.x, at.y, at.z, at.c
    steps = []
    for i, (pack, lane, lanes, kind) in enumerate(plan):
        cols = pl.ds(lane, lanes)
        own = own_ref.at[pack, :, cols]

        def one(xx, yy):
            return out_ref.at[pack, xx, z, yy, c, :, cols]

        def line(xx, yy, slot, device):
            ref = out_ref.at[pack, xx, :, yy, c, :, cols]
            return remote(ref, ref, sent.at[i, slot], came.at[i, slot], device)

        step = {"kind": kind, "keep": pltpu.make_async_copy(own, one(x, y), copied.at[i])}
        step["line"] = [remote(own, one(x, y), sent.at[i, k], came.at[i, k], at.line[k]) for k in range(3)]
        if kind == 0:
            step["near"] = line(x, y, 3, at.near)
        else:
            step["near"] = remote(own, one(x, y), sent.at[i, 3], came.at[i, 3], at.near)
            step["more"] = [
                remote(one(at.xa, at.ya), one(at.xa, at.ya), sent.at[i, 4 + k], came.at[i, 4 + k], at.line[k])
                for k in range(3)
            ]
        step["far"] = [line(x, y, 7, at.far), line(at.xa, at.ya, 8, at.far)]
        step["twin"] = [
            line(xx, yy, 9 + j, at.twin)
            for j, (xx, yy) in enumerate([(x, y), (at.xa, at.ya), (at.xb, at.yb), (1 - x, 1 - y)])
        ]
        steps.append(step)
    count = len(steps)

    def begin(i):
        if 0 <= i < count:
            steps[i]["keep"].start()
            for copy in steps[i]["line"]:
                copy.start()
            if steps[i]["kind"] == 1:
                steps[i]["near"].start()

    def first(i):
        if 0 <= i < count:
            step = steps[i]
            if step["kind"] == 1:
                step["near"].wait_recv()
                for copy in step["more"]:
                    copy.start()
            for copy in step["line"]:
                copy.wait_recv()
            step["keep"].wait()
            if step["kind"] == 0:
                step["near"].start()
            step["far"][0].start()
            step["twin"][0].start()

    def second(i):
        if 0 <= i < count:
            step = steps[i]
            for copy in [step["near"]] if step["kind"] == 0 else step["more"]:
                copy.wait_recv()
            step["far"][1].start()
            step["twin"][1].start()

    def third(i):
        if 0 <= i < count:
            step = steps[i]
            for j in range(2):
                step["far"][j].wait_recv()
                step["twin"][2 + j].start()

    for i in range(ahead):
        begin(i)
    for t in range(count + 2):
        first(t)
        begin(t + ahead)
        second(t - 1)
        third(t - 2)
    for step in steps:
        for copy in step["line"] + step.get("more", []) + [step["near"]] + step["far"]:
            copy.wait_send()
        for copy in step["twin"]:
            copy.wait()


def gather_special(packs):
    plan = GATHER_PLAN
    _, rows, lanes = packs.shape
    dma = pltpu.SemaphoreType.DMA
    anywhere = pl.BlockSpec(memory_space=pl.ANY)
    out = pl.pallas_call(
        lambda *refs: gather_kernel(plan, 2, *refs),
        out_shape=jax.ShapeDtypeStruct((PACKS, 2, 4, 2, 2, rows, lanes), packs.dtype),
        in_specs=[anywhere],
        out_specs=anywhere,
        scratch_shapes=[dma((len(plan),)), dma((len(plan), 13)), dma((len(plan), 13))],
        compiler_params=pltpu.CompilerParams(collective_id=1, has_side_effects=True),
        name="gather_weights",
    )(packs)
    return out.reshape(PACKS, 2, 16 * rows, lanes)


def scatter_kernel(plan, ahead, *refs):
    grad_ref, gain_ref, out_ref, gain_out_ref = refs[:4]
    own, from_twin, from_far, from_near, from_line, result, gains = refs[4:11]
    copied, stored, sent, came, gain_sent, gain_came = refs[11:]
    at = Place()
    at.greet()
    x, y, z, c = at.x, at.y, at.z, at.c
    mine = [(at.xb, at.yb), (1 - x, 1 - y), (at.xa, at.ya), (x, y)]
    theirs = [(at.xa, at.ya), (1 - x, 1 - y), (at.xb, at.yb), (x, y)]
    steps = []
    for i, (pack, lane, lanes) in enumerate(plan):
        cols = pl.ds(lane, lanes)

        def line(place, core):
            return grad_ref.at[pack, place[0], :, place[1], core, :, cols]

        def send(src, dst, slot, device):
            return remote(src, dst, sent.at[i, slot], came.at[i, slot], device)

        steps.append(
            {
                "twin": [send(line(theirs[j], 1 - c), from_twin.at[i, j], j, at.twin) for j in range(4)],
                "load": [
                    pltpu.make_async_copy(line(mine[j], c), own.at[i, j], copied.at[i, j]) for j in range(4)
                ],
                "far": [send(own.at[i, j], from_far.at[i, j], 4 + j, at.far) for j in range(2)],
                "near": send(own.at[i, 2], from_near.at[i], 6, at.near),
                "line": [
                    send(own.at[i, 3, at.others[k]], from_line.at[i, k], 7 + k, at.line[k]) for k in range(3)
                ],
                "store": pltpu.make_async_copy(result.at[i % 2], out_ref.at[pack, :, cols], stored.at[i]),
            }
        )
    count = len(steps)

    def add(total, terms):
        def body(q, carry):
            value = total[q].astype(f32)
            for term in terms:
                value = value + term[q].astype(f32)
            total[q] = value.astype(bf16)
            return carry

        lax.fori_loop(0, 4, body, 0)

    def begin(i):
        if 0 <= i < count:
            for j in (1, 0, 2, 3):
                steps[i]["twin"][j].start()
                steps[i]["load"][j].start()

    def first(i):
        if 0 <= i < count:
            step = steps[i]
            for j in (1, 0):
                step["twin"][j].wait_recv()
                step["load"][j].wait()
                add(own.at[i, j], [from_twin.at[i, j]])
                step["far"][j].start()

    def second(i):
        if 0 <= i < count:
            step = steps[i]
            step["twin"][2].wait_recv()
            step["load"][2].wait()
            step["far"][1].wait_recv()
            add(own.at[i, 2], [from_twin.at[i, 2], from_far.at[i, 1]])
            step["near"].start()

    def third(i):
        if 0 <= i < count:
            step = steps[i]
            step["twin"][3].wait_recv()
            step["load"][3].wait()
            step["far"][0].wait_recv()
            step["near"].wait_recv()

            def total(q):
                value = own[i, 3, q].astype(f32) + from_twin[i, 3, q].astype(f32)
                return value + from_far[i, 0, q].astype(f32) + from_near[i, q].astype(f32)

            for k in range(3):
                own[i, 3, at.others[k]] = total(at.others[k]).astype(bf16)
                step["line"][k].start()
            if i >= 2:
                steps[i - 2]["store"].wait()
            result[i % 2] = total(z)

    def fourth(i):
        if 0 <= i < count:
            step = steps[i]
            value = result[i % 2]
            for k in range(3):
                step["line"][k].wait_recv()
                value = value + from_line[i, k].astype(f32)
            result[i % 2] = value
            step["store"].start()

    for i in range(ahead):
        begin(i)
    gains[0] = gain_ref[...]
    exchanges = [
        remote(gains.at[2 * k], gains.at[2 * k + 1], gain_sent.at[k], gain_came.at[k], peer)
        for k, peer in enumerate([at.twin, at.near, at.far])
    ]
    everyone = [
        remote(gains.at[6 + z], gains.at[6 + z], gain_sent.at[3 + k], gain_came.at[3 + k], at.line[k])
        for k in range(3)
    ]
    for t in range(count + 3):
        first(t)
        begin(t + ahead)
        second(t - 1)
        third(t - 2)
        fourth(t - 3)
        if 2 <= t < 5:
            exchanges[t - 2].wait()
            spot = 6 + z if t == 4 else 2 * (t - 1)
            gains[spot] = gains[2 * (t - 2)] + gains[2 * (t - 2) + 1]
        if 1 <= t < 4:
            exchanges[t - 1].start()
        if t == 4:
            for copy in everyone:
                copy.start()
        if t == 5:
            for copy in everyone:
                copy.wait()
            gain_out_ref[...] = gains[6] + gains[7] + gains[8] + gains[9]
    for i, step in enumerate(steps):
        for copy in step["twin"] + step["far"] + [step["near"]] + step["line"]:
            copy.wait_send()
        if i >= count - 2:
            step["store"].wait()


def scatter_special(grads, gains):
    plan = SCATTER_PLAN
    count, lanes = len(plan), plan[0][2]
    rows, width = grads.shape[5:]
    dma, vmem = pltpu.SemaphoreType.DMA, pltpu.VMEM
    anywhere = pl.BlockSpec(memory_space=pl.ANY)
    near = pl.BlockSpec(memory_space=pltpu.VMEM)
    return pl.pallas_call(
        lambda *refs: scatter_kernel(plan, 2, *refs),
        out_shape=(
            jax.ShapeDtypeStruct((PACKS, rows, width), f32),
            jax.ShapeDtypeStruct(gains.shape, f32),
        ),
        in_specs=[anywhere, near],
        out_specs=(anywhere, near),
        scratch_shapes=[
            vmem((count, 4, 4, rows, lanes), bf16),
            vmem((count, 4, 4, rows, lanes), bf16),
            vmem((count, 2, 4, rows, lanes), bf16),
            vmem((count, 4, rows, lanes), bf16),
            vmem((count, 3, rows, lanes), bf16),
            vmem((2, rows, lanes), f32),
            vmem((10,) + gains.shape, f32),
            dma((count, 4)),
            dma((count,)),
            dma((count, 10)),
            dma((count, 10)),
            dma((6,)),
            dma((6,)),
        ],
        compiler_params=pltpu.CompilerParams(
            collective_id=2, has_side_effects=True, vmem_limit_bytes=VMEM_BYTES
        ),
        name="scatter_gradients",
    )(grads, gains)


def gather_packs(weights):
    if (lax.axis_size("row"), lax.axis_size("col")) != (16, 2):
        return gather_any(weights)
    query, key, value, out, gate, up, down = weights
    mix = jnp.concatenate([key, value, query, out.T], axis=1)
    full = gather_special(jnp.stack([mix, gate, up, down.T]))
    return [full[p] for p in range(PACKS)]


def scatter_packs(grads, gains):
    if (lax.axis_size("row"), lax.axis_size("col")) != (16, 2):
        return scatter_any(grads, gains)
    _, depth, lanes = grads[0].shape
    stacked = jnp.stack(grads).reshape(PACKS, 2, 4, 2, 2, depth // 16, lanes)
    sums, gain_sums = scatter_special(stacked, gains.reshape(-1, LANES))
    kv = lanes // 8
    first = sums[0]
    return (
        gain_sums.reshape(gains.shape),
        (
            first[:, 2 * kv : 5 * kv],
            first[:, :kv],
            first[:, kv : 2 * kv],
            first[:, 5 * kv :].T,
            sums[1],
            sums[2],
            sums[3].T,
        ),
    )


def lane_of(shape):
    return lax.broadcasted_iota(jnp.int32, shape, len(shape) - 1)


def turn(values, cosine, sine, lower):
    ahead = pltpu.roll(values, LANES - HEAD // 2, 1)
    behind = pltpu.roll(values, HEAD // 2, 1)
    return values * cosine + jnp.where(lower, -ahead, behind) * sine


def turn_back(values, cosine, sine, lower):
    scaled = values * sine
    ahead = pltpu.roll(scaled, LANES - HEAD // 2, 1)
    behind = pltpu.roll(scaled, HEAD // 2, 1)
    return values * cosine - jnp.where(lower, -ahead, behind)


def project_kernel(x_ref, gain_ref, weight_ref, cos_ref, sin_ref, attn_in_ref, y_ref):
    values = x_ref[...].astype(f32)
    inverse = lax.rsqrt(jnp.mean(values * values, axis=1, keepdims=True) + eps)
    attn_in = (values * inverse * gain_ref[...]).astype(bf16)
    attn_in_ref[...] = attn_in
    cosine, sine = cos_ref[...], sin_ref[...]
    lane = lane_of(cosine.shape)
    lower = lane % HEAD < HEAD // 2
    for half in range(2):
        for tile in range(8):
            cols = pl.ds(tile * LANES, LANES)
            raw = dot_nn(attn_in, weight_ref[half, :, cols]).astype(bf16).astype(f32)
            if tile == 0:
                out = turn(raw, cosine, sine, lower)
            elif tile == 1:
                out = jnp.where(lane < HEAD, turn(raw, cosine, sine, lower), raw)
            elif tile == 2:
                out = raw
            else:
                out = turn(raw, cosine, sine, lower) * HEAD ** (-0.5)
            y_ref[half, :, cols] = out.astype(bf16)


def head_rows(values, side, lane):
    return jnp.where((lane < HEAD) if side == 0 else (lane >= HEAD), values, jnp.zeros_like(values))


def twice(tile, side, lane):
    values = tile.astype(f32)
    other = pltpu.roll(values, HEAD, 1)
    keep = (lane < HEAD) if side == 0 else (lane >= HEAD)
    return jnp.where(keep, values, other)


def load_groups(kv_ref, half, dup_ref, flip_ref):
    for slot in range(6):
        tile = kv_ref[half, :, pl.ds((slot // 2) * LANES, LANES)]
        both = twice(tile, slot % 2, lane_of(tile.shape))
        dup_ref[slot] = both.astype(bf16)
        flip_ref[slot] = both.T.astype(bf16)


def seen(first_ref, last_ref, rows, keys):
    index = lax.broadcasted_iota(jnp.int32, (keys, rows.size), 0)
    return (index >= first_ref[:, rows]) & (index <= last_ref[:, rows])


def attend_kernel(block, y_ref, kv_ref, first_ref, last_ref, mix_ref, log_ref, dup_ref, flip_ref):
    keys = kv_ref.shape[1]
    half = pl.program_id(0)
    load_groups(kv_ref, 0, dup_ref, flip_ref)
    lane = lane_of((block, LANES))

    def rows_of(step, carry):
        rows = pl.ds(pl.multiple_of(step * block, block), block)
        allowed = seen(first_ref, last_ref, rows, keys)
        previous = jnp.zeros((block, LANES), f32)
        for head in range(9):
            group = head // 3
            query = head_rows(y_ref[0, rows, pl.ds((3 + head // 2) * LANES, LANES)], head % 2, lane)
            scores = jnp.where(allowed, dot_nt(dup_ref[group], query), neg_fill)
            top = jnp.max(scores, axis=0, keepdims=True)
            powers = jnp.exp(scores - top)
            total = jnp.sum(powers, axis=0, keepdims=True)
            probs = (powers * (1.0 / total)).astype(bf16)
            mixed = dot_nn(flip_ref[3 + group], probs).T
            log_ref[0, pl.ds(head, 1), rows] = top + jnp.log(total)
            if head % 2 == 0:
                tile = jnp.where(lane < HEAD, previous, mixed)
                mix_ref[0, rows, pl.ds((head // 2) * LANES, LANES)] = tile.astype(bf16)
            previous = mixed
        return carry

    lax.fori_loop(0, y_ref.shape[1] // block, rows_of, 0)


def attend_back_kernel(
    block, y_ref, kv_ref, first_ref, last_ref, log_ref, grad_ref, cos_ref, sin_ref, dq_ref, dkv_ref, dup_ref, flip_ref, acc_ref
):
    keys = kv_ref.shape[1]
    load_groups(kv_ref, 0, dup_ref, flip_ref)
    acc_ref[...] = jnp.zeros_like(acc_ref)
    lane = lane_of((block, LANES))
    lower = lane % HEAD < HEAD // 2

    def rows_of(step, carry):
        rows = pl.ds(pl.multiple_of(step * block, block), block)
        allowed = seen(first_ref, last_ref, rows, keys)
        previous = None
        for head in range(9):
            group = head // 3
            query = head_rows(y_ref[0, rows, pl.ds((3 + head // 2) * LANES, LANES)], head % 2, lane)
            upstream = head_rows(grad_ref[0, rows, pl.ds(((head + 1) // 2) * LANES, LANES)], (head + 1) % 2, lane)
            scores = jnp.where(allowed, dot_nt(dup_ref[group], query), neg_fill)
            probs = jnp.exp(scores - log_ref[0, pl.ds(head, 1), rows])
            grad_probs = dot_nt(dup_ref[3 + group], upstream)
            inner = jnp.sum(probs * grad_probs, axis=0, keepdims=True)
            grad_scores = (probs * (grad_probs - inner)).astype(bf16)
            acc_ref[3 + group] += dot_nn(probs.astype(bf16), upstream)
            acc_ref[group] += dot_nn(grad_scores, query)
            grad_query = dot_nn(flip_ref[group], grad_scores).T
            if head % 2 == 1 or head == 8:
                if head == 8:
                    tile = jnp.where(lane < HEAD, grad_query, 0.0)
                else:
                    tile = jnp.where(lane < HEAD, previous, grad_query)
                tile = turn_back(tile * HEAD ** (-0.5), cos_ref[rows, :], sin_ref[rows, :], lower)
                dq_ref[0, rows, pl.ds((head // 2) * LANES, LANES)] = tile.astype(bf16)
            previous = grad_query
        return carry

    lax.fori_loop(0, y_ref.shape[1] // block, rows_of, 0)
    lane_k = lane_of((keys, LANES))
    for tile in range(3):
        low, high = acc_ref[2 * tile], acc_ref[2 * tile + 1]
        low = low + pltpu.roll(low, HEAD, 1)
        high = high + pltpu.roll(high, HEAD, 1)
        dkv_ref[0, :, pl.ds(tile * LANES, LANES)] = jnp.where(lane_k < HEAD, low, high).astype(dkv_ref.dtype)


def full_spec(shape):
    return pl.BlockSpec(shape, lambda i: (0,) * len(shape))


def half_spec(shape):
    return pl.BlockSpec((1,) + shape[1:], lambda i: (i,) + (0,) * (len(shape) - 1))


def params():
    return pltpu.CompilerParams(vmem_limit_bytes=VMEM_BYTES)


def project(layer_input, gain, first_pack, cosine, sine):
    tokens, width = layer_input.shape
    vm = pl.BlockSpec(memory_space=pltpu.VMEM)
    return pl.pallas_call(
        project_kernel,
        grid=(1,),
        out_shape=(
            jax.ShapeDtypeStruct((tokens, width), bf16),
            jax.ShapeDtypeStruct((2, tokens, 8 * LANES), bf16),
        ),
        in_specs=[
            full_spec((tokens, width)),
            full_spec((1, width)),
            full_spec((2, width, 8 * LANES)),
            full_spec((tokens, LANES)),
            full_spec((tokens, LANES)),
        ],
        out_specs=(full_spec((tokens, width)), full_spec((2, tokens, 8 * LANES))),
        compiler_params=params(),
        name="project",
    )(layer_input, gain, first_pack, cosine, sine)


def attend(y, kv, first, last):
    tokens, keys = y.shape[1], kv.shape[1]
    block = min(256, tokens)
    return pl.pallas_call(
        lambda *refs: attend_kernel(block, *refs),
        grid=(2,),
        out_shape=(
            jax.ShapeDtypeStruct((2, tokens, 5 * LANES), bf16),
            jax.ShapeDtypeStruct((2, 16, tokens), f32),
        ),
        in_specs=[half_spec(y.shape), half_spec(kv.shape), full_spec((1, tokens)), full_spec((1, tokens))],
        out_specs=(half_spec((2, tokens, 5 * LANES)), half_spec((2, 16, tokens))),
        scratch_shapes=[pltpu.VMEM((6, keys, LANES), bf16), pltpu.VMEM((6, LANES, keys), bf16)],
        compiler_params=params(),
        name="attend",
    )(y, kv, first, last)


def attend_back(y, kv, first, last, logs, grad, cosine, sine):
    tokens, keys = y.shape[1], kv.shape[1]
    block = min(256, tokens)
    return pl.pallas_call(
        lambda *refs: attend_back_kernel(block, *refs),
        grid=(2,),
        out_shape=(
            jax.ShapeDtypeStruct((2, tokens, 5 * LANES), bf16),
            jax.ShapeDtypeStruct((2, keys, 3 * LANES), f32),
        ),
        in_specs=[
            half_spec(y.shape),
            half_spec(kv.shape),
            full_spec((1, tokens)),
            full_spec((1, tokens)),
            half_spec(logs.shape),
            half_spec(grad.shape),
            full_spec((tokens, LANES)),
            full_spec((tokens, LANES)),
        ],
        out_specs=(half_spec((2, tokens, 5 * LANES)), half_spec((2, keys, 3 * LANES))),
        scratch_shapes=[
            pltpu.VMEM((6, keys, LANES), bf16),
            pltpu.VMEM((6, LANES, keys), bf16),
            pltpu.VMEM((6, keys, LANES), f32),
        ],
        compiler_params=params(),
        name="attend_back",
    )(y, kv, first, last, logs, grad, cosine, sine)


def rope_tables(position):
    lane_index = (jnp.arange(LANES, dtype=jnp.int32) % (HEAD // 2)).astype(f32)
    frequency = jnp.exp(lane_index * (-2.0 * math.log(rope_base) / HEAD))
    angles = position[:, None] * frequency[None, :]
    return jnp.cos(angles), jnp.sin(angles)


def shards(
    layer_input,
    attn_gain,
    mlp_gain,
    query_weight,
    key_weight,
    value_weight,
    out_weight,
    gate_weight,
    up_weight,
    down_weight,
    seq_ids,
    block_ends,
    grad_output,
):
    tokens, width = layer_input.shape
    span = seq_ids.shape[0]
    start = lax.axis_index("col") * tokens
    index = jnp.arange(span, dtype=jnp.int32)
    in_first = seq_ids == seq_ids[0]
    seq_first = jnp.where(in_first, 0, jnp.sum(in_first.astype(jnp.int32)))
    block_last = block_ends - lax.axis_index("row") * span
    own_first = lax.dynamic_slice_in_dim(seq_first, start, tokens)
    own_last = lax.dynamic_slice_in_dim(block_last, start, tokens)
    position = lax.dynamic_slice_in_dim(index - seq_first, start, tokens).astype(f32)
    cosine, sine = rope_tables(position)
    own_first, own_last = own_first[None, :], own_last[None, :]
    gain_one = attn_gain.astype(f32)[None, :]
    gain_two = mlp_gain.astype(f32)[None, :]

    pack_first, pack_gate, pack_up, pack_down = gather_packs(
        (query_weight, key_weight, value_weight, out_weight, gate_weight, up_weight, down_weight)
    )
    attn_in, y = project(layer_input, gain_one, pack_first, cosine, sine)
    kv = lax.all_gather(y[:, :, : 3 * LANES], "col", axis=1, tiled=True)
    mix, logs = attend(y, kv, own_first, own_last)
    pack_out = pack_first[:, :, 7 * LANES :]
    branch = jnp.einsum("htq,hdq->td", mix, pack_out, preferred_element_type=f32)
    own = layer_input.astype(f32)
    residual = own + branch
    inv_two = lax.rsqrt(jnp.mean(residual * residual, axis=1, keepdims=True) + eps)
    normed_two = residual * inv_two
    mlp_in = (normed_two * gain_two).astype(bf16)
    gate_act = jnp.einsum("td,hdf->htf", mlp_in, pack_gate, preferred_element_type=f32)
    up_act = jnp.einsum("td,hdf->htf", mlp_in, pack_up, preferred_element_type=f32)
    hidden = (jax.nn.silu(gate_act) * up_act).astype(bf16)
    layer_output = (
        residual + jnp.einsum("htf,hdf->td", hidden, pack_down, preferred_element_type=f32)
    ).astype(bf16)
    grad_down = jnp.einsum("td,htf->hdf", grad_output, hidden, preferred_element_type=f32).astype(bf16)
    grad_hidden = jnp.einsum("td,hdf->htf", grad_output, pack_down, preferred_element_type=f32)
    sigmoid = jax.nn.sigmoid(gate_act)
    grad_gate_act = (grad_hidden * up_act * sigmoid * (1.0 + gate_act * (1.0 - sigmoid))).astype(bf16)
    grad_up_act = (grad_hidden * gate_act * sigmoid).astype(bf16)
    grad_gate = jnp.einsum("td,htf->hdf", mlp_in, grad_gate_act, preferred_element_type=f32).astype(bf16)
    grad_up = jnp.einsum("td,htf->hdf", mlp_in, grad_up_act, preferred_element_type=f32).astype(bf16)
    grad_mlp_in = jnp.einsum(
        "htf,hdf->td", grad_gate_act, pack_gate, preferred_element_type=f32
    ) + jnp.einsum("htf,hdf->td", grad_up_act, pack_up, preferred_element_type=f32)
    scaled_two = grad_mlp_in * gain_two
    inner_two = jnp.mean(scaled_two * normed_two, axis=1, keepdims=True)
    grad_residual = grad_output.astype(f32) + inv_two * (scaled_two - normed_two * inner_two)
    grad_mlp_gain = jnp.sum(grad_mlp_in * normed_two, axis=0)
    grad_branch = grad_residual.astype(bf16)
    grad_mixture = jnp.einsum("td,hdq->htq", grad_branch, pack_out, preferred_element_type=f32).astype(bf16)
    grad_q, grad_kv = attend_back(y, kv, own_first, own_last, logs, grad_mixture, cosine, sine)
    grad_kv = lax.psum_scatter(grad_kv, "col", scatter_dimension=1, tiled=True)
    key_cos, key_sin = jnp.tile(cosine, (1, 3)), jnp.tile(sine, (1, 3))
    lane = jnp.arange(3 * LANES, dtype=jnp.int32)
    is_key = lane < 3 * HEAD
    scaled = grad_kv * key_sin
    turned = jnp.where(
        lane % HEAD < HEAD // 2, -jnp.roll(scaled, -(HEAD // 2), axis=2), jnp.roll(scaled, HEAD // 2, axis=2)
    )
    grad_kv = jnp.where(is_key, grad_kv * key_cos - turned, grad_kv).astype(bf16)
    grad_y = jnp.concatenate([grad_kv, grad_q], axis=2)
    grad_proj = jnp.einsum("td,htf->hdf", attn_in, grad_y, preferred_element_type=f32)
    grad_out = jnp.einsum("td,htq->hdq", grad_branch, mix, preferred_element_type=f32)
    grad_first = jnp.concatenate(
        [
            grad_proj[:, :, : 7 * LANES],
            grad_proj[:, :, 7 * LANES :] + grad_out[:, :, :LANES],
            grad_out[:, :, LANES:],
        ],
        axis=2,
    ).astype(bf16)
    grad_attn_in = jnp.einsum(
        "htf,hdf->td", grad_y, pack_first[:, :, : 8 * LANES], preferred_element_type=f32
    )
    inv_one = lax.rsqrt(jnp.mean(own * own, axis=1, keepdims=True) + eps)
    normed_one = own * inv_one
    scaled_one = grad_attn_in * gain_one
    inner_one = jnp.mean(scaled_one * normed_one, axis=1, keepdims=True)
    grad_input = (grad_residual + inv_one * (scaled_one - normed_one * inner_one)).astype(bf16)
    grad_attn_gain = jnp.sum(grad_attn_in * normed_one, axis=0)
    gain_sums, weight_sums = scatter_packs(
        (grad_first, grad_gate, grad_up, grad_down), jnp.stack([grad_attn_gain, grad_mlp_gain])
    )
    return (layer_output, grad_input, gain_sums[0], gain_sums[1]) + tuple(weight_sums)


def solution(mesh):
    tokens_spec = P(("row", "col"), None)
    in_specs = (
        tokens_spec,
        P(),
        P(),
        P("row", "col"),
        P("row", "col"),
        P("row", "col"),
        P("col", "row"),
        P("row", "col"),
        P("row", "col"),
        P("col", "row"),
        P("row"),
        P("row"),
        tokens_spec,
    )
    out_specs = (
        tokens_spec,
        tokens_spec,
        P(),
        P(),
        P("row", "col"),
        P("row", "col"),
        P("row", "col"),
        P("col", "row"),
        P("row", "col"),
        P("row", "col"),
        P("col", "row"),
    )
    return jax.shard_map(shards, mesh=mesh, in_specs=in_specs, out_specs=out_specs, check_vma=False)
```

```python
import math

import jax
import jax.numpy as jnp
from jax import lax
from jax.experimental import pallas as pl
from jax.experimental.pallas import tpu as pltpu
from jax.sharding import PartitionSpec as P

HEAD = 64
LANES = 128
eps = 1e-05
rope_base = 10000.0
neg_fill = -1e30
f32 = jnp.float32
bf16 = jnp.bfloat16
VMEM_BYTES = 62 * 1024 * 1024


def dot_nn(a, b):
    return lax.dot_general(a, b, (((1,), (0,)), ((), ())), preferred_element_type=f32)


def dot_nt(a, b):
    return lax.dot_general(a, b, (((1,), (1,)), ((), ())), preferred_element_type=f32)


def halves(values):
    rows, cols = values.shape
    return jnp.transpose(values.reshape(rows, 2, cols // 2), (1, 0, 2))


def whole(values):
    two, rows, cols = values.shape
    return jnp.transpose(values, (1, 0, 2)).reshape(rows, two * cols)


def gather_any(weights):
    query, key, value, out, gate, up, down = weights

    def both(weight, row_axis):
        part = lax.all_gather(weight, "row", axis=row_axis, tiled=True)
        return lax.all_gather(part, "col", axis=1 - row_axis, tiled=True)

    mix = [halves(both(key, 0)), halves(both(value, 0)), halves(both(query, 0)), halves(both(out, 1).T)]
    return [
        jnp.concatenate(mix, axis=2),
        halves(both(gate, 0)),
        halves(both(up, 0)),
        halves(both(down, 1).T),
    ]


def scatter_any(grads, gains):
    first, gate, up, down = [grad.astype(f32) for grad in grads]
    kv = first.shape[2] // 8
    key, value, query, out = (
        whole(first[:, :, :kv]),
        whole(first[:, :, kv : 2 * kv]),
        whole(first[:, :, 2 * kv : 5 * kv]),
        whole(first[:, :, 5 * kv :]).T,
    )

    def both(grad, row_axis):
        part = lax.psum_scatter(grad, "row", scatter_dimension=row_axis, tiled=True)
        return lax.psum_scatter(part, "col", scatter_dimension=1 - row_axis, tiled=True)

    return (
        lax.psum(gains, ("row", "col")),
        (
            both(query, 0),
            both(key, 0),
            both(value, 0),
            both(out, 1),
            both(whole(gate), 0),
            both(whole(up), 0),
            both(whole(down).T, 1),
        ),
    )


PACKS = 4
MESH = pl.DeviceIdType.MESH


class Place:
    def __init__(self):
        row, x = lax.axis_index("row"), lax.axis_index("col")
        z, y, c = row // 4, (row // 2) % 2, row % 2
        self.x, self.z, self.y, self.c = x, z, y, c
        self.xa, self.ya = jnp.where(c == 0, 1 - x, x), jnp.where(c == 0, y, 1 - y)
        self.xb, self.yb = jnp.where(c == 0, x, 1 - x), jnp.where(c == 0, 1 - y, y)
        self.others = [(z + k) % 4 for k in (1, 2, 3)]
        self.line = [self.device(x, other, y, c) for other in self.others]
        self.near = self.device(self.xa, z, self.ya, c)
        self.far = self.device(self.xb, z, self.yb, c)
        self.twin = self.device(x, z, y, 1 - c)
        self.cross = self.device(1 - x, z, y, c)

    @staticmethod
    def device(x, z, y, c):
        return ((z * 2 + y) * 2 + c, x)

    def greet(self):
        barrier = pltpu.get_barrier_semaphore()
        for peer in self.line + [self.near, self.far, self.twin]:
            pl.semaphore_signal(barrier, inc=1, device_id=peer, device_id_type=MESH)
        pl.semaphore_wait(barrier, 6)


def remote(src, dst, send, recv, device):
    return pltpu.make_async_remote_copy(
        src_ref=src, dst_ref=dst, send_sem=send, recv_sem=recv, device_id=device, device_id_type=MESH
    )


GATHER_PLAN = [
    (0, 0, 512, 0),
    (0, 512, 512, 0),
    (0, 1024, 512, 0),
    (1, 0, 768, 1),
    (2, 0, 768, 0),
    (1, 768, 768, 0),
    (2, 768, 768, 0),
    (3, 0, 768, 1),
    (3, 768, 768, 0),
]
SCATTER_PLAN = [(3, 0), (1, 0), (2, 0), (3, 1), (1, 1), (2, 1), (0, 0), (0, 1)]
RING = 6


class Gather:
    def __init__(self, at, plan, own_refs, out_refs, copied, sent, came):
        x, y, z = at.x, at.y, at.z
        size = own_refs[0].shape[0]
        rows = pl.ds(pl.multiple_of(at.c * size, 8), size)
        self.steps = []
        for i, (pack, lane, lanes, kind) in enumerate(plan):
            cols = pl.ds(lane, lanes)
            own = own_refs[pack].at[:, cols]

            def one(xx, yy):
                return out_refs[pack].at[xx, z, yy, rows, cols]

            def line(xx, yy, slot, device):
                ref = out_refs[pack].at[xx, :, yy, rows, cols]
                return remote(ref, ref, sent.at[i, slot], came.at[i, slot], device)

            step = {"kind": kind, "keep": pltpu.make_async_copy(own, one(x, y), copied.at[i])}
            step["line"] = [remote(own, one(x, y), sent.at[i, k], came.at[i, k], at.line[k]) for k in range(3)]
            if kind == 0:
                step["near"] = line(x, y, 3, at.near)
            else:
                step["near"] = remote(own, one(x, y), sent.at[i, 3], came.at[i, 3], at.near)
                step["more"] = [
                    remote(one(at.xa, at.ya), one(at.xa, at.ya), sent.at[i, 4 + k], came.at[i, 4 + k], at.line[k])
                    for k in range(3)
                ]
            step["far"] = [line(x, y, 7, at.far), line(at.xa, at.ya, 8, at.far)]
            step["twin"] = [
                line(xx, yy, 9 + j, at.twin)
                for j, (xx, yy) in enumerate([(x, y), (at.xa, at.ya), (at.xb, at.yb), (1 - x, 1 - y)])
            ]
            self.steps.append(step)

    def begin(self, i):
        if 0 <= i < len(self.steps):
            self.steps[i]["keep"].start()
            for copy in self.steps[i]["line"]:
                copy.start()
            if self.steps[i]["kind"] == 1:
                self.steps[i]["near"].start()

    def first(self, i):
        if 0 <= i < len(self.steps):
            step = self.steps[i]
            if step["kind"] == 1:
                step["near"].wait_recv()
                for copy in step["more"]:
                    copy.start()
            for copy in step["line"]:
                copy.wait_recv()
            step["keep"].wait()
            if step["kind"] == 0:
                step["near"].start()
            step["far"][0].start()
            step["twin"][0].start()

    def second(self, i):
        if 0 <= i < len(self.steps):
            step = self.steps[i]
            for copy in [step["near"]] if step["kind"] == 0 else step["more"]:
                copy.wait_recv()
            step["far"][1].start()
            step["twin"][1].start()

    def third(self, i):
        if 0 <= i < len(self.steps):
            step = self.steps[i]
            for j in range(2):
                step["far"][j].wait_recv()
                step["twin"][2 + j].start()

    def arrive(self, i):
        for copy in self.steps[i]["twin"]:
            copy.wait_recv()

    def move(self, t):
        self.first(t)
        self.begin(t + 2)
        self.second(t - 1)
        self.third(t - 2)

    def finish(self):
        for step in self.steps:
            for copy in step["line"] + step.get("more", []) + [step["near"]] + step["far"] + step["twin"]:
                copy.wait_send()


def forward_kernel(plan, *refs):
    x_ref, gain_one_ref, gain_two_ref, cos_ref, sin_ref, first_ref, last_ref = refs[:7]
    own_refs, full_refs = refs[7:11], refs[11:15]
    saved = refs[15:25]
    weights, attn_in, y, kv, dup, flip, mix, logs, residual, mlp_in, acts, hidden, output = refs[25:38]
    copied, sent, came, loaded, stored, kv_sent, kv_came = refs[38:]
    at = Place()
    at.greet()
    gather = Gather(at, plan, own_refs, full_refs, copied, sent, came)
    tokens, width = x_ref.shape
    lanes = weights.shape[2]

    def load(pack, cut, slot, k):
        size = lanes // 2
        return [
            pltpu.make_async_copy(
                full_refs[pack].at[half].reshape(width, lanes).at[:, pl.ds(cut * size, size)],
                weights.at[slot, :, pl.ds(half * size, size)],
                loaded.at[k, half],
            )
            for half in range(2)
        ]

    def load_first(half, lane, size, k):
        part = pl.ds(lane, size)
        return pltpu.make_async_copy(
            full_refs[0].at[half].reshape(width, lanes).at[:, part], weights.at[half, :, part], loaded.at[k, half]
        )

    project_loads = [load_first(half, 0, 8 * LANES, 0) for half in range(2)]
    out_loads = [load_first(half, 8 * LANES, lanes - 8 * LANES, 1) for half in range(2)]
    gate_loads = [load(1, 0, 2, 2) + load(2, 0, 3, 3), load(1, 1, 0, 4) + load(2, 1, 1, 5)]
    down_loads = [load(3, 0, 2, 6), load(3, 1, 3, 7)]

    def save(k, ref):
        copy = pltpu.make_async_copy(ref, saved[k], stored.at[k])
        copy.start()
        return copy

    gather.begin(0)
    gather.begin(1)
    values = x_ref[...].astype(f32)
    inverse = lax.rsqrt(jnp.mean(values * values, axis=1, keepdims=True) + eps)
    attn_in[...] = (values * inverse * gain_one_ref[...]).astype(bf16)
    saves = [save(0, attn_in)]
    for t in range(4):
        gather.move(t)
    gather.arrive(0)
    gather.arrive(1)
    start(project_loads)
    mine = pl.ds(pl.multiple_of(at.x * tokens, tokens), tokens)
    for half in range(2):
        project_loads[half].wait()
        project_half(half, attn_in, weights, cos_ref, sin_ref, y)
        kv[half, mine, :] = y[half, :, : 3 * LANES]
        exchange = remote(kv.at[half, mine, :], kv.at[half, mine, :], kv_sent.at[half], kv_came.at[half], at.cross)
        exchange.start()
    saves.append(save(1, y))
    gather.move(4)
    for half in range(2):
        remote(kv.at[half, mine, :], kv.at[half, mine, :], kv_sent.at[half], kv_came.at[half], at.cross).wait()
    saves.append(save(2, kv))
    block = 256
    steps = tokens // block

    def rows_of(i, carry):
        half = i // steps

        @pl.when(i % steps == 0)
        def _():
            load_groups(kv, half, dup, flip)

        attend_rows(half, i % steps, block, y, dup, flip, first_ref, last_ref, mix, logs)
        for k in range(4):

            @pl.when(i == k * steps // 2)
            def _(k=k):
                gather.move(5 + k)

        return carry

    lax.fori_loop(0, 2 * steps, rows_of, 0)
    saves.append(save(3, mix))
    saves.append(save(4, logs))
    gather.arrive(2)
    start(out_loads)
    wait(out_loads)
    span = pl.ds(7 * LANES, 5 * LANES)

    def branch_of(i, carry):
        rows = pl.ds(pl.multiple_of(i * 256, 256), 256)
        total = x_ref[rows, :].astype(f32)
        for half in range(2):
            total = total + dot_nt(mix[half, rows, :], weights[half, :, span])
        residual[rows, :] = total
        inverse = lax.rsqrt(jnp.mean(total * total, axis=1, keepdims=True) + eps)
        mlp_in[rows, :] = (total * inverse * gain_two_ref[...]).astype(bf16)
        return carry

    lax.fori_loop(0, tokens // 256, branch_of, 0)
    saves.append(save(5, residual))
    saves.append(save(6, mlp_in))
    gather.move(9)
    gather.move(10)
    for cut in range(2):
        for i in (3, 4) if cut == 0 else (5, 6):
            gather.arrive(i)
        start(gate_loads[cut])
    size = lanes // 2
    for cut in range(2):
        wait(gate_loads[cut])
        slot = 2 - 2 * cut

        def hidden_of(i, carry):
            half, tile = i // (size // 256), i % (size // 256)
            cols = pl.ds(pl.multiple_of(i * 256, 256), 256)
            into = pl.ds(pl.multiple_of(cut * size + tile * 256, 256), 256)
            gate = dot_nn(mlp_in[...], weights[slot, :, cols])
            up = dot_nn(mlp_in[...], weights[slot + 1, :, cols])
            acts[half, 0, :, into] = gate
            acts[half, 1, :, into] = up
            hidden[half, :, into] = (gate * jax.nn.sigmoid(gate) * up).astype(bf16)
            return carry

        lax.fori_loop(0, lanes // 256, hidden_of, 0)
        if cut == 0:
            gather.arrive(7)
            start(down_loads[0])
    gather.arrive(8)
    start(down_loads[1])
    saves.append(save(7, acts))
    saves.append(save(8, hidden))
    wait(down_loads[0] + down_loads[1])

    def output_of(i, carry):
        rows = pl.ds(pl.multiple_of(i * 256, 256), 256)
        total = residual[rows, :]
        for half in range(2):
            for cut in range(2):
                total = total + dot_nt(
                    hidden[half, rows, pl.ds(cut * size, size)], weights[2 + cut, :, pl.ds(half * size, size)]
                )
        output[rows, :] = total.astype(bf16)
        return carry

    lax.fori_loop(0, tokens // 256, output_of, 0)
    saves.append(save(9, output))
    gather.finish()
    for copy in saves:
        copy.wait()


def forward_special(layer_input, gains, cosine, sine, first, last, packs):
    plan = GATHER_PLAN
    tokens, width = layer_input.shape
    rows, lanes = packs[0].shape
    keys = 2 * tokens
    dma, vmem = pltpu.SemaphoreType.DMA, pltpu.VMEM
    anywhere = pl.BlockSpec(memory_space=pl.ANY)
    near = pl.BlockSpec(memory_space=pltpu.VMEM)
    saved = [
        ((tokens, width), bf16),
        ((2, tokens, 8 * LANES), bf16),
        ((2, keys, 3 * LANES), bf16),
        ((2, tokens, 5 * LANES), bf16),
        ((2, 16, tokens), f32),
        ((tokens, width), f32),
        ((tokens, width), bf16),
        ((2, 2, tokens, lanes), f32),
        ((2, tokens, lanes), bf16),
        ((tokens, width), bf16),
    ]
    full = [((2, 4, 2, 2 * rows, lanes), bf16)] * PACKS
    count = len(plan)
    outs = pl.pallas_call(
        lambda *refs: forward_kernel(plan, *refs),
        out_shape=[jax.ShapeDtypeStruct(*shape) for shape in full + saved],
        in_specs=[near] * 7 + [anywhere] * PACKS,
        out_specs=[anywhere] * (PACKS + len(saved)),
        scratch_shapes=[
            vmem((4, width, lanes), bf16),
            vmem(*saved[0]),
            vmem(*saved[1]),
            vmem(*saved[2]),
            vmem((6, keys, LANES), bf16),
            vmem((6, LANES, keys), bf16),
            vmem(*saved[3]),
            vmem(*saved[4]),
            vmem(*saved[5]),
            vmem(*saved[6]),
            vmem(*saved[7]),
            vmem(*saved[8]),
            vmem(*saved[9]),
            dma((count,)),
            dma((count, 13)),
            dma((count, 13)),
            dma((8, 2)),
            dma((len(saved),)),
            dma((2,)),
            dma((2,)),
        ],
        compiler_params=pltpu.CompilerParams(
            collective_id=1, has_side_effects=True, vmem_limit_bytes=VMEM_BYTES
        ),
        name="forward",
    )(layer_input, gains[0], gains[1], cosine, sine, first, last, *packs)
    return [part.reshape(2, 16 * rows, lanes) for part in outs[:PACKS]], outs[PACKS:]


def start(copies):
    for copy in copies:
        copy.start()


def wait(copies):
    for copy in copies:
        copy.wait()


class Scatter:
    def __init__(self, at, grad_ref, parts, sums, temps, sems, out_ref):
        self.at, self.grad, self.sums, self.temps = at, grad_ref, sums, temps
        self.from_twin, self.from_far, self.from_near, self.from_line = parts
        self.sent, self.came, self.loaded, self.stored = sems
        self.out_ref = out_ref
        x, y = at.x, at.y
        self.mine = [(at.xb, at.yb), (1 - x, 1 - y), (at.xa, at.ya), (x, y)]
        self.theirs = [(at.xa, at.ya), (1 - x, 1 - y), (at.xb, at.yb), (x, y)]
        to_far, to_near, to_line, result = sums
        self.steps = []
        for i, (pack, cut) in enumerate(SCATTER_PLAN):
            lanes = result.shape[2]

            def send(src, dst, slot, device, i=i):
                return remote(src, dst, self.sent.at[i, slot], self.came.at[i, slot], device)

            self.steps.append(
                {
                    "twin": [
                        send(self.line(i, self.theirs[j], 1 - at.c), self.from_twin.at[i, j], j, at.twin)
                        for j in range(4)
                    ],
                    "far": [
                        send(to_far.at[i % RING, j], self.from_far.at[i, j], 4 + j, at.far) for j in range(2)
                    ],
                    "near": send(to_near.at[i % RING], self.from_near.at[i], 6, at.near),
                    "line": [
                        send(to_line.at[i % RING, k], self.from_line.at[i, k], 7 + k, at.line[k])
                        for k in range(3)
                    ],
                    "store": pltpu.make_async_copy(
                        result.at[i % RING], out_ref.at[pack, :, pl.ds(cut * lanes, lanes)], self.stored.at[i]
                    ),
                }
            )

    def line(self, i, place, core):
        size = self.sums[3].shape[1]
        return self.grad.at[i, place[0], :, place[1], pl.ds(pl.multiple_of(core * size, 8), size)]

    def load(self, src, dst, k):
        copy = pltpu.make_async_copy(src, dst, self.loaded.at[k])
        copy.start()
        return copy

    def begin(self, i):
        for j in (1, 0, 2, 3):
            self.steps[i]["twin"][j].start()

    def first(self, i):
        step, to_far, temp, slot = self.steps[i], self.sums[0], self.temps[0], i % RING
        self.free(i, lambda old: old["far"])
        copies = []
        for j in (1, 0):
            own = self.load(self.line(i, self.mine[j], self.at.c), to_far.at[slot, j], 2 * j)
            step["twin"][j].wait_recv()
            copies.append((j, [own, self.load(self.from_twin.at[i, j], temp.at[j], 2 * j + 1)]))
        for j, pair in copies:
            wait(pair)

            def body(q, carry, j=j):
                to_far[slot, j, q] = (to_far[slot, j, q].astype(f32) + temp[j, q].astype(f32)).astype(bf16)
                return carry

            lax.fori_loop(0, 4, body, 0)
            step["far"][j].start()

    def second(self, i):
        step, to_near, temp, slot = self.steps[i], self.sums[1], self.temps[0], i % RING
        self.free(i, lambda old: [old["near"]])
        copies = [self.load(self.line(i, self.mine[2], self.at.c), to_near.at[slot], 4)]
        step["twin"][2].wait_recv()
        copies.append(self.load(self.from_twin.at[i, 2], temp.at[0], 5))
        step["far"][1].wait_recv()
        copies.append(self.load(self.from_far.at[i, 1], temp.at[1], 6))
        wait(copies)

        def body(q, carry):
            value = to_near[slot, q].astype(f32) + temp[0, q].astype(f32) + temp[1, q].astype(f32)
            to_near[slot, q] = value.astype(bf16)
            return carry

        lax.fori_loop(0, 4, body, 0)
        step["near"].start()

    def third(self, i):
        step, temp, slot = self.steps[i], self.temps[0], i % RING
        to_line, result = self.sums[2:]
        self.free(i, lambda old: old["line"])
        if i >= RING:
            self.steps[slot]["store"].wait()
        copies = [self.load(self.line(i, self.mine[3], self.at.c), temp.at[0], 7)]
        step["twin"][3].wait_recv()
        copies.append(self.load(self.from_twin.at[i, 3], temp.at[1], 8))
        step["far"][0].wait_recv()
        copies.append(self.load(self.from_far.at[i, 0], temp.at[2], 9))
        step["near"].wait_recv()
        copies.append(self.load(self.from_near.at[i], temp.at[3], 10))
        wait(copies)

        def total(q):
            return (temp[0, q].astype(f32) + temp[1, q].astype(f32)) + (
                temp[2, q].astype(f32) + temp[3, q].astype(f32)
            )

        for k in range(3):
            to_line[slot, k] = total(self.at.others[k]).astype(bf16)
            step["line"][k].start()
        result[slot] = total(self.at.z)

    def fourth(self, i):
        step, temp, result, slot = self.steps[i], self.temps[1], self.sums[3], i % RING
        copies = []
        for k in range(3):
            step["line"][k].wait_recv()
            copies.append(self.load(self.from_line.at[i, k], temp.at[k], 11 + k))
        wait(copies)
        result[slot] = result[slot] + temp[0].astype(f32) + temp[1].astype(f32) + temp[2].astype(f32)
        step["store"].start()

    def free(self, i, sends):
        if i >= RING:
            for copy in sends(self.steps[i - RING]):
                copy.wait_send()

    def finish(self):
        for i, step in enumerate(self.steps):
            for copy in step["twin"]:
                copy.wait_send()
            if i + RING >= len(self.steps):
                for copy in step["far"] + [step["near"]] + step["line"]:
                    copy.wait_send()
                step["store"].wait()


def flip_rows(src, dst):
    for tile in range(src.shape[1] // LANES):
        cols = pl.ds(tile * LANES, LANES)
        dst[cols, :] = src[:, cols].astype(f32).T.astype(bf16)


def backward_kernel(*refs):
    grad_out_ref, x_ref, gain_one_ref, gain_two_ref, cos_ref, sin_ref, first_ref, last_ref = refs[:8]
    full_refs, kept = refs[8:12], refs[12:21]
    attn_in_ref, y_ref, kv_ref, mix_ref, logs_ref, residual_ref, mlp_in_ref, acts_ref, hidden_ref = kept
    sum_ref, grad_in_ref, gain_sum_ref, grad_ref = refs[21:25]
    parts = refs[25:29]
    scratch = refs[29:]
    sums, temps = scratch[:4], scratch[4:6]
    staging, grad_res, branch, kv_out, kv_in, gains = scratch[6:12]
    sems, pulled, pushed, kv_sent, kv_came, gain_sent, gain_came = scratch[12:16], *scratch[16:22]
    at = Place()
    at.greet()
    scatter = Scatter(at, grad_ref, parts, sums, temps, sems, sum_ref)
    dma = pltpu.SemaphoreType.DMA
    vmem = pltpu.VMEM
    tokens, width = grad_res.shape
    lanes = hidden_ref.shape[2]
    size = lanes // 2
    tiles = size // 256

    def pull(src, dst, k):
        return pltpu.make_async_copy(src, dst, pulled.at[k])

    def pull_cut(pack, cut, dst, k):
        return [
            pull(
                full_refs[pack].at[half].reshape(width, lanes).at[:, pl.ds(cut * size, size)],
                dst.at[:, pl.ds(half * size, size)],
                k + half,
            )
            for half in range(2)
        ]

    def push(i):
        slot = i % 2
        return [
            pltpu.make_async_copy(
                staging.at[slot, half], grad_ref.at[i, half].reshape(width, size), pushed.at[slot, half]
            )
            for half in range(2)
        ]

    def weight_grad(i, left, right):
        def body(k, carry):
            half, cols = k // tiles, pl.ds(pl.multiple_of((k % tiles) * 256, 256), 256)
            staging[i % 2, half, :, cols] = dot_nn(left[...], right[half, :, cols]).astype(bf16)
            return carry

        lax.fori_loop(0, 2 * tiles, body, 0)
        start(push(i))

    def feed_forward(weights, acts, hidden, grad_out, out_turned, in_turned, grad_acts):
        def pulls(cut):
            cols = pl.ds(cut * size, size)
            return {
                "hidden": [pull(hidden_ref.at[:, :, cols], hidden, 0)],
                "down": pull_cut(3, cut, weights.at[0], 1),
                "acts": [pull(acts_ref.at[:, :, :, cols], acts, 3)],
                "gate": pull_cut(1, cut, weights.at[1], 4) + pull_cut(2, cut, weights.at[2], 6),
            }

        copies = pulls(0)
        given = [pull(grad_out_ref, grad_out, 8), pull(mlp_in_ref, branch, 9)]
        start(given + copies["hidden"] + copies["down"] + copies["acts"] + copies["gate"])
        wait(given)
        flip_rows(grad_out, out_turned)
        flip_rows(branch, in_turned)
        later = pulls(1)
        for cut in range(2):
            i = 3 * cut
            wait(copies["hidden"])
            if cut == 1:
                wait(push(i - 2))
                scatter.begin(i - 2)
            weight_grad(i, out_turned, hidden)
            if cut == 0:
                start(later["hidden"])
            else:
                scatter.first(i - 2)
            wait(copies["down"] + copies["acts"])

            def act_grads(k, carry):
                half, tile = k // tiles, k % tiles
                cols = pl.ds(pl.multiple_of(tile * 256, 256), 256)
                grad = dot_nn(grad_out[...], weights[0, :, pl.ds(pl.multiple_of(k * 256, 256), 256)])
                gate, up = acts[half, 0, :, cols], acts[half, 1, :, cols]
                sigmoid = jax.nn.sigmoid(gate)
                grad_acts[0, half, :, cols] = (
                    grad * up * sigmoid * (1.0 + gate * (1.0 - sigmoid))
                ).astype(bf16)
                grad_acts[1, half, :, cols] = (grad * gate * sigmoid).astype(bf16)
                return carry

            lax.fori_loop(0, 2 * tiles, act_grads, 0)
            if cut == 0:
                start(later["down"] + later["acts"])
            else:
                wait(push(i - 1))
                scatter.begin(i - 1)
            weight_grad(i + 1, in_turned, grad_acts.at[0])
            wait(push(i))
            scatter.begin(i)
            if cut == 1:
                scatter.first(i - 1)
            weight_grad(i + 2, in_turned, grad_acts.at[1])
            scatter.first(i)
            wait(copies["gate"])

            def rows_of(k, carry, cut=cut):
                rows = pl.ds(pl.multiple_of(k * 256, 256), 256)
                total = None if cut == 0 else grad_res[rows, :]
                for half in range(2):
                    for part in range(2):
                        term = dot_nt(
                            grad_acts[part, half, rows, :], weights[1 + part, :, pl.ds(half * size, size)]
                        )
                        total = term if total is None else total + term
                grad_res[rows, :] = total
                return carry

            lax.fori_loop(0, tokens // 256, rows_of, 0)
            if cut == 0:
                start(later["gate"])
            copies = later

    pl.run_scoped(
        feed_forward,
        vmem((3, width, lanes), bf16),
        vmem((2, 2, tokens, size), f32),
        vmem((2, tokens, size), bf16),
        vmem((tokens, width), bf16),
        vmem((width, tokens), bf16),
        vmem((width, tokens), bf16),
        vmem((2, 2, tokens, size), bf16),
    )
    wait(push(4))
    scatter.begin(4)
    wait(push(5))
    scatter.begin(5)
    scatter.first(4)

    def second_norm(residual, grad_out):
        copies = [pull(residual_ref, residual, 0), pull(grad_out_ref, grad_out, 1)]
        start(copies)
        wait(copies)
        gain = gain_two_ref[...]

        def rows_of(k, carry):
            rows = pl.ds(pl.multiple_of(k * 128, 128), 128)
            value, grad = residual[rows, :], grad_res[rows, :]
            inverse = lax.rsqrt(jnp.mean(value * value, axis=1, keepdims=True) + eps)
            normed = value * inverse
            scaled = grad * gain
            inner = jnp.mean(scaled * normed, axis=1, keepdims=True)
            total = grad_out[rows, :].astype(f32) + inverse * (scaled - normed * inner)
            grad_res[rows, :] = total
            branch[rows, :] = total.astype(bf16)
            return carry + jnp.sum(grad * normed, axis=0, keepdims=True)

        gains[0, pl.ds(1, 1), :] = lax.fori_loop(0, tokens // 128, rows_of, jnp.zeros((1, width), f32))

    gains[0] = jnp.zeros(gains.shape[1:], f32)
    pl.run_scoped(second_norm, vmem((tokens, width), f32), vmem((tokens, width), bf16))
    scatter.first(5)

    def attention(weights, y, kv, dup, flip, acc, mix, grad_mix, grad_y, turned, logs, grad_kv, held):
        copies = [
            pull(full_refs[0].at[half].reshape(width, lanes), weights.at[half], half) for half in range(2)
        ] + [
            pull(y_ref, y, 2),
            pull(kv_ref, kv, 3),
            pull(mix_ref, mix, 4),
            pull(logs_ref, logs, 5),
            pull(attn_in_ref, held, 6),
        ]
        start(copies)
        scatter.second(0)
        wait(copies[:2])

        def mix_of(k, carry):
            half, rows = k // 2, pl.ds(pl.multiple_of((k % 2) * 256, 256), 256)
            grad_mix[half, rows, :] = dot_nn(
                branch[rows, :], weights[half, :, pl.ds(7 * LANES, 5 * LANES)]
            ).astype(bf16)
            return carry

        lax.fori_loop(0, 4, mix_of, 0)
        scatter.second(1)
        wait(copies[2:])
        mine = pl.ds(pl.multiple_of(at.x * tokens, tokens), tokens)
        other = pl.ds(pl.multiple_of((1 - at.x) * tokens, tokens), tokens)
        block = 256
        steps = tokens // block

        def send_kv(half):
            return remote(kv_out.at[half], kv_in.at[half], kv_sent.at[half], kv_came.at[half], at.cross)

        def rows_of(i, carry):
            half = i // steps

            @pl.when(i % steps == 0)
            def _():
                load_groups(kv, half, dup, flip)
                acc[...] = jnp.zeros_like(acc)

            attend_back_rows(
                half, i % steps, block, y, dup, flip, first_ref, last_ref, logs, grad_mix, cos_ref, sin_ref, grad_y, acc
            )

            @pl.when(i % steps == steps - 1)
            def _():
                join_groups(acc, grad_kv, half)
                kv_out[half] = grad_kv[half, other, :].astype(bf16)

            for k, work in enumerate(
                [
                    lambda: (scatter.third(0), scatter.second(2)),
                    lambda: (send_kv(0).start(), scatter.third(1), scatter.second(3)),
                    lambda: (scatter.third(2), scatter.fourth(0), scatter.second(4)),
                    lambda: (send_kv(1).start(), scatter.third(3), scatter.fourth(1), scatter.second(5)),
                ]
            ):

                @pl.when(i == k)
                def _(work=work):
                    work()

            return carry

        lax.fori_loop(0, 2 * steps, rows_of, 0)
        flip_rows(held, turned.at[0])
        flip_rows(branch, turned.at[1])
        scatter.third(4)
        scatter.fourth(2)
        lane = lane_of((tokens, LANES))
        lower = lane % HEAD < HEAD // 2
        for half in range(2):
            send_kv(half).wait()
            for tile in range(3):
                cols = pl.ds(tile * LANES, LANES)
                total = grad_kv[half, mine, cols] + kv_in[half, :, cols].astype(f32)
                if tile < 2:
                    back = turn_back(total, cos_ref[...], sin_ref[...], lower)
                    total = back if tile == 0 else jnp.where(lane < HEAD, back, total)
                grad_y[half, :, cols] = total.astype(bf16)

        def first_part(k, carry):
            half, cols = k // tiles, pl.ds(pl.multiple_of((k % tiles) * 256, 256), 256)
            staging[0, half, :, cols] = dot_nn(turned[0], grad_y[half, :, cols]).astype(bf16)
            return carry

        lax.fori_loop(0, 2 * tiles, first_part, 0)
        start(push(6))
        for half in range(2):
            tail = dot_nn(turned[0], grad_y[half, :, pl.ds(6 * LANES, 2 * LANES)])
            head = dot_nn(turned[1], mix[half, :, pl.ds(0, LANES)])
            staging[1, half, :, pl.ds(0, LANES)] = tail[:, :LANES].astype(bf16)
            staging[1, half, :, pl.ds(LANES, LANES)] = (tail[:, LANES:] + head).astype(bf16)
            for k in range(2):
                staging[1, half, :, pl.ds((2 + 2 * k) * LANES, 2 * LANES)] = dot_nn(
                    turned[1], mix[half, :, pl.ds((1 + 2 * k) * LANES, 2 * LANES)]
                ).astype(bf16)
        start(push(7))
        wait(push(6))
        scatter.begin(6)
        scatter.third(5)
        scatter.fourth(3)
        wait(push(7))
        scatter.begin(7)
        scatter.first(6)
        scatter.first(7)
        load_x = pull(x_ref, held, 6)
        load_x.start()
        gain = gain_one_ref[...]
        load_x.wait()

        def input_rows(k, carry):
            rows = pl.ds(pl.multiple_of(k * 128, 128), 128)
            grad = dot_nt(grad_y[0, rows, :], weights[0, :, pl.ds(0, 8 * LANES)]) + dot_nt(
                grad_y[1, rows, :], weights[1, :, pl.ds(0, 8 * LANES)]
            )
            value = held[rows, :].astype(f32)
            inverse = lax.rsqrt(jnp.mean(value * value, axis=1, keepdims=True) + eps)
            normed = value * inverse
            scaled = grad * gain
            inner = jnp.mean(scaled * normed, axis=1, keepdims=True)
            branch[rows, :] = (grad_res[rows, :] + inverse * (scaled - normed * inner)).astype(bf16)
            return carry + jnp.sum(grad * normed, axis=0, keepdims=True)

        gains[0, pl.ds(0, 1), :] = lax.fori_loop(0, tokens // 128, input_rows, jnp.zeros((1, width), f32))

    keys = kv_ref.shape[1]
    pl.run_scoped(
        attention,
        vmem((2, width, lanes), bf16),
        vmem(y_ref.shape, bf16),
        vmem(kv_ref.shape, bf16),
        vmem((6, keys, LANES), bf16),
        vmem((6, LANES, keys), bf16),
        vmem((6, keys, LANES), f32),
        vmem(mix_ref.shape, bf16),
        vmem(mix_ref.shape, bf16),
        vmem(y_ref.shape, bf16),
        vmem((2, width, tokens), bf16),
        vmem(logs_ref.shape, f32),
        vmem((2, keys, 3 * LANES), f32),
        vmem((tokens, width), bf16),
    )
    out = pull(branch, grad_in_ref, 0)
    out.start()
    exchanges = [
        remote(gains.at[2 * k], gains.at[2 * k + 1], gain_sent.at[k], gain_came.at[k], peer)
        for k, peer in enumerate([at.twin, at.near, at.far])
    ]
    everyone = [
        remote(gains.at[6 + at.z], gains.at[6 + at.z], gain_sent.at[3 + k], gain_came.at[3 + k], at.line[k])
        for k in range(3)
    ]

    def fold(k):
        exchanges[k].wait()
        gains[6 + at.z if k == 2 else 2 * (k + 1)] = gains[2 * k] + gains[2 * k + 1]

    exchanges[0].start()
    scatter.fourth(4)
    scatter.second(6)
    fold(0)
    exchanges[1].start()
    scatter.second(7)
    scatter.fourth(5)
    fold(1)
    exchanges[2].start()
    scatter.third(6)
    fold(2)
    start(everyone)
    scatter.third(7)
    scatter.fourth(6)
    wait(everyone)
    gain_sum_ref[...] = gains[6] + gains[7] + gains[8] + gains[9]
    scatter.fourth(7)
    out.wait()
    scatter.finish()


def backward_special(grad_output, layer_input, gains, cosine, sine, first, last, packs, kept):
    tokens, width = layer_input.shape
    _, depth, lanes = packs[0].shape
    rows, size = depth // 16, lanes // 2
    count = len(SCATTER_PLAN)
    dma, vmem = pltpu.SemaphoreType.DMA, pltpu.VMEM
    anywhere = pl.BlockSpec(memory_space=pl.ANY)
    near = pl.BlockSpec(memory_space=pltpu.VMEM)
    shape = jax.ShapeDtypeStruct
    outs = pl.pallas_call(
        backward_kernel,
        out_shape=[
            shape((PACKS, rows, lanes), f32),
            shape((tokens, width), bf16),
            shape((8, width), f32),
            shape((count, 2, 4, 2, 2 * rows, size), bf16),
            shape((count, 4, 4, rows, size), bf16),
            shape((count, 2, 4, rows, size), bf16),
            shape((count, 4, rows, size), bf16),
            shape((count, 3, rows, size), bf16),
        ],
        in_specs=[anywhere] * 2 + [near] * 6 + [anywhere] * (PACKS + len(kept)),
        out_specs=[anywhere, anywhere, near] + [anywhere] * 5,
        scratch_shapes=[
            vmem((RING, 2, 4, rows, size), bf16),
            vmem((RING, 4, rows, size), bf16),
            vmem((RING, 3, rows, size), bf16),
            vmem((RING, rows, size), f32),
            vmem((4, 4, rows, size), bf16),
            vmem((3, rows, size), bf16),
            vmem((2, 2, width, size), bf16),
            vmem((tokens, width), f32),
            vmem((tokens, width), bf16),
            vmem((2, tokens, 3 * LANES), bf16),
            vmem((2, tokens, 3 * LANES), bf16),
            vmem((10, 8, width), f32),
            dma((count, 10)),
            dma((count, 10)),
            dma((14,)),
            dma((count,)),
            dma((10,)),
            dma((2, 2)),
            dma((2,)),
            dma((2,)),
            dma((6,)),
            dma((6,)),
        ],
        compiler_params=pltpu.CompilerParams(
            collective_id=2, has_side_effects=True, vmem_limit_bytes=VMEM_BYTES
        ),
        name="backward",
    )(
        grad_output,
        layer_input,
        gains[0],
        gains[1],
        cosine,
        sine,
        first,
        last,
        *[pack.reshape(2, 4, 2, 2 * rows, lanes) for pack in packs],
        *kept,
    )
    sums, grad_input, gain_sums = outs[:3]
    kv = lanes // 8
    mixed = sums[0]
    return (
        grad_input,
        gain_sums[:2],
        (
            mixed[:, 2 * kv : 5 * kv],
            mixed[:, :kv],
            mixed[:, kv : 2 * kv],
            mixed[:, 5 * kv :].T,
            sums[1],
            sums[2],
            sums[3].T,
        ),
    )


def special():
    return (lax.axis_size("row"), lax.axis_size("col")) == (16, 2)


def lane_of(shape):
    return lax.broadcasted_iota(jnp.int32, shape, len(shape) - 1)


def turn(values, cosine, sine, lower):
    ahead = pltpu.roll(values, LANES - HEAD // 2, 1)
    behind = pltpu.roll(values, HEAD // 2, 1)
    return values * cosine + jnp.where(lower, -ahead, behind) * sine


def turn_back(values, cosine, sine, lower):
    scaled = values * sine
    ahead = pltpu.roll(scaled, LANES - HEAD // 2, 1)
    behind = pltpu.roll(scaled, HEAD // 2, 1)
    return values * cosine - jnp.where(lower, -ahead, behind)


def project_half(half, attn_in_ref, weight_ref, cos_ref, sin_ref, y_ref):
    cosine, sine = cos_ref[...], sin_ref[...]
    lane = lane_of(cosine.shape)
    lower = lane % HEAD < HEAD // 2
    for pair in range(4):
        two = dot_nn(attn_in_ref[...], weight_ref[half, :, pl.ds(pair * 2 * LANES, 2 * LANES)]).astype(bf16)
        for side in range(2):
            tile = 2 * pair + side
            raw = two[:, side * LANES : (side + 1) * LANES].astype(f32)
            if tile == 2:
                out = raw
            else:
                out = turn(raw, cosine, sine, lower)
                if tile == 1:
                    out = jnp.where(lane < HEAD, out, raw)
                elif tile > 2:
                    out = out * HEAD ** (-0.5)
            y_ref[half, :, pl.ds(tile * LANES, LANES)] = out.astype(bf16)


def project_kernel(x_ref, gain_ref, weight_ref, cos_ref, sin_ref, attn_in_ref, y_ref):
    values = x_ref[...].astype(f32)
    inverse = lax.rsqrt(jnp.mean(values * values, axis=1, keepdims=True) + eps)
    attn_in_ref[...] = (values * inverse * gain_ref[...]).astype(bf16)
    for half in range(2):
        project_half(half, attn_in_ref, weight_ref, cos_ref, sin_ref, y_ref)


def head_rows(values, side, lane):
    return jnp.where((lane < HEAD) if side == 0 else (lane >= HEAD), values, jnp.zeros_like(values))


def twice(tile, side, lane):
    values = tile.astype(f32)
    other = pltpu.roll(values, HEAD, 1)
    keep = (lane < HEAD) if side == 0 else (lane >= HEAD)
    return jnp.where(keep, values, other)


def load_groups(kv_ref, half, dup_ref, flip_ref):
    for slot in range(6):
        tile = kv_ref[half, :, pl.ds((slot // 2) * LANES, LANES)]
        both = twice(tile, slot % 2, lane_of(tile.shape))
        dup_ref[slot] = both.astype(bf16)
        flip_ref[slot] = both.T.astype(bf16)


def seen(first_ref, last_ref, rows, keys):
    index = lax.broadcasted_iota(jnp.int32, (keys, rows.size), 0)
    return (index >= first_ref[:, rows]) & (index <= last_ref[:, rows])


def attend_rows(half, step, block, y_ref, dup_ref, flip_ref, first_ref, last_ref, mix_ref, log_ref):
    keys = dup_ref.shape[1]
    lane = lane_of((block, LANES))
    rows = pl.ds(pl.multiple_of(step * block, block), block)
    allowed = seen(first_ref, last_ref, rows, keys)
    previous = jnp.zeros((block, LANES), f32)
    for head in range(9):
        group = head // 3
        query = head_rows(y_ref[half, rows, pl.ds((3 + head // 2) * LANES, LANES)], head % 2, lane)
        scores = jnp.where(allowed, dot_nt(dup_ref[group], query), neg_fill)
        top = jnp.max(scores, axis=0, keepdims=True)
        powers = jnp.exp(scores - top)
        total = jnp.sum(powers, axis=0, keepdims=True)
        probs = (powers * (1.0 / total)).astype(bf16)
        mixed = dot_nn(flip_ref[3 + group], probs).T
        log_ref[half, pl.ds(head, 1), rows] = top + jnp.log(total)
        if head % 2 == 0:
            tile = jnp.where(lane < HEAD, previous, mixed)
            mix_ref[half, rows, pl.ds((head // 2) * LANES, LANES)] = tile.astype(bf16)
        previous = mixed


def attend_kernel(block, y_ref, kv_ref, first_ref, last_ref, mix_ref, log_ref, dup_ref, flip_ref):
    load_groups(kv_ref, 0, dup_ref, flip_ref)

    def rows_of(step, carry):
        attend_rows(0, step, block, y_ref, dup_ref, flip_ref, first_ref, last_ref, mix_ref, log_ref)
        return carry

    lax.fori_loop(0, y_ref.shape[1] // block, rows_of, 0)


def attend_back_rows(
    half, step, block, y_ref, dup_ref, flip_ref, first_ref, last_ref, log_ref, grad_ref, cos_ref, sin_ref, out_ref, acc_ref
):
    keys = dup_ref.shape[1]
    lane = lane_of((block, LANES))
    lower = lane % HEAD < HEAD // 2
    rows = pl.ds(pl.multiple_of(step * block, block), block)
    allowed = seen(first_ref, last_ref, rows, keys)
    previous = None
    for head in range(9):
        group = head // 3
        query = head_rows(y_ref[half, rows, pl.ds((3 + head // 2) * LANES, LANES)], head % 2, lane)
        upstream = head_rows(
            grad_ref[half, rows, pl.ds(((head + 1) // 2) * LANES, LANES)], (head + 1) % 2, lane
        )
        scores = jnp.where(allowed, dot_nt(dup_ref[group], query), neg_fill)
        probs = jnp.exp(scores - log_ref[half, pl.ds(head, 1), rows])
        grad_probs = dot_nt(dup_ref[3 + group], upstream)
        inner = jnp.sum(probs * grad_probs, axis=0, keepdims=True)
        grad_scores = (probs * (grad_probs - inner)).astype(bf16)
        acc_ref[3 + group] += dot_nn(probs.astype(bf16), upstream)
        acc_ref[group] += dot_nn(grad_scores, query)
        grad_query = dot_nn(flip_ref[group], grad_scores).T
        if head % 2 == 1 or head == 8:
            if head == 8:
                tile = jnp.where(lane < HEAD, grad_query, 0.0)
            else:
                tile = jnp.where(lane < HEAD, previous, grad_query)
            tile = turn_back(tile * HEAD ** (-0.5), cos_ref[rows, :], sin_ref[rows, :], lower)
            out_ref[half, rows, pl.ds((3 + head // 2) * LANES, LANES)] = tile.astype(bf16)
        previous = grad_query


def join_groups(acc_ref, out_ref, half):
    lane = lane_of((acc_ref.shape[1], LANES))
    for tile in range(3):
        low, high = acc_ref[2 * tile], acc_ref[2 * tile + 1]
        low = low + pltpu.roll(low, HEAD, 1)
        high = high + pltpu.roll(high, HEAD, 1)
        out_ref[half, :, pl.ds(tile * LANES, LANES)] = jnp.where(lane < HEAD, low, high)


def attend_back_kernel(
    block, y_ref, kv_ref, first_ref, last_ref, log_ref, grad_ref, cos_ref, sin_ref, dq_ref, dkv_ref, dup_ref, flip_ref, acc_ref
):
    load_groups(kv_ref, 0, dup_ref, flip_ref)
    acc_ref[...] = jnp.zeros_like(acc_ref)

    def rows_of(step, carry):
        attend_back_rows(
            0, step, block, y_ref, dup_ref, flip_ref, first_ref, last_ref, log_ref, grad_ref, cos_ref, sin_ref, dq_ref, acc_ref
        )
        return carry

    lax.fori_loop(0, y_ref.shape[1] // block, rows_of, 0)
    join_groups(acc_ref, dkv_ref, 0)


def full_spec(shape):
    return pl.BlockSpec(shape, lambda i: (0,) * len(shape))


def half_spec(shape):
    return pl.BlockSpec((1,) + shape[1:], lambda i: (i,) + (0,) * (len(shape) - 1))


def params():
    return pltpu.CompilerParams(vmem_limit_bytes=VMEM_BYTES)


def project(layer_input, gain, first_pack, cosine, sine):
    tokens, width = layer_input.shape
    vm = pl.BlockSpec(memory_space=pltpu.VMEM)
    return pl.pallas_call(
        project_kernel,
        grid=(1,),
        out_shape=(
            jax.ShapeDtypeStruct((tokens, width), bf16),
            jax.ShapeDtypeStruct((2, tokens, 8 * LANES), bf16),
        ),
        in_specs=[
            full_spec((tokens, width)),
            full_spec((1, width)),
            full_spec((2, width, 8 * LANES)),
            full_spec((tokens, LANES)),
            full_spec((tokens, LANES)),
        ],
        out_specs=(full_spec((tokens, width)), full_spec((2, tokens, 8 * LANES))),
        compiler_params=params(),
        name="project",
    )(layer_input, gain, first_pack, cosine, sine)


def attend(y, kv, first, last):
    tokens, keys = y.shape[1], kv.shape[1]
    block = min(256, tokens)
    return pl.pallas_call(
        lambda *refs: attend_kernel(block, *refs),
        grid=(2,),
        out_shape=(
            jax.ShapeDtypeStruct((2, tokens, 5 * LANES), bf16),
            jax.ShapeDtypeStruct((2, 16, tokens), f32),
        ),
        in_specs=[half_spec(y.shape), half_spec(kv.shape), full_spec((1, tokens)), full_spec((1, tokens))],
        out_specs=(half_spec((2, tokens, 5 * LANES)), half_spec((2, 16, tokens))),
        scratch_shapes=[pltpu.VMEM((6, keys, LANES), bf16), pltpu.VMEM((6, LANES, keys), bf16)],
        compiler_params=params(),
        name="attend",
    )(y, kv, first, last)


def attend_back(y, kv, first, last, logs, grad, cosine, sine):
    tokens, keys = y.shape[1], kv.shape[1]
    block = min(256, tokens)
    return pl.pallas_call(
        lambda *refs: attend_back_kernel(block, *refs),
        grid=(2,),
        out_shape=(
            jax.ShapeDtypeStruct((2, tokens, 8 * LANES), bf16),
            jax.ShapeDtypeStruct((2, keys, 3 * LANES), f32),
        ),
        in_specs=[
            half_spec(y.shape),
            half_spec(kv.shape),
            full_spec((1, tokens)),
            full_spec((1, tokens)),
            half_spec(logs.shape),
            half_spec(grad.shape),
            full_spec((tokens, LANES)),
            full_spec((tokens, LANES)),
        ],
        out_specs=(half_spec((2, tokens, 8 * LANES)), half_spec((2, keys, 3 * LANES))),
        scratch_shapes=[
            pltpu.VMEM((6, keys, LANES), bf16),
            pltpu.VMEM((6, LANES, keys), bf16),
            pltpu.VMEM((6, keys, LANES), f32),
        ],
        compiler_params=params(),
        name="attend_back",
    )(y, kv, first, last, logs, grad, cosine, sine)


def rope_tables(position):
    lane_index = (jnp.arange(LANES, dtype=jnp.int32) % (HEAD // 2)).astype(f32)
    frequency = jnp.exp(lane_index * (-2.0 * math.log(rope_base) / HEAD))
    angles = position[:, None] * frequency[None, :]
    return jnp.cos(angles), jnp.sin(angles)


def shards(
    layer_input,
    attn_gain,
    mlp_gain,
    query_weight,
    key_weight,
    value_weight,
    out_weight,
    gate_weight,
    up_weight,
    down_weight,
    seq_ids,
    block_ends,
    grad_output,
):
    tokens, width = layer_input.shape
    span = seq_ids.shape[0]
    start = lax.axis_index("col") * tokens
    index = jnp.arange(span, dtype=jnp.int32)
    in_first = seq_ids == seq_ids[0]
    seq_first = jnp.where(in_first, 0, jnp.sum(in_first.astype(jnp.int32)))
    block_last = block_ends - lax.axis_index("row") * span
    own_first = lax.dynamic_slice_in_dim(seq_first, start, tokens)
    own_last = lax.dynamic_slice_in_dim(block_last, start, tokens)
    position = lax.dynamic_slice_in_dim(index - seq_first, start, tokens).astype(f32)
    cosine, sine = rope_tables(position)
    own_first, own_last = own_first[None, :], own_last[None, :]
    gain_one = attn_gain.astype(f32)[None, :]
    gain_two = mlp_gain.astype(f32)[None, :]

    weights = (query_weight, key_weight, value_weight, out_weight, gate_weight, up_weight, down_weight)
    own = layer_input.astype(f32)
    if special():
        mine = jnp.concatenate([key_weight, value_weight, query_weight, out_weight.T], axis=1)
        packs, kept = forward_special(
            layer_input,
            (gain_one, gain_two),
            cosine,
            sine,
            own_first,
            own_last,
            (mine, gate_weight, up_weight, down_weight.T),
        )
        grad_input, gain_sums, weight_sums = backward_special(
            grad_output, layer_input, (gain_one, gain_two), cosine, sine, own_first, own_last, packs, kept[:9]
        )
        return (kept[9], grad_input, gain_sums[0], gain_sums[1]) + tuple(weight_sums)
    pack_first, pack_gate, pack_up, pack_down = gather_any(weights)
    attn_in, y = project(layer_input, gain_one, pack_first, cosine, sine)
    kv = lax.all_gather(y[:, :, : 3 * LANES], "col", axis=1, tiled=True)
    mix, logs = attend(y, kv, own_first, own_last)
    pack_out = pack_first[:, :, 7 * LANES :]
    branch = jnp.einsum("htq,hdq->td", mix, pack_out, preferred_element_type=f32)
    residual = own + branch
    inv_two = lax.rsqrt(jnp.mean(residual * residual, axis=1, keepdims=True) + eps)
    normed_two = residual * inv_two
    mlp_in = (normed_two * gain_two).astype(bf16)
    gate_act = jnp.einsum("td,hdf->htf", mlp_in, pack_gate, preferred_element_type=f32)
    up_act = jnp.einsum("td,hdf->htf", mlp_in, pack_up, preferred_element_type=f32)
    hidden = (jax.nn.silu(gate_act) * up_act).astype(bf16)
    layer_output = (
        residual + jnp.einsum("htf,hdf->td", hidden, pack_down, preferred_element_type=f32)
    ).astype(bf16)
    grad_down = jnp.einsum("td,htf->hdf", grad_output, hidden, preferred_element_type=f32).astype(bf16)
    grad_hidden = jnp.einsum("td,hdf->htf", grad_output, pack_down, preferred_element_type=f32)
    sigmoid = jax.nn.sigmoid(gate_act)
    grad_gate_act = (grad_hidden * up_act * sigmoid * (1.0 + gate_act * (1.0 - sigmoid))).astype(bf16)
    grad_up_act = (grad_hidden * gate_act * sigmoid).astype(bf16)
    grad_gate = jnp.einsum("td,htf->hdf", mlp_in, grad_gate_act, preferred_element_type=f32).astype(bf16)
    grad_up = jnp.einsum("td,htf->hdf", mlp_in, grad_up_act, preferred_element_type=f32).astype(bf16)
    grad_mlp_in = jnp.einsum(
        "htf,hdf->td", grad_gate_act, pack_gate, preferred_element_type=f32
    ) + jnp.einsum("htf,hdf->td", grad_up_act, pack_up, preferred_element_type=f32)
    scaled_two = grad_mlp_in * gain_two
    inner_two = jnp.mean(scaled_two * normed_two, axis=1, keepdims=True)
    grad_residual = grad_output.astype(f32) + inv_two * (scaled_two - normed_two * inner_two)
    grad_mlp_gain = jnp.sum(grad_mlp_in * normed_two, axis=0)
    grad_branch = grad_residual.astype(bf16)
    grad_mixture = jnp.einsum("td,hdq->htq", grad_branch, pack_out, preferred_element_type=f32).astype(bf16)
    grad_q, grad_kv = attend_back(y, kv, own_first, own_last, logs, grad_mixture, cosine, sine)
    grad_kv = lax.psum_scatter(grad_kv, "col", scatter_dimension=1, tiled=True)
    key_cos, key_sin = jnp.tile(cosine, (1, 3)), jnp.tile(sine, (1, 3))
    lane = jnp.arange(3 * LANES, dtype=jnp.int32)
    is_key = lane < 3 * HEAD
    scaled = grad_kv * key_sin
    turned = jnp.where(
        lane % HEAD < HEAD // 2, -jnp.roll(scaled, -(HEAD // 2), axis=2), jnp.roll(scaled, HEAD // 2, axis=2)
    )
    grad_kv = jnp.where(is_key, grad_kv * key_cos - turned, grad_kv).astype(bf16)
    grad_y = jnp.concatenate([grad_kv, grad_q[:, :, 3 * LANES :]], axis=2)
    grad_proj = jnp.einsum("td,htf->hdf", attn_in, grad_y, preferred_element_type=f32)
    grad_out = jnp.einsum("td,htq->hdq", grad_branch, mix, preferred_element_type=f32)
    grad_first = jnp.concatenate(
        [
            grad_proj[:, :, : 7 * LANES],
            grad_proj[:, :, 7 * LANES :] + grad_out[:, :, :LANES],
            grad_out[:, :, LANES:],
        ],
        axis=2,
    ).astype(bf16)
    grad_attn_in = jnp.einsum(
        "htf,hdf->td", grad_y, pack_first[:, :, : 8 * LANES], preferred_element_type=f32
    )
    inv_one = lax.rsqrt(jnp.mean(own * own, axis=1, keepdims=True) + eps)
    normed_one = own * inv_one
    scaled_one = grad_attn_in * gain_one
    inner_one = jnp.mean(scaled_one * normed_one, axis=1, keepdims=True)
    grad_input = (grad_residual + inv_one * (scaled_one - normed_one * inner_one)).astype(bf16)
    grad_attn_gain = jnp.sum(grad_attn_in * normed_one, axis=0)
    gain_sums, weight_sums = scatter_any(
        (grad_first, grad_gate, grad_up, grad_down), jnp.stack([grad_attn_gain, grad_mlp_gain])
    )
    return (layer_output, grad_input, gain_sums[0], gain_sums[1]) + tuple(weight_sums)


def solution(mesh):
    tokens_spec = P(("row", "col"), None)
    in_specs = (
        tokens_spec,
        P(),
        P(),
        P("row", "col"),
        P("row", "col"),
        P("row", "col"),
        P("col", "row"),
        P("row", "col"),
        P("row", "col"),
        P("col", "row"),
        P("row"),
        P("row"),
        tokens_spec,
    )
    out_specs = (
        tokens_spec,
        tokens_spec,
        P(),
        P(),
        P("row", "col"),
        P("row", "col"),
        P("row", "col"),
        P("col", "row"),
        P("row", "col"),
        P("row", "col"),
        P("col", "row"),
    )
    return jax.shard_map(shards, mesh=mesh, in_specs=in_specs, out_specs=out_specs, check_vma=False)
```

```python
import math

import jax
import jax.numpy as jnp
from jax import lax
from jax.experimental import pallas as pl
from jax.experimental.pallas import tpu as pltpu
from jax.sharding import PartitionSpec as P

HEAD = 64
LANES = 128
eps = 1e-05
rope_base = 10000.0
neg_fill = -1e30
f32 = jnp.float32
bf16 = jnp.bfloat16
VMEM_BYTES = 62 * 1024 * 1024


def dot_nn(a, b):
    return lax.dot_general(a, b, (((1,), (0,)), ((), ())), preferred_element_type=f32)


def dot_nt(a, b):
    return lax.dot_general(a, b, (((1,), (1,)), ((), ())), preferred_element_type=f32)


def halves(values):
    rows, cols = values.shape
    return jnp.transpose(values.reshape(rows, 2, cols // 2), (1, 0, 2))


def whole(values):
    two, rows, cols = values.shape
    return jnp.transpose(values, (1, 0, 2)).reshape(rows, two * cols)


def gather_any(weights):
    query, key, value, out, gate, up, down = weights

    def both(weight, row_axis):
        part = lax.all_gather(weight, "row", axis=row_axis, tiled=True)
        return lax.all_gather(part, "col", axis=1 - row_axis, tiled=True)

    mix = [halves(both(key, 0)), halves(both(value, 0)), halves(both(query, 0)), halves(both(out, 1).T)]
    return [
        jnp.concatenate(mix, axis=2),
        halves(both(gate, 0)),
        halves(both(up, 0)),
        halves(both(down, 1).T),
    ]


def scatter_any(grads, gains):
    first, gate, up, down = [grad.astype(f32) for grad in grads]
    kv = first.shape[2] // 8
    key, value, query, out = (
        whole(first[:, :, :kv]),
        whole(first[:, :, kv : 2 * kv]),
        whole(first[:, :, 2 * kv : 5 * kv]),
        whole(first[:, :, 5 * kv :]).T,
    )

    def both(grad, row_axis):
        part = lax.psum_scatter(grad, "row", scatter_dimension=row_axis, tiled=True)
        return lax.psum_scatter(part, "col", scatter_dimension=1 - row_axis, tiled=True)

    return (
        lax.psum(gains, ("row", "col")),
        (
            both(query, 0),
            both(key, 0),
            both(value, 0),
            both(out, 1),
            both(whole(gate), 0),
            both(whole(up), 0),
            both(whole(down).T, 1),
        ),
    )


PACKS = 4
MESH = pl.DeviceIdType.MESH


class Sides:
    def __init__(self, at, core0, core1):
        if core0 == core1:
            along_x = twin_x = int(core0 == "x")
        else:
            along_x = at.c if core0 == "y" else 1 - at.c
            twin_x = 1 - along_x
        self.near_x, self.near_y, self.far_x, self.far_y = self.spots(at, along_x)
        self.near = at.device(self.near_x, at.z, self.near_y, at.c)
        self.far = at.device(self.far_x, at.z, self.far_y, at.c)
        twin = self.spots(at, twin_x)
        rest = (1 - at.x, 1 - at.y)
        self.order = [(self.far_x, self.far_y), rest, (self.near_x, self.near_y), (at.x, at.y)]
        self.twin_order = [twin[2:], rest, twin[:2], (at.x, at.y)]

    @staticmethod
    def spots(at, along_x):
        x, y = at.x, at.y
        near = (x + along_x * (1 - 2 * x), y + (1 - along_x) * (1 - 2 * y))
        far = (x + (1 - along_x) * (1 - 2 * x), y + along_x * (1 - 2 * y))
        return near + far


class Place:
    def __init__(self):
        row, x = lax.axis_index("row"), lax.axis_index("col")
        z, y, c = row // 4, (row // 2) % 2, row % 2
        self.x, self.z, self.y, self.c = x, z, y, c
        self.xa, self.ya = jnp.where(c == 0, 1 - x, x), jnp.where(c == 0, y, 1 - y)
        self.xb, self.yb = jnp.where(c == 0, x, 1 - x), jnp.where(c == 0, 1 - y, y)
        self.others = [(z + k) % 4 for k in (1, 2, 3)]
        self.line = [self.device(x, other, y, c) for other in self.others]
        self.near = self.device(self.xa, z, self.ya, c)
        self.far = self.device(self.xb, z, self.yb, c)
        self.twin = self.device(x, z, y, 1 - c)
        self.cross = self.device(1 - x, z, y, c)

    @staticmethod
    def device(x, z, y, c):
        return ((z * 2 + y) * 2 + c, x)

    def greet(self):
        barrier = pltpu.get_barrier_semaphore()
        for peer in self.line + [self.near, self.far, self.twin]:
            pl.semaphore_signal(barrier, inc=1, device_id=peer, device_id_type=MESH)
        pl.semaphore_wait(barrier, 6)


def remote(src, dst, send, recv, device):
    return pltpu.make_async_remote_copy(
        src_ref=src, dst_ref=dst, send_sem=send, recv_sem=recv, device_id=device, device_id_type=MESH
    )


GATHER_PLAN = [
    (0, 0, 512, 0, "y", "y"),
    (0, 512, 512, 0, "y", "x"),
    (0, 1024, 512, 0, "x", "x"),
    (1, 0, 768, 0, "y", "x"),
    (2, 0, 768, 1, "x", "x"),
    (1, 768, 768, 1, "y", "x"),
    (2, 768, 768, 0, "x", "x"),
    (3, 0, 768, 0, "x", "y"),
    (3, 768, 768, 1, "y", "y"),
]
FORWARD_ORDER = [
    ("B", 0), ("B", 1), ("B", 2), ("F", 0), ("B", 6), ("F", 1), ("S", 1), ("F", 2), ("S", 0), "norm",
    ("F", 6), ("B", 4), ("B", 3), ("T", 0), ("B", 7), ("S", 2), ("T", 1), "kv", ("S", 6), "q", ("B", 5),
    ("F", 4), ("F", 3), "a0", ("B", 8), ("F", 7), "a1", "a2", ("T", 2), ("S", 3), ("S", 4), ("F", 5),
    ("F", 8), "a3", ("T", 6), "br", ("T", 3), ("S", 5), ("T", 4), ("S", 8), "h0", ("T", 5), ("S", 7), "h1",
    ("T", 7), ("T", 8), "o0", "o1",
]
SCATTER_PLAN = [
    (3, 0, 1, "y", "x"),
    (1, 0, 1, "y", "x"),
    (2, 0, 1, "x", "x"),
    (3, 1, 0, "y", "x"),
    (1, 1, 0, "x", "y"),
    (2, 1, 0, "y", "y"),
    (0, 1, 0, "y", "x"),
    (0, 0, 0, "x", "y"),
]
BACKWARD_ORDER = [
    "ld", "w0", "d0", ("B", 0), "w1", "w2", ("1", 0), "m0", ("B", 1), "w3", "d1", ("1", 1), ("B", 3),
    ("2", 0), "w4", "w5", ("B", 5), ("1", 3), "m1", ("2", 1), ("B", 2), ("3", 0), ("B", 4), ("1", 5), "norm",
    "mx", ("2", 3), ("1", 2), "a0", "a1", ("2", 2), "a2", ("2", 5), ("4", 0), ("1", 4), ("3", 1), ("3", 3),
    "a3", "g1", ("B", 6), ("3", 5), ("1", 6), "kvw", ("3", 2), "g0", ("2", 4), ("B", 7), ("4", 1), "in",
    ("2", 6), ("1", 7), ("4", 3), ("3", 4), ("2", 7), ("3", 6), ("3", 7), ("4", 4), ("4", 6), ("4", 5),
    ("4", 2), ("4", 7),
]
RING = 6


class Gather:
    def __init__(self, at, plan, own_refs, out_refs, copied, sent, came):
        x, y, z = at.x, at.y, at.z
        self.plan, self.arrived = plan, set()
        size = own_refs[0].shape[0]
        rows = pl.ds(pl.multiple_of(at.c * size, 8), size)
        self.steps = []
        for i, (pack, lane, lanes, kind, *axes) in enumerate(plan):
            sides = Sides(at, *axes)
            cols = pl.ds(lane, lanes)
            own = own_refs[pack].at[:, cols]

            def one(xx, yy):
                return out_refs[pack].at[xx, z, yy, rows, cols]

            def line(xx, yy, slot, device):
                ref = out_refs[pack].at[xx, :, yy, rows, cols]
                return remote(ref, ref, sent.at[i, slot], came.at[i, slot], device)

            step = {"kind": kind, "keep": pltpu.make_async_copy(own, one(x, y), copied.at[i])}
            step["line"] = [remote(own, one(x, y), sent.at[i, k], came.at[i, k], at.line[k]) for k in range(3)]
            if kind == 0:
                step["near"] = line(x, y, 3, sides.near)
            else:
                step["near"] = remote(own, one(x, y), sent.at[i, 3], came.at[i, 3], sides.near)
                step["more"] = [
                    remote(
                        one(sides.near_x, sides.near_y),
                        one(sides.near_x, sides.near_y),
                        sent.at[i, 4 + k],
                        came.at[i, 4 + k],
                        at.line[k],
                    )
                    for k in range(3)
                ]
            step["far"] = [line(x, y, 7, sides.far), line(sides.near_x, sides.near_y, 8, sides.far)]
            step["twin"] = [
                line(xx, yy, 9 + j, at.twin)
                for j, (xx, yy) in enumerate(
                    [(x, y), (sides.near_x, sides.near_y), (sides.far_x, sides.far_y), (1 - x, 1 - y)]
                )
            ]
            self.steps.append(step)

    def begin(self, i):
        if 0 <= i < len(self.steps):
            self.steps[i]["keep"].start()
            for copy in self.steps[i]["line"]:
                copy.start()
            if self.steps[i]["kind"] == 1:
                self.steps[i]["near"].start()

    def first(self, i):
        if 0 <= i < len(self.steps):
            step = self.steps[i]
            if step["kind"] == 1:
                step["near"].wait_recv()
                for copy in step["more"]:
                    copy.start()
            for copy in step["line"]:
                copy.wait_recv()
            step["keep"].wait()
            if step["kind"] == 0:
                step["near"].start()
            step["far"][0].start()
            step["twin"][0].start()

    def second(self, i):
        if 0 <= i < len(self.steps):
            step = self.steps[i]
            for copy in [step["near"]] if step["kind"] == 0 else step["more"]:
                copy.wait_recv()
            step["far"][1].start()
            step["twin"][1].start()

    def third(self, i):
        if 0 <= i < len(self.steps):
            step = self.steps[i]
            for j in range(2):
                step["far"][j].wait_recv()
                step["twin"][2 + j].start()

    def arrive(self, *chunks):
        for i in chunks:
            if i not in self.arrived:
                self.arrived.add(i)
                for copy in self.steps[i]["twin"]:
                    copy.wait_recv()

    def arrive_lanes(self, pack, low, high):
        for i, (held, lane, lanes, *_) in enumerate(self.plan):
            if held == pack and lane < high and lane + lanes > low:
                self.arrive(i)

    def run(self, moves):
        for name, i in moves:
            {"B": self.begin, "F": self.first, "S": self.second, "T": self.third}[name](i)

    def finish(self):
        for step in self.steps:
            for copy in step["line"] + step.get("more", []) + [step["near"]] + step["far"] + step["twin"]:
                copy.wait_send()


def forward_kernel(plan, *refs):
    x_ref, gain_ref, frequency_ref, ids_ref, ends_ref = refs[:5]
    own_refs, full_refs = refs[5:9], refs[9:13]
    saved = refs[13:27]
    weights, attn_in, y, kv, dup, flip, mix, logs, residual, mlp_in, acts, hidden, output = refs[27:40]
    cos_ref, sin_ref, first_ref, last_ref = refs[40:44]
    copied, sent, came, loaded, stored, kv_sent, kv_came = refs[44:]
    gain_one_ref, gain_two_ref = gain_ref.at[pl.ds(0, 1)], gain_ref.at[pl.ds(1, 1)]
    at = Place()
    at.greet()
    gather = Gather(at, plan, own_refs, full_refs, copied, sent, came)
    tokens, width = x_ref.shape
    lanes = weights.shape[2]

    def load(pack, cut, slot, k):
        size = lanes // 2
        return [
            pltpu.make_async_copy(
                full_refs[pack].at[half].reshape(width, lanes).at[:, pl.ds(cut * size, size)],
                weights.at[slot, :, pl.ds(half * size, size)],
                loaded.at[k, half],
            )
            for half in range(2)
        ]

    def load_first(half, lane, size, k):
        part = pl.ds(lane, size)
        return pltpu.make_async_copy(
            full_refs[0].at[half].reshape(width, lanes).at[:, part], weights.at[half, :, part], loaded.at[k, half]
        )

    project_loads = [load_first(half, 0, 8 * LANES, 0) for half in range(2)]
    out_loads = [load_first(half, 8 * LANES, lanes - 8 * LANES, 1) for half in range(2)]
    gate_loads = [load(1, 0, 2, 2) + load(2, 0, 3, 3), load(1, 1, 0, 4) + load(2, 1, 1, 5)]
    down_loads = [load(3, 0, 2, 6), load(3, 1, 3, 7)]

    def save(k, ref):
        copy = pltpu.make_async_copy(ref, saved[k], stored.at[k])
        copy.start()
        return copy

    mine = pl.ds(pl.multiple_of(at.x * tokens, tokens), tokens)
    exchanges = [
        remote(kv.at[half, mine, :], kv.at[half, mine, :], kv_sent.at[half], kv_came.at[half], at.cross)
        for half in range(2)
    ]
    block = 256
    steps = tokens // block
    span = pl.ds(7 * LANES, 5 * LANES)
    size = lanes // 2
    saves = {}

    def norm():
        length = jnp.sum(1 - (ids_ref[...] & 1), axis=1, keepdims=True)
        index = at.x * tokens + lax.broadcasted_iota(jnp.int32, (1, tokens), 1)
        first_ref[...] = jnp.where(index < length, 0, length)
        row_start = lax.axis_index("row") * ids_ref.shape[1]
        last_ref[...] = ends_ref[:, pl.ds(pl.multiple_of(at.x * tokens, LANES), tokens)] - row_start
        index = at.x * tokens + lax.broadcasted_iota(jnp.int32, (tokens, LANES), 0)
        position = (index - jnp.where(index < length, 0, length)).astype(f32)
        angles = position * frequency_ref[...]
        cos_ref[...] = jnp.cos(angles)
        sin_ref[...] = jnp.sin(angles)
        for k, ref in enumerate((cos_ref, sin_ref, first_ref, last_ref)):
            saves[10 + k] = save(10 + k, ref)
        values = x_ref[...].astype(f32)
        inverse = lax.rsqrt(jnp.mean(values * values, axis=1, keepdims=True) + eps)
        attn_in[...] = (values * inverse * gain_one_ref[...]).astype(bf16)
        saves[0] = save(0, attn_in)

    def keys():
        gather.arrive_lanes(0, 0, 8 * LANES)
        start(project_loads)
        for half in range(2):
            project_loads[half].wait()
            project_tiles(half, range(2), attn_in, weights, cos_ref, sin_ref, y)
            kv[half, mine, :] = y[half, :, : 3 * LANES]
            exchanges[half].start()

    def queries():
        for half in range(2):
            project_tiles(half, range(2, 4), attn_in, weights, cos_ref, sin_ref, y)
        saves[1] = save(1, y)

    def attend_all(moves):
        def rows_of(i, carry):
            half = i // steps
            for k in range(2):

                @pl.when(i == k * steps)
                def _(k=k):
                    exchanges[k].wait()

            @pl.when(i % steps == 0)
            def _():
                load_groups(kv, half, dup, flip)

            attend_rows(half, i % steps, block, y, dup, flip, first_ref, last_ref, mix, logs)
            for k, part in enumerate(moves):
                if part:

                    @pl.when(i == k * steps // 2)
                    def _(part=part):
                        gather.run(part)

            return carry

        lax.fori_loop(0, 2 * steps, rows_of, 0)
        saves[2], saves[3], saves[4] = save(2, kv), save(3, mix), save(4, logs)

    def branch():
        gather.arrive_lanes(0, 8 * LANES, lanes)
        start(out_loads)
        wait(out_loads)

        def rows_of(i, carry):
            rows = pl.ds(pl.multiple_of(i * 256, 256), 256)
            total = x_ref[rows, :].astype(f32)
            for half in range(2):
                total = total + dot_nt(mix[half, rows, :], weights[half, :, span])
            residual[rows, :] = total
            inverse = lax.rsqrt(jnp.mean(total * total, axis=1, keepdims=True) + eps)
            mlp_in[rows, :] = (total * inverse * gain_two_ref[...]).astype(bf16)
            return carry

        lax.fori_loop(0, tokens // 256, rows_of, 0)
        saves[5], saves[6] = save(5, residual), save(6, mlp_in)

    def hide(cut):
        gather.arrive_lanes(1, cut * size, (cut + 1) * size)
        gather.arrive_lanes(2, cut * size, (cut + 1) * size)
        start(gate_loads[cut])
        wait(gate_loads[cut])
        slot = 2 - 2 * cut

        def tile_of(i, carry):
            half, tile = i // (size // 256), i % (size // 256)
            cols = pl.ds(pl.multiple_of(i * 256, 256), 256)
            into = pl.ds(pl.multiple_of(cut * size + tile * 256, 256), 256)
            gate = dot_nn(mlp_in[...], weights[slot, :, cols])
            up = dot_nn(mlp_in[...], weights[slot + 1, :, cols])
            acts[half, 0, :, into] = gate
            acts[half, 1, :, into] = up
            hidden[half, :, into] = (gate * jax.nn.sigmoid(gate) * up).astype(bf16)
            return carry

        lax.fori_loop(0, lanes // 256, tile_of, 0)
        if cut == 1:
            saves[7], saves[8] = save(7, acts), save(8, hidden)

    def finish_rows(cut):
        gather.arrive_lanes(3, cut * size, (cut + 1) * size)
        start(down_loads[cut])
        wait(down_loads[cut])
        if cut == 0:
            saves.pop(5).wait()

        def rows_of(i, carry):
            rows = pl.ds(pl.multiple_of(i * 256, 256), 256)
            total = residual[rows, :]
            for half in range(2):
                total = total + dot_nt(
                    hidden[half, rows, pl.ds(cut * size, size)], weights[2 + cut, :, pl.ds(half * size, size)]
                )
            if cut == 0:
                residual[rows, :] = total
            else:
                output[rows, :] = total.astype(bf16)
            return carry

        lax.fori_loop(0, tokens // 256, rows_of, 0)
        if cut == 1:
            saves[9] = save(9, output)

    work = {
        "norm": norm,
        "kv": keys,
        "q": queries,
        "br": branch,
        "h0": lambda: hide(0),
        "h1": lambda: hide(1),
        "o0": lambda: finish_rows(0),
        "o1": lambda: finish_rows(1),
    }
    plain, looped = split_schedule(FORWARD_ORDER)
    for entry in plain:
        if isinstance(entry, tuple):
            gather.run([entry])
        elif entry == "a":
            attend_all(looped)
        else:
            work[entry]()
    gather.finish()
    for copy in saves.values():
        copy.wait()


def forward_special(layer_input, gains, frequency, ids, ends, packs):
    plan = GATHER_PLAN
    tokens, width = layer_input.shape
    rows, lanes = packs[0].shape
    keys = 2 * tokens
    dma, vmem = pltpu.SemaphoreType.DMA, pltpu.VMEM
    anywhere = pl.BlockSpec(memory_space=pl.ANY)
    near = pl.BlockSpec(memory_space=pltpu.VMEM)
    saved = [
        ((tokens, width), bf16),
        ((2, tokens, 8 * LANES), bf16),
        ((2, keys, 3 * LANES), bf16),
        ((2, tokens, 5 * LANES), bf16),
        ((2, 16, tokens), f32),
        ((tokens, width), f32),
        ((tokens, width), bf16),
        ((2, 2, tokens, lanes), f32),
        ((2, tokens, lanes), bf16),
        ((tokens, width), bf16),
        ((tokens, LANES), f32),
        ((tokens, LANES), f32),
        ((1, tokens), jnp.int32),
        ((1, tokens), jnp.int32),
    ]
    full = [((2, 4, 2, 2 * rows, lanes), bf16)] * PACKS
    count = len(plan)
    outs = pl.pallas_call(
        lambda *refs: forward_kernel(plan, *refs),
        out_shape=[jax.ShapeDtypeStruct(*shape) for shape in full + saved],
        in_specs=[near] * 5 + [anywhere] * PACKS,
        out_specs=[anywhere] * (PACKS + len(saved)),
        scratch_shapes=[
            vmem((4, width, lanes), bf16),
            vmem(*saved[0]),
            vmem(*saved[1]),
            vmem(*saved[2]),
            vmem((6, keys, LANES), bf16),
            vmem((6, LANES, keys), bf16),
            vmem(*saved[3]),
            vmem(*saved[4]),
            vmem(*saved[5]),
            vmem(*saved[6]),
            vmem(*saved[7]),
            vmem(*saved[8]),
            vmem(*saved[9]),
            vmem(*saved[10]),
            vmem(*saved[11]),
            vmem(*saved[12]),
            vmem(*saved[13]),
            dma((count,)),
            dma((count, 13)),
            dma((count, 13)),
            dma((8, 2)),
            dma((len(saved),)),
            dma((2,)),
            dma((2,)),
        ],
        compiler_params=pltpu.CompilerParams(
            collective_id=1, has_side_effects=True, vmem_limit_bytes=VMEM_BYTES
        ),
        name="forward",
    )(layer_input, gains, frequency, ids, ends, *packs)
    return [part.reshape(2, 16 * rows, lanes) for part in outs[:PACKS]], outs[PACKS:]


def split_schedule(order):
    plain, looped, part = [], [[] for _ in range(4)], None
    for entry in order:
        if isinstance(entry, str) and entry[0] == "a":
            part = int(entry[1])
            if part == 0:
                plain.append("a")
        elif isinstance(entry, tuple) and part is not None and part < 4:
            looped[part].append(entry)
        else:
            part = None
            plain.append(entry)
    return plain, looped


def start(copies):
    for copy in copies:
        copy.start()


def wait(copies):
    for copy in copies:
        copy.wait()


class Scatter:
    def __init__(self, at, grad_ref, parts, sums, temps, sems, out_ref, pushes):
        self.pushes, self.ready = pushes, set()
        self.at, self.grad, self.sums, self.temps = at, grad_ref, sums, temps
        self.from_twin, self.from_far, self.from_near, self.from_line = parts
        self.sent, self.came, self.loaded, self.stored = sems
        self.out_ref = out_ref
        to_far, to_near, to_line, result = sums
        self.steps = []
        for i, (pack, cut, kind, *axes) in enumerate(SCATTER_PLAN):
            sides = Sides(at, *axes)
            lanes = result.shape[2]

            def send(src, dst, slot, device, i=i):
                return remote(src, dst, self.sent.at[i, slot], self.came.at[i, slot], device)

            self.steps.append(
                {
                    "twin": [
                        send(self.line(i, sides.twin_order[j], 1 - at.c), self.from_twin.at[i, j], j, at.twin)
                        for j in range(4)
                    ],
                    "far": [
                        send(to_far.at[i % RING, j], self.from_far.at[i, j], 4 + j, sides.far) for j in range(2)
                    ],
                    "kind": kind,
                    "near": (
                        send(to_near.at[i % RING], self.from_near.at[i], 6, sides.near)
                        if kind == 0
                        else send(to_near.at[i % RING, at.z], self.from_near.at[i, 3], 6, sides.near)
                    ),
                    "more": [
                        send(to_near.at[i % RING, at.others[k]], self.from_near.at[i, k], 10 + k, at.line[k])
                        for k in range(3 * kind)
                    ],
                    "own": [self.line(i, sides.order[j], at.c) for j in range(4)],
                    "line": [
                        send(to_line.at[i % RING, k], self.from_line.at[i, k], 7 + k, at.line[k])
                        for k in range(3)
                    ],
                    "store": pltpu.make_async_copy(
                        result.at[i % RING], out_ref.at[pack, :, pl.ds(cut * lanes, lanes)], self.stored.at[i]
                    ),
                }
            )

    def line(self, i, place, core):
        size = self.sums[3].shape[1]
        return self.grad.at[i, place[0], :, place[1], pl.ds(pl.multiple_of(core * size, 8), size)]

    def load(self, src, dst, k):
        copy = pltpu.make_async_copy(src, dst, self.loaded.at[k])
        copy.start()
        return copy

    def pushed(self, i):
        if i not in self.ready:
            self.ready.add(i)
            wait(self.pushes(i))

    def begin(self, i):
        self.pushed(i)
        for j in (1, 0, 2, 3):
            self.steps[i]["twin"][j].start()

    def first(self, i):
        step, to_far, temp, slot = self.steps[i], self.sums[0], self.temps[0], i % RING
        self.free(i, lambda old: old["far"])
        copies = []
        for j in (1, 0):
            own = self.load(step["own"][j], to_far.at[slot, j], 2 * j)
            step["twin"][j].wait_recv()
            copies.append((j, [own, self.load(self.from_twin.at[i, j], temp.at[j], 2 * j + 1)]))
        yield
        for j, pair in copies:
            wait(pair)

            def body(q, carry, j=j):
                to_far[slot, j, q] = (to_far[slot, j, q].astype(f32) + temp[j, q].astype(f32)).astype(bf16)
                return carry

            lax.fori_loop(0, 4, body, 0)
            step["far"][j].start()

    def second(self, i):
        step, to_near, temp, slot = self.steps[i], self.sums[1], self.temps[1], i % RING
        self.free(i, lambda old: [old["near"]] + old["more"])
        copies = [self.load(step["own"][2], to_near.at[slot], 4)]
        step["twin"][2].wait_recv()
        copies.append(self.load(self.from_twin.at[i, 2], temp.at[0], 5))
        step["far"][1].wait_recv()
        copies.append(self.load(self.from_far.at[i, 1], temp.at[1], 6))
        yield
        wait(copies)

        def body(q, carry):
            value = to_near[slot, q].astype(f32) + temp[0, q].astype(f32) + temp[1, q].astype(f32)
            to_near[slot, q] = value.astype(bf16)
            return carry

        lax.fori_loop(0, 4, body, 0)
        if step["kind"] == 0:
            step["near"].start()
        start(step["more"])

    def third(self, i):
        step, temp, slot = self.steps[i], self.temps[2], i % RING
        to_near, to_line, result = self.sums[1:]
        early = step["kind"] == 1
        self.free(i, lambda old: old["line"])
        if i >= RING:
            self.steps[slot]["store"].wait()
        copies = [self.load(step["own"][3], temp.at[0], 7)]
        step["twin"][3].wait_recv()
        copies.append(self.load(self.from_twin.at[i, 3], temp.at[1], 8))
        step["far"][0].wait_recv()
        copies.append(self.load(self.from_far.at[i, 0], temp.at[2], 9))
        if early:
            for copy in step["more"]:
                copy.wait_recv()
            copies.append(self.load(self.from_near.at[i, pl.ds(0, 3)], temp.at[3, pl.ds(0, 3)], 10))
        else:
            step["near"].wait_recv()
            copies.append(self.load(self.from_near.at[i], temp.at[3], 10))
        yield
        wait(copies)
        if early:
            value = to_near[slot, self.at.z].astype(f32)
            for k in range(3):
                value = value + temp[3, k].astype(f32)
            to_near[slot, self.at.z] = value.astype(bf16)
            step["near"].start()

        def total(q):
            value = (temp[0, q].astype(f32) + temp[1, q].astype(f32)) + temp[2, q].astype(f32)
            return value if early else value + temp[3, q].astype(f32)

        for k in range(3):
            to_line[slot, k] = total(self.at.others[k]).astype(bf16)
            step["line"][k].start()
        result[slot] = total(self.at.z)

    def fourth(self, i):
        step, temp, result, slot = self.steps[i], self.temps[3], self.sums[3], i % RING
        copies = []
        for k in range(3):
            step["line"][k].wait_recv()
            copies.append(self.load(self.from_line.at[i, k], temp.at[k], 11 + k))
        if step["kind"] == 1:
            step["near"].wait_recv()
            copies.append(self.load(self.from_near.at[i, 3], temp.at[3], 14))
        yield
        wait(copies)
        value = result[slot]
        for k in range(len(copies)):
            value = value + temp[k].astype(f32)
        result[slot] = value
        step["store"].start()

    def run(self, stages):
        names = {"1": self.first, "2": self.second, "3": self.third, "4": self.fourth}
        turn = []

        def flush():
            works = [names[name](i) for name, i in turn]
            for work in works:
                next(work)
            for work in works:
                next(work, None)
            turn.clear()

        for name, i in stages:
            if name == "B":
                self.begin(i)
            else:
                if any(name == held or (name > held and i == j) or i == j + RING for held, j in turn):
                    flush()
                turn.append((name, i))
        flush()

    def free(self, i, sends):
        if i >= RING:
            for copy in sends(self.steps[i - RING]):
                copy.wait_send()

    def finish(self):
        for i, step in enumerate(self.steps):
            for copy in step["twin"]:
                copy.wait_send()
            if i + RING >= len(self.steps):
                for copy in step["far"] + [step["near"]] + step["more"] + step["line"]:
                    copy.wait_send()
                step["store"].wait()


def flip_rows(src, dst):
    for tile in range(src.shape[1] // LANES):
        cols = pl.ds(tile * LANES, LANES)
        dst[cols, :] = src[:, cols].astype(f32).T.astype(bf16)


def backward_kernel(*refs):
    grad_out_ref, x_ref, gain_ref, cos_ref, sin_ref, first_ref, last_ref = refs[:7]
    full_refs, kept = refs[7:11], refs[11:20]
    gain_one_ref, gain_two_ref = gain_ref.at[pl.ds(0, 1)], gain_ref.at[pl.ds(1, 1)]
    attn_in_ref, y_ref, kv_ref, mix_ref, logs_ref, residual_ref, mlp_in_ref, acts_ref, hidden_ref = kept
    sum_ref, grad_in_ref, gain_sum_ref, grad_ref = refs[20:24]
    parts = refs[24:28]
    scratch = refs[28:]
    sums, temps = scratch[:4], scratch[4:8]
    staging, grad_res, branch, kv_out, kv_in, gains = scratch[8:14]
    sems, pulled, pushed, kv_sent, kv_came, gain_sent, gain_came = scratch[14:18], *scratch[18:24]
    at = Place()
    at.greet()
    dma = pltpu.SemaphoreType.DMA
    vmem = pltpu.VMEM
    tokens, width = grad_res.shape
    lanes = hidden_ref.shape[2]
    size = lanes // 2
    tiles = size // 256

    def pull(src, dst, k):
        return pltpu.make_async_copy(src, dst, pulled.at[k])

    def pull_cut(pack, cut, dst, k):
        return [
            pull(
                full_refs[pack].at[half].reshape(width, lanes).at[:, pl.ds(cut * size, size)],
                dst.at[:, pl.ds(half * size, size)],
                k + half,
            )
            for half in range(2)
        ]

    def push(i):
        slot = i % 2
        return [
            pltpu.make_async_copy(
                staging.at[slot, half], grad_ref.at[i, half].reshape(width, size), pushed.at[slot, half]
            )
            for half in range(2)
        ]

    scatter = Scatter(at, grad_ref, parts, sums, temps, sems, sum_ref, push)
    plain, looped = split_schedule(BACKWARD_ORDER)
    first_end, second_end, third_end = (plain.index(name) for name in ("norm", "mx", "in"))

    def follow(entries, work):
        moves = []
        for entry in entries:
            if isinstance(entry, tuple):
                moves.append(entry)
            else:
                scatter.run(moves)
                moves = []
                work[entry]()
        scatter.run(moves)

    def weight_grad(i, left, right):
        def body(k, carry):
            half, cols = k // tiles, pl.ds(pl.multiple_of((k % tiles) * 256, 256), 256)
            staging[i % 2, half, :, cols] = dot_nn(left[...], right[half, :, cols]).astype(bf16)
            return carry

        if i >= 2:
            scatter.pushed(i - 2)
        lax.fori_loop(0, 2 * tiles, body, 0)
        start(push(i))

    def feed_forward(weights, acts, hidden, grad_out, out_turned, in_turned, grad_acts):
        def pulls(cut):
            cols = pl.ds(cut * size, size)
            return {
                "hidden": [pull(hidden_ref.at[:, :, cols], hidden, 0)],
                "down": pull_cut(3, cut, weights.at[0], 1),
                "acts": [pull(acts_ref.at[:, :, :, cols], acts, 3)],
                "gate": pull_cut(1, cut, weights.at[1], 4) + pull_cut(2, cut, weights.at[2], 6),
            }

        cuts = [pulls(0), pulls(1)]
        given = [pull(grad_out_ref, grad_out, 8), pull(mlp_in_ref, branch, 9)]

        def load():
            copies = cuts[0]
            start(given + copies["hidden"] + copies["down"] + copies["acts"] + copies["gate"])
            wait(given)
            flip_rows(grad_out, out_turned)
            flip_rows(branch, in_turned)

        def down_grad(cut):
            wait(cuts[cut]["hidden"])
            weight_grad(3 * cut, out_turned, hidden)
            if cut == 0:
                start(cuts[1]["hidden"])

        def act_grad(cut):
            wait(cuts[cut]["down"] + cuts[cut]["acts"])

            def tile_of(k, carry):
                half, tile = k // tiles, k % tiles
                cols = pl.ds(pl.multiple_of(tile * 256, 256), 256)
                grad = dot_nn(grad_out[...], weights[0, :, pl.ds(pl.multiple_of(k * 256, 256), 256)])
                gate, up = acts[half, 0, :, cols], acts[half, 1, :, cols]
                sigmoid = jax.nn.sigmoid(gate)
                grad_acts[0, half, :, cols] = (
                    grad * up * sigmoid * (1.0 + gate * (1.0 - sigmoid))
                ).astype(bf16)
                grad_acts[1, half, :, cols] = (grad * gate * sigmoid).astype(bf16)
                return carry

            lax.fori_loop(0, 2 * tiles, tile_of, 0)
            if cut == 0:
                start(cuts[1]["down"] + cuts[1]["acts"])

        def input_grad(cut):
            wait(cuts[cut]["gate"])

            def rows_of(k, carry):
                rows = pl.ds(pl.multiple_of(k * 256, 256), 256)
                total = None if cut == 0 else grad_res[rows, :]
                for half in range(2):
                    for part in range(2):
                        term = dot_nt(
                            grad_acts[part, half, rows, :], weights[1 + part, :, pl.ds(half * size, size)]
                        )
                        total = term if total is None else total + term
                grad_res[rows, :] = total
                return carry

            lax.fori_loop(0, tokens // 256, rows_of, 0)
            if cut == 0:
                start(cuts[1]["gate"])

        work = {"ld": load}
        for cut in range(2):
            work["w" + str(3 * cut)] = lambda cut=cut: down_grad(cut)
            work["d" + str(cut)] = lambda cut=cut: act_grad(cut)
            work["w" + str(3 * cut + 1)] = lambda cut=cut: weight_grad(3 * cut + 1, in_turned, grad_acts.at[0])
            work["w" + str(3 * cut + 2)] = lambda cut=cut: weight_grad(3 * cut + 2, in_turned, grad_acts.at[1])
            work["m" + str(cut)] = lambda cut=cut: input_grad(cut)
        follow(plain[:first_end], work)

    pl.run_scoped(
        feed_forward,
        vmem((3, width, lanes), bf16),
        vmem((2, 2, tokens, size), f32),
        vmem((2, tokens, size), bf16),
        vmem((tokens, width), bf16),
        vmem((width, tokens), bf16),
        vmem((width, tokens), bf16),
        vmem((2, 2, tokens, size), bf16),
    )
    def second_norm(residual, grad_out):
        copies = [pull(residual_ref, residual, 0), pull(grad_out_ref, grad_out, 1)]
        start(copies)
        wait(copies)
        gain = gain_two_ref[...]

        def rows_of(k, carry):
            rows = pl.ds(pl.multiple_of(k * 128, 128), 128)
            value, grad = residual[rows, :], grad_res[rows, :]
            inverse = lax.rsqrt(jnp.mean(value * value, axis=1, keepdims=True) + eps)
            normed = value * inverse
            scaled = grad * gain
            inner = jnp.mean(scaled * normed, axis=1, keepdims=True)
            total = grad_out[rows, :].astype(f32) + inverse * (scaled - normed * inner)
            grad_res[rows, :] = total
            branch[rows, :] = total.astype(bf16)
            return carry + jnp.sum(grad * normed, axis=0, keepdims=True)

        gains[0, pl.ds(1, 1), :] = lax.fori_loop(0, tokens // 128, rows_of, jnp.zeros((1, width), f32))

    gains[0] = jnp.zeros(gains.shape[1:], f32)
    pl.run_scoped(second_norm, vmem((tokens, width), f32), vmem((tokens, width), bf16))
    follow(plain[first_end + 1 : second_end], {})

    def attention(weights, y, kv, dup, flip, acc, mix, grad_mix, grad_y, turned, logs, grad_kv, held):
        copies = [
            pull(full_refs[0].at[half].reshape(width, lanes), weights.at[half], half) for half in range(2)
        ] + [
            pull(y_ref, y, 2),
            pull(kv_ref, kv, 3),
            pull(mix_ref, mix, 4),
            pull(logs_ref, logs, 5),
            pull(attn_in_ref, held, 6),
        ]
        def mix_grad():
            start(copies)
            wait(copies[:2])

            def rows_of(k, carry):
                half, rows = k // 2, pl.ds(pl.multiple_of((k % 2) * 256, 256), 256)
                grad_mix[half, rows, :] = dot_nn(
                    branch[rows, :], weights[half, :, pl.ds(7 * LANES, 5 * LANES)]
                ).astype(bf16)
                return carry

            lax.fori_loop(0, 4, rows_of, 0)
            wait(copies[2:])

        mine = pl.ds(pl.multiple_of(at.x * tokens, tokens), tokens)
        other = pl.ds(pl.multiple_of((1 - at.x) * tokens, tokens), tokens)
        block = 256
        steps = tokens // block

        def send_kv(half):
            return remote(kv_out.at[half], kv_in.at[half], kv_sent.at[half], kv_came.at[half], at.cross)

        def attend_back_all():
            def rows_of(i, carry):
                half = i // steps

                @pl.when(i % steps == 0)
                def _():
                    load_groups(kv, half, dup, flip)
                    acc[...] = jnp.zeros_like(acc)

                attend_back_rows(
                    half, i % steps, block, y, dup, flip, first_ref, last_ref, logs, grad_mix, cos_ref, sin_ref, grad_y, acc
                )

                @pl.when(i % steps == steps - 1)
                def _():
                    join_groups(acc, grad_kv, half)
                    kv_out[half] = grad_kv[half, other, :].astype(bf16)

                for k in range(2):

                    @pl.when(i == (k + 1) * steps - 1)
                    def _(k=k):
                        send_kv(k).start()

                for k, part in enumerate(looped):
                    if part:

                        @pl.when(i == k * steps // 2)
                        def _(part=part):
                            scatter.run(part)

                return carry

            lax.fori_loop(0, 2 * steps, rows_of, 0)

        def late_part():
            scatter.pushed(4)
            flip_rows(held, turned.at[0])
            flip_rows(branch, turned.at[1])
            for half in range(2):
                tail = dot_nn(turned[0], grad_y[half, :, pl.ds(6 * LANES, 2 * LANES)])
                head = dot_nn(turned[1], mix[half, :, pl.ds(0, LANES)])
                staging[0, half, :, pl.ds(0, LANES)] = tail[:, :LANES].astype(bf16)
                staging[0, half, :, pl.ds(LANES, LANES)] = (tail[:, LANES:] + head).astype(bf16)
                for k in range(2):
                    staging[0, half, :, pl.ds((2 + 2 * k) * LANES, 2 * LANES)] = dot_nn(
                        turned[1], mix[half, :, pl.ds((1 + 2 * k) * LANES, 2 * LANES)]
                    ).astype(bf16)
            start(push(6))
            load_x.start()

        def join_keys():
            lane = lane_of((tokens, LANES))
            lower = lane % HEAD < HEAD // 2
            for half in range(2):
                send_kv(half).wait()
                for tile in range(3):
                    cols = pl.ds(tile * LANES, LANES)
                    total = grad_kv[half, mine, cols] + kv_in[half, :, cols].astype(f32)
                    if tile < 2:
                        back = turn_back(total, cos_ref[...], sin_ref[...], lower)
                        total = back if tile == 0 else jnp.where(lane < HEAD, back, total)
                    grad_y[half, :, cols] = total.astype(bf16)

        def input_rows():
            load_x.wait()
            gain = gain_one_ref[...]

            def rows_of(k, carry):
                rows = pl.ds(pl.multiple_of(k * 128, 128), 128)
                grad = dot_nt(grad_y[0, rows, :], weights[0, :, pl.ds(0, 8 * LANES)]) + dot_nt(
                    grad_y[1, rows, :], weights[1, :, pl.ds(0, 8 * LANES)]
                )
                value = held[rows, :].astype(f32)
                inverse = lax.rsqrt(jnp.mean(value * value, axis=1, keepdims=True) + eps)
                normed = value * inverse
                scaled = grad * gain
                inner = jnp.mean(scaled * normed, axis=1, keepdims=True)
                branch[rows, :] = (grad_res[rows, :] + inverse * (scaled - normed * inner)).astype(bf16)
                return carry + jnp.sum(grad * normed, axis=0, keepdims=True)

            gains[0, pl.ds(0, 1), :] = lax.fori_loop(0, tokens // 128, rows_of, jnp.zeros((1, width), f32))

        load_x = pull(x_ref, held, 6)
        follow(
            plain[second_end : third_end + 1],
            {
                "mx": mix_grad,
                "a": attend_back_all,
                "g1": late_part,
                "kvw": join_keys,
                "g0": lambda: weight_grad(7, turned.at[0], grad_y),
                "in": input_rows,
            },
        )

    keys = kv_ref.shape[1]
    pl.run_scoped(
        attention,
        vmem((2, width, lanes), bf16),
        vmem(y_ref.shape, bf16),
        vmem(kv_ref.shape, bf16),
        vmem((6, keys, LANES), bf16),
        vmem((6, LANES, keys), bf16),
        vmem((6, keys, LANES), f32),
        vmem(mix_ref.shape, bf16),
        vmem(mix_ref.shape, bf16),
        vmem(y_ref.shape, bf16),
        vmem((2, width, tokens), bf16),
        vmem(logs_ref.shape, f32),
        vmem((2, keys, 3 * LANES), f32),
        vmem((tokens, width), bf16),
    )
    out = pull(branch, grad_in_ref, 0)
    out.start()
    exchanges = [
        remote(gains.at[2 * k], gains.at[2 * k + 1], gain_sent.at[k], gain_came.at[k], peer)
        for k, peer in enumerate([at.twin, at.near, at.far])
    ]
    everyone = [
        remote(gains.at[6 + at.z], gains.at[6 + at.z], gain_sent.at[3 + k], gain_came.at[3 + k], at.line[k])
        for k in range(3)
    ]

    def fold(k):
        exchanges[k].wait()
        gains[6 + at.z if k == 2 else 2 * (k + 1)] = gains[2 * k] + gains[2 * k + 1]

    rest = plain[third_end + 1 :]
    share = -(-len(rest) // 4)
    for k in range(4):
        if k < 3:
            exchanges[k].start()
        else:
            start(everyone)
        follow(rest[k * share : (k + 1) * share], {})
        if k < 3:
            fold(k)
    wait(everyone)
    gain_sum_ref[...] = gains[6] + gains[7] + gains[8] + gains[9]
    out.wait()
    scatter.finish()


def backward_special(grad_output, layer_input, gains, cosine, sine, first, last, packs, kept):
    tokens, width = layer_input.shape
    _, depth, lanes = packs[0].shape
    rows, size = depth // 16, lanes // 2
    count = len(SCATTER_PLAN)
    dma, vmem = pltpu.SemaphoreType.DMA, pltpu.VMEM
    anywhere = pl.BlockSpec(memory_space=pl.ANY)
    near = pl.BlockSpec(memory_space=pltpu.VMEM)
    shape = jax.ShapeDtypeStruct
    outs = pl.pallas_call(
        backward_kernel,
        out_shape=[
            shape((PACKS, rows, lanes), f32),
            shape((tokens, width), bf16),
            shape((8, width), f32),
            shape((count, 2, 4, 2, 2 * rows, size), bf16),
            shape((count, 4, 4, rows, size), bf16),
            shape((count, 2, 4, rows, size), bf16),
            shape((count, 4, rows, size), bf16),
            shape((count, 3, rows, size), bf16),
        ],
        in_specs=[anywhere] * 2 + [near] * 5 + [anywhere] * (PACKS + len(kept)),
        out_specs=[anywhere, anywhere, near] + [anywhere] * 5,
        scratch_shapes=[
            vmem((RING, 2, 4, rows, size), bf16),
            vmem((RING, 4, rows, size), bf16),
            vmem((RING, 3, rows, size), bf16),
            vmem((RING, rows, size), f32),
            vmem((2, 4, rows, size), bf16),
            vmem((2, 4, rows, size), bf16),
            vmem((4, 4, rows, size), bf16),
            vmem((4, rows, size), bf16),
            vmem((2, 2, width, size), bf16),
            vmem((tokens, width), f32),
            vmem((tokens, width), bf16),
            vmem((2, tokens, 3 * LANES), bf16),
            vmem((2, tokens, 3 * LANES), bf16),
            vmem((10, 8, width), f32),
            dma((count, 13)),
            dma((count, 13)),
            dma((15,)),
            dma((count,)),
            dma((10,)),
            dma((2, 2)),
            dma((2,)),
            dma((2,)),
            dma((6,)),
            dma((6,)),
        ],
        compiler_params=pltpu.CompilerParams(
            collective_id=2, has_side_effects=True, vmem_limit_bytes=VMEM_BYTES
        ),
        name="backward",
    )(
        grad_output,
        layer_input,
        gains,
        cosine,
        sine,
        first,
        last,
        *[pack.reshape(2, 4, 2, 2 * rows, lanes) for pack in packs],
        *kept,
    )
    sums, grad_input, gain_sums = outs[:3]
    kv = lanes // 8
    mixed = sums[0]
    return (
        grad_input,
        gain_sums[:2],
        (
            mixed[:, 2 * kv : 5 * kv],
            mixed[:, :kv],
            mixed[:, kv : 2 * kv],
            mixed[:, 5 * kv :].T,
            sums[1],
            sums[2],
            sums[3].T,
        ),
    )


def special():
    return (lax.axis_size("row"), lax.axis_size("col")) == (16, 2)


def lane_of(shape):
    return lax.broadcasted_iota(jnp.int32, shape, len(shape) - 1)


def turn(values, cosine, sine, lower):
    ahead = pltpu.roll(values, LANES - HEAD // 2, 1)
    behind = pltpu.roll(values, HEAD // 2, 1)
    return values * cosine + jnp.where(lower, -ahead, behind) * sine


def turn_back(values, cosine, sine, lower):
    scaled = values * sine
    ahead = pltpu.roll(scaled, LANES - HEAD // 2, 1)
    behind = pltpu.roll(scaled, HEAD // 2, 1)
    return values * cosine - jnp.where(lower, -ahead, behind)


def project_tiles(half, pairs, attn_in_ref, weight_ref, cos_ref, sin_ref, y_ref):
    cosine, sine = cos_ref[...], sin_ref[...]
    lane = lane_of(cosine.shape)
    lower = lane % HEAD < HEAD // 2
    for pair in pairs:
        two = dot_nn(attn_in_ref[...], weight_ref[half, :, pl.ds(pair * 2 * LANES, 2 * LANES)]).astype(bf16)
        for side in range(2):
            tile = 2 * pair + side
            raw = two[:, side * LANES : (side + 1) * LANES].astype(f32)
            if tile == 2:
                out = raw
            else:
                out = turn(raw, cosine, sine, lower)
                if tile == 1:
                    out = jnp.where(lane < HEAD, out, raw)
                elif tile > 2:
                    out = out * HEAD ** (-0.5)
            y_ref[half, :, pl.ds(tile * LANES, LANES)] = out.astype(bf16)


def project_kernel(x_ref, gain_ref, weight_ref, cos_ref, sin_ref, attn_in_ref, y_ref):
    values = x_ref[...].astype(f32)
    inverse = lax.rsqrt(jnp.mean(values * values, axis=1, keepdims=True) + eps)
    attn_in_ref[...] = (values * inverse * gain_ref[...]).astype(bf16)
    for half in range(2):
        project_tiles(half, range(4), attn_in_ref, weight_ref, cos_ref, sin_ref, y_ref)


def head_rows(values, side, lane):
    return jnp.where((lane < HEAD) if side == 0 else (lane >= HEAD), values, jnp.zeros_like(values))


def twice(tile, side, lane):
    values = tile.astype(f32)
    other = pltpu.roll(values, HEAD, 1)
    keep = (lane < HEAD) if side == 0 else (lane >= HEAD)
    return jnp.where(keep, values, other)


def load_groups(kv_ref, half, dup_ref, flip_ref):
    for slot in range(6):
        tile = kv_ref[half, :, pl.ds((slot // 2) * LANES, LANES)]
        both = twice(tile, slot % 2, lane_of(tile.shape))
        dup_ref[slot] = both.astype(bf16)
        flip_ref[slot] = both.T.astype(bf16)


def seen(first_ref, last_ref, rows, keys):
    index = lax.broadcasted_iota(jnp.int32, (keys, rows.size), 0)
    return (index >= first_ref[:, rows]) & (index <= last_ref[:, rows])


def attend_rows(half, step, block, y_ref, dup_ref, flip_ref, first_ref, last_ref, mix_ref, log_ref):
    keys = dup_ref.shape[1]
    lane = lane_of((block, LANES))
    rows = pl.ds(pl.multiple_of(step * block, block), block)
    allowed = seen(first_ref, last_ref, rows, keys)
    previous = jnp.zeros((block, LANES), f32)
    for head in range(9):
        group = head // 3
        query = head_rows(y_ref[half, rows, pl.ds((3 + head // 2) * LANES, LANES)], head % 2, lane)
        scores = jnp.where(allowed, dot_nt(dup_ref[group], query), neg_fill)
        top = jnp.max(scores, axis=0, keepdims=True)
        powers = jnp.exp(scores - top)
        total = jnp.sum(powers, axis=0, keepdims=True)
        probs = (powers * (1.0 / total)).astype(bf16)
        mixed = dot_nn(flip_ref[3 + group], probs).T
        log_ref[half, pl.ds(head, 1), rows] = top + jnp.log(total)
        if head % 2 == 0:
            tile = jnp.where(lane < HEAD, previous, mixed)
            mix_ref[half, rows, pl.ds((head // 2) * LANES, LANES)] = tile.astype(bf16)
        previous = mixed


def attend_kernel(block, y_ref, kv_ref, first_ref, last_ref, mix_ref, log_ref, dup_ref, flip_ref):
    load_groups(kv_ref, 0, dup_ref, flip_ref)

    def rows_of(step, carry):
        attend_rows(0, step, block, y_ref, dup_ref, flip_ref, first_ref, last_ref, mix_ref, log_ref)
        return carry

    lax.fori_loop(0, y_ref.shape[1] // block, rows_of, 0)


def attend_back_rows(
    half, step, block, y_ref, dup_ref, flip_ref, first_ref, last_ref, log_ref, grad_ref, cos_ref, sin_ref, out_ref, acc_ref
):
    keys = dup_ref.shape[1]
    lane = lane_of((block, LANES))
    lower = lane % HEAD < HEAD // 2
    rows = pl.ds(pl.multiple_of(step * block, block), block)
    allowed = seen(first_ref, last_ref, rows, keys)
    previous = None
    for head in range(9):
        group = head // 3
        query = head_rows(y_ref[half, rows, pl.ds((3 + head // 2) * LANES, LANES)], head % 2, lane)
        upstream = head_rows(
            grad_ref[half, rows, pl.ds(((head + 1) // 2) * LANES, LANES)], (head + 1) % 2, lane
        )
        scores = jnp.where(allowed, dot_nt(dup_ref[group], query), neg_fill)
        probs = jnp.exp(scores - log_ref[half, pl.ds(head, 1), rows])
        grad_probs = dot_nt(dup_ref[3 + group], upstream)
        inner = jnp.sum(probs * grad_probs, axis=0, keepdims=True)
        grad_scores = (probs * (grad_probs - inner)).astype(bf16)
        acc_ref[3 + group] += dot_nn(probs.astype(bf16), upstream)
        acc_ref[group] += dot_nn(grad_scores, query)
        grad_query = dot_nn(flip_ref[group], grad_scores).T
        if head % 2 == 1 or head == 8:
            if head == 8:
                tile = jnp.where(lane < HEAD, grad_query, 0.0)
            else:
                tile = jnp.where(lane < HEAD, previous, grad_query)
            tile = turn_back(tile * HEAD ** (-0.5), cos_ref[rows, :], sin_ref[rows, :], lower)
            out_ref[half, rows, pl.ds((3 + head // 2) * LANES, LANES)] = tile.astype(bf16)
        previous = grad_query


def join_groups(acc_ref, out_ref, half):
    lane = lane_of((acc_ref.shape[1], LANES))
    for tile in range(3):
        low, high = acc_ref[2 * tile], acc_ref[2 * tile + 1]
        low = low + pltpu.roll(low, HEAD, 1)
        high = high + pltpu.roll(high, HEAD, 1)
        out_ref[half, :, pl.ds(tile * LANES, LANES)] = jnp.where(lane < HEAD, low, high)


def attend_back_kernel(
    block, y_ref, kv_ref, first_ref, last_ref, log_ref, grad_ref, cos_ref, sin_ref, dq_ref, dkv_ref, dup_ref, flip_ref, acc_ref
):
    load_groups(kv_ref, 0, dup_ref, flip_ref)
    acc_ref[...] = jnp.zeros_like(acc_ref)

    def rows_of(step, carry):
        attend_back_rows(
            0, step, block, y_ref, dup_ref, flip_ref, first_ref, last_ref, log_ref, grad_ref, cos_ref, sin_ref, dq_ref, acc_ref
        )
        return carry

    lax.fori_loop(0, y_ref.shape[1] // block, rows_of, 0)
    join_groups(acc_ref, dkv_ref, 0)


def full_spec(shape):
    return pl.BlockSpec(shape, lambda i: (0,) * len(shape))


def half_spec(shape):
    return pl.BlockSpec((1,) + shape[1:], lambda i: (i,) + (0,) * (len(shape) - 1))


def params():
    return pltpu.CompilerParams(vmem_limit_bytes=VMEM_BYTES)


def project(layer_input, gain, first_pack, cosine, sine):
    tokens, width = layer_input.shape
    vm = pl.BlockSpec(memory_space=pltpu.VMEM)
    return pl.pallas_call(
        project_kernel,
        grid=(1,),
        out_shape=(
            jax.ShapeDtypeStruct((tokens, width), bf16),
            jax.ShapeDtypeStruct((2, tokens, 8 * LANES), bf16),
        ),
        in_specs=[
            full_spec((tokens, width)),
            full_spec((1, width)),
            full_spec((2, width, 8 * LANES)),
            full_spec((tokens, LANES)),
            full_spec((tokens, LANES)),
        ],
        out_specs=(full_spec((tokens, width)), full_spec((2, tokens, 8 * LANES))),
        compiler_params=params(),
        name="project",
    )(layer_input, gain, first_pack, cosine, sine)


def attend(y, kv, first, last):
    tokens, keys = y.shape[1], kv.shape[1]
    block = min(256, tokens)
    return pl.pallas_call(
        lambda *refs: attend_kernel(block, *refs),
        grid=(2,),
        out_shape=(
            jax.ShapeDtypeStruct((2, tokens, 5 * LANES), bf16),
            jax.ShapeDtypeStruct((2, 16, tokens), f32),
        ),
        in_specs=[half_spec(y.shape), half_spec(kv.shape), full_spec((1, tokens)), full_spec((1, tokens))],
        out_specs=(half_spec((2, tokens, 5 * LANES)), half_spec((2, 16, tokens))),
        scratch_shapes=[pltpu.VMEM((6, keys, LANES), bf16), pltpu.VMEM((6, LANES, keys), bf16)],
        compiler_params=params(),
        name="attend",
    )(y, kv, first, last)


def attend_back(y, kv, first, last, logs, grad, cosine, sine):
    tokens, keys = y.shape[1], kv.shape[1]
    block = min(256, tokens)
    return pl.pallas_call(
        lambda *refs: attend_back_kernel(block, *refs),
        grid=(2,),
        out_shape=(
            jax.ShapeDtypeStruct((2, tokens, 8 * LANES), bf16),
            jax.ShapeDtypeStruct((2, keys, 3 * LANES), f32),
        ),
        in_specs=[
            half_spec(y.shape),
            half_spec(kv.shape),
            full_spec((1, tokens)),
            full_spec((1, tokens)),
            half_spec(logs.shape),
            half_spec(grad.shape),
            full_spec((tokens, LANES)),
            full_spec((tokens, LANES)),
        ],
        out_specs=(half_spec((2, tokens, 8 * LANES)), half_spec((2, keys, 3 * LANES))),
        scratch_shapes=[
            pltpu.VMEM((6, keys, LANES), bf16),
            pltpu.VMEM((6, LANES, keys), bf16),
            pltpu.VMEM((6, keys, LANES), f32),
        ],
        compiler_params=params(),
        name="attend_back",
    )(y, kv, first, last, logs, grad, cosine, sine)


def rope_frequency():
    lane_index = (jnp.arange(LANES, dtype=jnp.int32) % (HEAD // 2)).astype(f32)
    return jnp.exp(lane_index * (-2.0 * math.log(rope_base) / HEAD))


def shards(
    layer_input,
    attn_gain,
    mlp_gain,
    query_weight,
    key_weight,
    value_weight,
    out_weight,
    gate_weight,
    up_weight,
    down_weight,
    seq_ids,
    block_ends,
    grad_output,
):
    tokens, width = layer_input.shape
    span = seq_ids.shape[0]
    start = lax.axis_index("col") * tokens
    gains = jnp.stack([attn_gain, mlp_gain]).astype(f32)
    weights = (query_weight, key_weight, value_weight, out_weight, gate_weight, up_weight, down_weight)
    if special():
        mine = jnp.concatenate([key_weight, value_weight, query_weight, out_weight.T], axis=1)
        packs, kept = forward_special(
            layer_input,
            gains,
            rope_frequency()[None, :],
            seq_ids[None, :],
            block_ends[None, :],
            (mine, gate_weight, up_weight, down_weight.T),
        )
        grad_input, gain_sums, weight_sums = backward_special(
            grad_output, layer_input, gains, *kept[10:], packs, kept[:9]
        )
        return (kept[9], grad_input, gain_sums[0], gain_sums[1]) + tuple(weight_sums)
    own = layer_input.astype(f32)
    gain_one, gain_two = gains[:1], gains[1:]
    index = start + jnp.arange(tokens, dtype=jnp.int32)
    length = jnp.sum(1 - (seq_ids & 1))
    own_first = jnp.where(index < length, 0, length)
    own_last = lax.dynamic_slice_in_dim(block_ends, start, tokens) - lax.axis_index("row") * span
    angles = (index - own_first).astype(f32)[:, None] * rope_frequency()[None, :]
    cosine, sine = jnp.cos(angles), jnp.sin(angles)
    own_first, own_last = own_first[None, :], own_last[None, :]
    pack_first, pack_gate, pack_up, pack_down = gather_any(weights)
    attn_in, y = project(layer_input, gain_one, pack_first, cosine, sine)
    kv = lax.all_gather(y[:, :, : 3 * LANES], "col", axis=1, tiled=True)
    mix, logs = attend(y, kv, own_first, own_last)
    pack_out = pack_first[:, :, 7 * LANES :]
    branch = jnp.einsum("htq,hdq->td", mix, pack_out, preferred_element_type=f32)
    residual = own + branch
    inv_two = lax.rsqrt(jnp.mean(residual * residual, axis=1, keepdims=True) + eps)
    normed_two = residual * inv_two
    mlp_in = (normed_two * gain_two).astype(bf16)
    gate_act = jnp.einsum("td,hdf->htf", mlp_in, pack_gate, preferred_element_type=f32)
    up_act = jnp.einsum("td,hdf->htf", mlp_in, pack_up, preferred_element_type=f32)
    hidden = (jax.nn.silu(gate_act) * up_act).astype(bf16)
    layer_output = (
        residual + jnp.einsum("htf,hdf->td", hidden, pack_down, preferred_element_type=f32)
    ).astype(bf16)
    grad_down = jnp.einsum("td,htf->hdf", grad_output, hidden, preferred_element_type=f32).astype(bf16)
    grad_hidden = jnp.einsum("td,hdf->htf", grad_output, pack_down, preferred_element_type=f32)
    sigmoid = jax.nn.sigmoid(gate_act)
    grad_gate_act = (grad_hidden * up_act * sigmoid * (1.0 + gate_act * (1.0 - sigmoid))).astype(bf16)
    grad_up_act = (grad_hidden * gate_act * sigmoid).astype(bf16)
    grad_gate = jnp.einsum("td,htf->hdf", mlp_in, grad_gate_act, preferred_element_type=f32).astype(bf16)
    grad_up = jnp.einsum("td,htf->hdf", mlp_in, grad_up_act, preferred_element_type=f32).astype(bf16)
    grad_mlp_in = jnp.einsum(
        "htf,hdf->td", grad_gate_act, pack_gate, preferred_element_type=f32
    ) + jnp.einsum("htf,hdf->td", grad_up_act, pack_up, preferred_element_type=f32)
    scaled_two = grad_mlp_in * gain_two
    inner_two = jnp.mean(scaled_two * normed_two, axis=1, keepdims=True)
    grad_residual = grad_output.astype(f32) + inv_two * (scaled_two - normed_two * inner_two)
    grad_mlp_gain = jnp.sum(grad_mlp_in * normed_two, axis=0)
    grad_branch = grad_residual.astype(bf16)
    grad_mixture = jnp.einsum("td,hdq->htq", grad_branch, pack_out, preferred_element_type=f32).astype(bf16)
    grad_q, grad_kv = attend_back(y, kv, own_first, own_last, logs, grad_mixture, cosine, sine)
    grad_kv = lax.psum_scatter(grad_kv, "col", scatter_dimension=1, tiled=True)
    key_cos, key_sin = jnp.tile(cosine, (1, 3)), jnp.tile(sine, (1, 3))
    lane = jnp.arange(3 * LANES, dtype=jnp.int32)
    is_key = lane < 3 * HEAD
    scaled = grad_kv * key_sin
    turned = jnp.where(
        lane % HEAD < HEAD // 2, -jnp.roll(scaled, -(HEAD // 2), axis=2), jnp.roll(scaled, HEAD // 2, axis=2)
    )
    grad_kv = jnp.where(is_key, grad_kv * key_cos - turned, grad_kv).astype(bf16)
    grad_y = jnp.concatenate([grad_kv, grad_q[:, :, 3 * LANES :]], axis=2)
    grad_proj = jnp.einsum("td,htf->hdf", attn_in, grad_y, preferred_element_type=f32)
    grad_out = jnp.einsum("td,htq->hdq", grad_branch, mix, preferred_element_type=f32)
    grad_first = jnp.concatenate(
        [
            grad_proj[:, :, : 7 * LANES],
            grad_proj[:, :, 7 * LANES :] + grad_out[:, :, :LANES],
            grad_out[:, :, LANES:],
        ],
        axis=2,
    ).astype(bf16)
    grad_attn_in = jnp.einsum(
        "htf,hdf->td", grad_y, pack_first[:, :, : 8 * LANES], preferred_element_type=f32
    )
    inv_one = lax.rsqrt(jnp.mean(own * own, axis=1, keepdims=True) + eps)
    normed_one = own * inv_one
    scaled_one = grad_attn_in * gain_one
    inner_one = jnp.mean(scaled_one * normed_one, axis=1, keepdims=True)
    grad_input = (grad_residual + inv_one * (scaled_one - normed_one * inner_one)).astype(bf16)
    grad_attn_gain = jnp.sum(grad_attn_in * normed_one, axis=0)
    gain_sums, weight_sums = scatter_any(
        (grad_first, grad_gate, grad_up, grad_down), jnp.stack([grad_attn_gain, grad_mlp_gain])
    )
    return (layer_output, grad_input, gain_sums[0], gain_sums[1]) + tuple(weight_sums)


def solution(mesh):
    tokens_spec = P(("row", "col"), None)
    in_specs = (
        tokens_spec,
        P(),
        P(),
        P("row", "col"),
        P("row", "col"),
        P("row", "col"),
        P("col", "row"),
        P("row", "col"),
        P("row", "col"),
        P("col", "row"),
        P("row"),
        P("row"),
        tokens_spec,
    )
    out_specs = (
        tokens_spec,
        tokens_spec,
        P(),
        P(),
        P("row", "col"),
        P("row", "col"),
        P("row", "col"),
        P("col", "row"),
        P("row", "col"),
        P("row", "col"),
        P("col", "row"),
    )
    return jax.shard_map(shards, mesh=mesh, in_specs=in_specs, out_specs=out_specs, check_vma=False)
```

```python
import math

import jax
import jax.numpy as jnp
from jax import lax
from jax.experimental import pallas as pl
from jax.experimental.pallas import tpu as pltpu
from jax.sharding import PartitionSpec as P

HEAD = 64
LANES = 128
eps = 1e-05
rope_base = 10000.0
neg_fill = -1e30
f32 = jnp.float32
bf16 = jnp.bfloat16
VMEM_BYTES = 62 * 1024 * 1024


def dot_nn(a, b):
    return lax.dot_general(a, b, (((1,), (0,)), ((), ())), preferred_element_type=f32)


def dot_nt(a, b):
    return lax.dot_general(a, b, (((1,), (1,)), ((), ())), preferred_element_type=f32)


def halves(values):
    rows, cols = values.shape
    return jnp.transpose(values.reshape(rows, 2, cols // 2), (1, 0, 2))


def whole(values):
    two, rows, cols = values.shape
    return jnp.transpose(values, (1, 0, 2)).reshape(rows, two * cols)


def gather_any(weights):
    query, key, value, out, gate, up, down = weights

    def both(weight, row_axis):
        part = lax.all_gather(weight, "row", axis=row_axis, tiled=True)
        return lax.all_gather(part, "col", axis=1 - row_axis, tiled=True)

    mix = [halves(both(key, 0)), halves(both(value, 0)), halves(both(query, 0)), halves(both(out, 1).T)]
    return [
        jnp.concatenate(mix, axis=2),
        halves(both(gate, 0)),
        halves(both(up, 0)),
        halves(both(down, 1).T),
    ]


def scatter_any(grads, gains):
    first, gate, up, down = [grad.astype(f32) for grad in grads]
    kv = first.shape[2] // 8
    key, value, query, out = (
        whole(first[:, :, :kv]),
        whole(first[:, :, kv : 2 * kv]),
        whole(first[:, :, 2 * kv : 5 * kv]),
        whole(first[:, :, 5 * kv :]).T,
    )

    def both(grad, row_axis):
        part = lax.psum_scatter(grad, "row", scatter_dimension=row_axis, tiled=True)
        return lax.psum_scatter(part, "col", scatter_dimension=1 - row_axis, tiled=True)

    return (
        lax.psum(gains, ("row", "col")),
        (
            both(query, 0),
            both(key, 0),
            both(value, 0),
            both(out, 1),
            both(whole(gate), 0),
            both(whole(up), 0),
            both(whole(down).T, 1),
        ),
    )


PACKS = 4
MESH = pl.DeviceIdType.MESH


class Sides:
    def __init__(self, at, core0, core1):
        if core0 == core1:
            along_x = twin_x = int(core0 == "x")
        else:
            along_x = at.c if core0 == "y" else 1 - at.c
            twin_x = 1 - along_x
        self.near_x, self.near_y, self.far_x, self.far_y = self.spots(at, along_x)
        self.near = at.device(self.near_x, at.z, self.near_y, at.c)
        self.far = at.device(self.far_x, at.z, self.far_y, at.c)
        twin = self.spots(at, twin_x)
        rest = (1 - at.x, 1 - at.y)
        self.order = [(self.far_x, self.far_y), rest, (self.near_x, self.near_y), (at.x, at.y)]
        self.twin_order = [twin[2:], rest, twin[:2], (at.x, at.y)]

    @staticmethod
    def spots(at, along_x):
        x, y = at.x, at.y
        near = (x + along_x * (1 - 2 * x), y + (1 - along_x) * (1 - 2 * y))
        far = (x + (1 - along_x) * (1 - 2 * x), y + along_x * (1 - 2 * y))
        return near + far


class Place:
    def __init__(self):
        row, x = lax.axis_index("row"), lax.axis_index("col")
        z, y, c = row // 4, (row // 2) % 2, row % 2
        self.x, self.z, self.y, self.c = x, z, y, c
        self.xa, self.ya = jnp.where(c == 0, 1 - x, x), jnp.where(c == 0, y, 1 - y)
        self.xb, self.yb = jnp.where(c == 0, x, 1 - x), jnp.where(c == 0, 1 - y, y)
        self.others = [(z + k) % 4 for k in (1, 2, 3)]
        self.line = [self.device(x, other, y, c) for other in self.others]
        self.near = self.device(self.xa, z, self.ya, c)
        self.far = self.device(self.xb, z, self.yb, c)
        self.twin = self.device(x, z, y, 1 - c)
        self.cross = self.device(1 - x, z, y, c)
        self.corner = self.device(1 - x, z, 1 - y, c)

    @staticmethod
    def device(x, z, y, c):
        return ((z * 2 + y) * 2 + c, x)

    def greet(self):
        barrier = pltpu.get_barrier_semaphore()
        peers = self.line + [self.near, self.far, self.corner, self.twin]
        for peer in peers:
            pl.semaphore_signal(barrier, inc=1, device_id=peer, device_id_type=MESH)
        pl.semaphore_wait(barrier, len(peers))


def remote(src, dst, send, recv, device):
    return pltpu.make_async_remote_copy(
        src_ref=src, dst_ref=dst, send_sem=send, recv_sem=recv, device_id=device, device_id_type=MESH
    )


GATHER_PLAN = [
    (0, 0, 512, 0, "x", "y"),
    (0, 512, 512, 0, "y", "x"),
    (0, 1024, 512, 0, "x", "x"),
    (1, 0, 768, 0, "y", "y"),
    (2, 0, 768, 1, "x", "x"),
    (1, 768, 768, 0, "y", "x"),
    (2, 768, 768, 0, "x", "y"),
    (3, 0, 768, 1, "x", "y"),
    (3, 768, 768, 1, "x", "y"),
]
FORWARD_ORDER = [
    ("B", 0), ("B", 1), "norm", ("F", 0), ("B", 2), ("F", 1), ("B", 3), ("S", 0), ("F", 2), ("B", 4),
    ("S", 1), ("T", 0), ("F", 3), ("B", 5), ("S", 2), ("T", 1), "kv", ("F", 4), ("B", 6), "q", ("T", 2),
    ("S", 3), ("F", 5), ("B", 7), "a0", ("S", 4), "a1", ("F", 6), ("B", 8), "a2", ("F", 7), ("S", 5),
    ("T", 3), ("T", 4), "a3", "br", ("S", 7), ("S", 6), ("F", 8), "h0", ("T", 5), ("S", 8), ("T", 6),
    ("T", 7), "h1", ("T", 8), "o0", "o1",
]
SCATTER_PLAN = [
    (3, 0, 1, "y", "x"),
    (1, 0, 0, "x", "y"),
    (2, 0, 0, "y", "x"),
    (3, 1, 1, "y", "x"),
    (1, 1, 0, "x", "x"),
    (2, 1, 0, "y", "y"),
    (0, 1, 0, "y", "x"),
    (0, 0, 0, "x", "y"),
]
BACKWARD_ORDER = [
    "ld", "w0", ("B", 0), "d0", "w1", ("B", 1), ("1", 0), "w2", "m0", ("1", 1), ("B", 2), "w3", ("B", 3),
    ("1", 2), "d1", "w4", "w5", ("B", 5), "m1", ("2", 1), ("1", 3), ("B", 4), "norm", ("1", 5), ("2", 0),
    "mx", "a0", ("1", 4), ("2", 3), ("3", 0), "a1", "a2", ("2", 2), ("3", 1), ("2", 5), "a3", ("3", 3), "g1",
    ("B", 6), ("4", 1), ("3", 2), ("3", 5), ("2", 4), ("1", 6), "kvw", "g0", "in", ("4", 0), ("B", 7),
    ("3", 4), ("2", 6), ("4", 3), ("1", 7), ("4", 2), ("3", 6), ("4", 4), ("2", 7), ("4", 5), ("3", 7),
    ("4", 6), ("4", 7),
]
RING = 6


class Gather:
    def __init__(self, at, plan, own_refs, out_refs, copied, sent, came):
        x, y, z = at.x, at.y, at.z
        self.plan, self.arrived = plan, set()
        size = own_refs[0].shape[0]
        rows = pl.ds(pl.multiple_of(at.c * size, 8), size)
        self.steps = []
        for i, (pack, lane, lanes, kind, *axes) in enumerate(plan):
            sides = Sides(at, *axes)
            cols = pl.ds(lane, lanes)
            own = own_refs[pack].at[:, cols]

            def one(xx, yy):
                return out_refs[pack].at[xx, z, yy, rows, cols]

            def line(xx, yy, slot, device):
                ref = out_refs[pack].at[xx, :, yy, rows, cols]
                return remote(ref, ref, sent.at[i, slot], came.at[i, slot], device)

            step = {"kind": kind, "keep": pltpu.make_async_copy(own, one(x, y), copied.at[i])}
            step["line"] = [remote(own, one(x, y), sent.at[i, k], came.at[i, k], at.line[k]) for k in range(3)]
            if kind == 0:
                step["near"] = line(x, y, 3, sides.near)
            else:
                step["near"] = remote(own, one(x, y), sent.at[i, 3], came.at[i, 3], sides.near)
                step["more"] = [
                    remote(
                        one(sides.near_x, sides.near_y),
                        one(sides.near_x, sides.near_y),
                        sent.at[i, 4 + k],
                        came.at[i, 4 + k],
                        at.line[k],
                    )
                    for k in range(3)
                ]
            step["far"] = [line(x, y, 7, sides.far), line(sides.near_x, sides.near_y, 8, sides.far)]
            step["twin"] = [
                line(xx, yy, 9 + j, at.twin)
                for j, (xx, yy) in enumerate(
                    [(x, y), (sides.near_x, sides.near_y), (sides.far_x, sides.far_y), (1 - x, 1 - y)]
                )
            ]
            self.steps.append(step)

    def begin(self, i):
        if 0 <= i < len(self.steps):
            self.steps[i]["keep"].start()
            for copy in self.steps[i]["line"]:
                copy.start()
            if self.steps[i]["kind"] == 1:
                self.steps[i]["near"].start()

    def first(self, i):
        if 0 <= i < len(self.steps):
            step = self.steps[i]
            if step["kind"] == 1:
                step["near"].wait_recv()
                for copy in step["more"]:
                    copy.start()
            for copy in step["line"]:
                copy.wait_recv()
            step["keep"].wait()
            if step["kind"] == 0:
                step["near"].start()
            step["far"][0].start()
            step["twin"][0].start()

    def second(self, i):
        if 0 <= i < len(self.steps):
            step = self.steps[i]
            for copy in [step["near"]] if step["kind"] == 0 else step["more"]:
                copy.wait_recv()
            step["far"][1].start()
            step["twin"][1].start()

    def third(self, i):
        if 0 <= i < len(self.steps):
            step = self.steps[i]
            for j in range(2):
                step["far"][j].wait_recv()
                step["twin"][2 + j].start()

    def arrive(self, *chunks):
        for i in chunks:
            if i not in self.arrived:
                self.arrived.add(i)
                for copy in self.steps[i]["twin"]:
                    copy.wait_recv()

    def arrive_lanes(self, pack, low, high):
        for i, (held, lane, lanes, *_) in enumerate(self.plan):
            if held == pack and lane < high and lane + lanes > low:
                self.arrive(i)

    def run(self, moves):
        for name, i in moves:
            {"B": self.begin, "F": self.first, "S": self.second, "T": self.third}[name](i)

    def finish(self):
        for step in self.steps:
            for copy in step["line"] + step.get("more", []) + [step["near"]] + step["far"] + step["twin"]:
                copy.wait_send()


def forward_kernel(plan, *refs):
    x_ref, gain_ref, frequency_ref, ids_ref, ends_ref = refs[:5]
    own_refs, full_refs = refs[5:9], refs[9:13]
    saved = refs[13:27]
    weights, attn_in, y, kv, dup, flip, mix, logs, residual, mlp_in, acts, hidden, output = refs[27:40]
    cos_ref, sin_ref, first_ref, last_ref = refs[40:44]
    copied, sent, came, loaded, stored, kv_sent, kv_came = refs[44:]
    gain_one_ref, gain_two_ref = gain_ref.at[pl.ds(0, 1)], gain_ref.at[pl.ds(1, 1)]
    at = Place()
    at.greet()
    gather = Gather(at, plan, own_refs, full_refs, copied, sent, came)
    tokens, width = x_ref.shape
    lanes = weights.shape[2]

    def load(pack, cut, slot, k):
        size = lanes // 2
        return [
            pltpu.make_async_copy(
                full_refs[pack].at[half].reshape(width, lanes).at[:, pl.ds(cut * size, size)],
                weights.at[slot, :, pl.ds(half * size, size)],
                loaded.at[k, half],
            )
            for half in range(2)
        ]

    def load_first(half, lane, size, k):
        part = pl.ds(lane, size)
        return pltpu.make_async_copy(
            full_refs[0].at[half].reshape(width, lanes).at[:, part], weights.at[half, :, part], loaded.at[k, half]
        )

    project_loads = [load_first(half, 0, 8 * LANES, 0) for half in range(2)]
    out_loads = [load_first(half, 8 * LANES, lanes - 8 * LANES, 1) for half in range(2)]
    gate_loads = [load(1, 0, 2, 2) + load(2, 0, 3, 3), load(1, 1, 0, 4) + load(2, 1, 1, 5)]
    down_loads = [load(3, 0, 2, 6), load(3, 1, 3, 7)]

    def save(k, ref):
        copy = pltpu.make_async_copy(ref, saved[k], stored.at[k])
        copy.start()
        return copy

    mine = pl.ds(pl.multiple_of(at.x * tokens, tokens), tokens)
    exchanges = [
        remote(kv.at[half, mine, :], kv.at[half, mine, :], kv_sent.at[half], kv_came.at[half], at.cross)
        for half in range(2)
    ]
    block = 256
    steps = tokens // block
    span = pl.ds(7 * LANES, 5 * LANES)
    size = lanes // 2
    saves = {}

    def norm():
        length = jnp.sum(1 - (ids_ref[...] & 1), axis=1, keepdims=True)
        index = at.x * tokens + lax.broadcasted_iota(jnp.int32, (1, tokens), 1)
        first_ref[...] = jnp.where(index < length, 0, length)
        row_start = lax.axis_index("row") * ids_ref.shape[1]
        last_ref[...] = ends_ref[:, pl.ds(pl.multiple_of(at.x * tokens, LANES), tokens)] - row_start
        index = at.x * tokens + lax.broadcasted_iota(jnp.int32, (tokens, LANES), 0)
        position = (index - jnp.where(index < length, 0, length)).astype(f32)
        angles = position * frequency_ref[...]
        cos_ref[...] = jnp.cos(angles)
        sin_ref[...] = jnp.sin(angles)
        for k, ref in enumerate((cos_ref, sin_ref, first_ref, last_ref)):
            saves[10 + k] = save(10 + k, ref)
        values = x_ref[...].astype(f32)
        inverse = lax.rsqrt(jnp.mean(values * values, axis=1, keepdims=True) + eps)
        attn_in[...] = (values * inverse * gain_one_ref[...]).astype(bf16)
        saves[0] = save(0, attn_in)

    def keys():
        gather.arrive_lanes(0, 0, 8 * LANES)
        start(project_loads)
        for half in range(2):
            project_loads[half].wait()
            project_tiles(half, range(2), attn_in, weights, cos_ref, sin_ref, y)
            kv[half, mine, :] = y[half, :, : 3 * LANES]
            exchanges[half].start()

    def queries():
        for half in range(2):
            project_tiles(half, range(2, 4), attn_in, weights, cos_ref, sin_ref, y)
        saves[1] = save(1, y)

    def attend_all(moves):
        def rows_of(i, carry):
            half = i // steps
            for k in range(2):

                @pl.when(i == k * steps)
                def _(k=k):
                    exchanges[k].wait()

            @pl.when(i % steps == 0)
            def _():
                load_groups(kv, half, dup, flip)

            attend_rows(half, i % steps, block, y, dup, flip, first_ref, last_ref, mix, logs)
            for k, part in enumerate(moves):
                if part:

                    @pl.when(i == k * steps // 2)
                    def _(part=part):
                        gather.run(part)

            return carry

        lax.fori_loop(0, 2 * steps, rows_of, 0)
        saves[2], saves[3], saves[4] = save(2, kv), save(3, mix), save(4, logs)

    def branch():
        gather.arrive_lanes(0, 8 * LANES, lanes)
        start(out_loads)
        wait(out_loads)

        def rows_of(i, carry):
            rows = pl.ds(pl.multiple_of(i * 256, 256), 256)
            total = x_ref[rows, :].astype(f32)
            for half in range(2):
                total = total + dot_nt(mix[half, rows, :], weights[half, :, span])
            residual[rows, :] = total
            inverse = lax.rsqrt(jnp.mean(total * total, axis=1, keepdims=True) + eps)
            mlp_in[rows, :] = (total * inverse * gain_two_ref[...]).astype(bf16)
            return carry

        lax.fori_loop(0, tokens // 256, rows_of, 0)
        saves[5], saves[6] = save(5, residual), save(6, mlp_in)

    def hide(cut):
        gather.arrive_lanes(1, cut * size, (cut + 1) * size)
        gather.arrive_lanes(2, cut * size, (cut + 1) * size)
        start(gate_loads[cut])
        wait(gate_loads[cut])
        slot = 2 - 2 * cut

        def tile_of(i, carry):
            half, tile = i // (size // 256), i % (size // 256)
            cols = pl.ds(pl.multiple_of(i * 256, 256), 256)
            into = pl.ds(pl.multiple_of(cut * size + tile * 256, 256), 256)
            gate = dot_nn(mlp_in[...], weights[slot, :, cols])
            up = dot_nn(mlp_in[...], weights[slot + 1, :, cols])
            acts[half, 0, :, into] = gate
            acts[half, 1, :, into] = up
            hidden[half, :, into] = (gate * jax.nn.sigmoid(gate) * up).astype(bf16)
            return carry

        lax.fori_loop(0, lanes // 256, tile_of, 0)
        if cut == 1:
            saves[7], saves[8] = save(7, acts), save(8, hidden)

    def finish_rows(cut):
        gather.arrive_lanes(3, cut * size, (cut + 1) * size)
        start(down_loads[cut])
        wait(down_loads[cut])
        if cut == 0:
            saves.pop(5).wait()

        def rows_of(i, carry):
            rows = pl.ds(pl.multiple_of(i * 256, 256), 256)
            total = residual[rows, :]
            for half in range(2):
                total = total + dot_nt(
                    hidden[half, rows, pl.ds(cut * size, size)], weights[2 + cut, :, pl.ds(half * size, size)]
                )
            if cut == 0:
                residual[rows, :] = total
            else:
                output[rows, :] = total.astype(bf16)
            return carry

        lax.fori_loop(0, tokens // 256, rows_of, 0)
        if cut == 1:
            saves[9] = save(9, output)

    work = {
        "norm": norm,
        "kv": keys,
        "q": queries,
        "br": branch,
        "h0": lambda: hide(0),
        "h1": lambda: hide(1),
        "o0": lambda: finish_rows(0),
        "o1": lambda: finish_rows(1),
    }
    plain, looped = split_schedule(FORWARD_ORDER)
    for entry in plain:
        if isinstance(entry, tuple):
            gather.run([entry])
        elif entry == "a":
            attend_all(looped)
        else:
            work[entry]()
    gather.finish()
    for copy in saves.values():
        copy.wait()


def forward_special(layer_input, gains, frequency, ids, ends, packs):
    plan = GATHER_PLAN
    tokens, width = layer_input.shape
    rows, lanes = packs[0].shape
    keys = 2 * tokens
    dma, vmem = pltpu.SemaphoreType.DMA, pltpu.VMEM
    anywhere = pl.BlockSpec(memory_space=pl.ANY)
    near = pl.BlockSpec(memory_space=pltpu.VMEM)
    saved = [
        ((tokens, width), bf16),
        ((2, tokens, 8 * LANES), bf16),
        ((2, keys, 3 * LANES), bf16),
        ((2, tokens, 5 * LANES), bf16),
        ((2, 16, tokens), f32),
        ((tokens, width), f32),
        ((tokens, width), bf16),
        ((2, 2, tokens, lanes), f32),
        ((2, tokens, lanes), bf16),
        ((tokens, width), bf16),
        ((tokens, LANES), f32),
        ((tokens, LANES), f32),
        ((1, tokens), jnp.int32),
        ((1, tokens), jnp.int32),
    ]
    full = [((2, 4, 2, 2 * rows, lanes), bf16)] * PACKS
    count = len(plan)
    outs = pl.pallas_call(
        lambda *refs: forward_kernel(plan, *refs),
        out_shape=[jax.ShapeDtypeStruct(*shape) for shape in full + saved],
        in_specs=[near] * 5 + [anywhere] * PACKS,
        out_specs=[anywhere] * (PACKS + len(saved)),
        scratch_shapes=[
            vmem((4, width, lanes), bf16),
            vmem(*saved[0]),
            vmem(*saved[1]),
            vmem(*saved[2]),
            vmem((6, keys, LANES), bf16),
            vmem((6, LANES, keys), bf16),
            vmem(*saved[3]),
            vmem(*saved[4]),
            vmem(*saved[5]),
            vmem(*saved[6]),
            vmem(*saved[7]),
            vmem(*saved[8]),
            vmem(*saved[9]),
            vmem(*saved[10]),
            vmem(*saved[11]),
            vmem(*saved[12]),
            vmem(*saved[13]),
            dma((count,)),
            dma((count, 13)),
            dma((count, 13)),
            dma((8, 2)),
            dma((len(saved),)),
            dma((2,)),
            dma((2,)),
        ],
        compiler_params=pltpu.CompilerParams(
            collective_id=1, has_side_effects=True, vmem_limit_bytes=VMEM_BYTES
        ),
        name="forward",
    )(layer_input, gains, frequency, ids, ends, *packs)
    return [part.reshape(2, 16 * rows, lanes) for part in outs[:PACKS]], outs[PACKS:]


def split_schedule(order):
    plain, looped, part = [], [[] for _ in range(4)], None
    for entry in order:
        if isinstance(entry, str) and entry[0] == "a":
            part = int(entry[1])
            if part == 0:
                plain.append("a")
        elif isinstance(entry, tuple) and part is not None and part < 4:
            looped[part].append(entry)
        else:
            part = None
            plain.append(entry)
    return plain, looped


def start(copies):
    for copy in copies:
        copy.start()


def wait(copies):
    for copy in copies:
        copy.wait()


class Scatter:
    def __init__(self, at, grad_ref, parts, sums, temps, sems, out_ref, pushes):
        self.pushes, self.ready = pushes, set()
        self.at, self.grad, self.sums, self.temps = at, grad_ref, sums, temps
        self.from_twin, self.from_far, self.from_near, self.from_line = parts
        self.sent, self.came, self.loaded, self.stored = sems
        self.out_ref = out_ref
        to_far, to_near, to_line, result = sums
        self.steps = []
        for i, (pack, cut, kind, *axes) in enumerate(SCATTER_PLAN):
            sides = Sides(at, *axes)
            lanes = result.shape[2]

            def send(src, dst, slot, device, i=i):
                return remote(src, dst, self.sent.at[i, slot], self.came.at[i, slot], device)

            self.steps.append(
                {
                    "twin": [
                        send(self.line(i, sides.twin_order[j], 1 - at.c), self.from_twin.at[i, j], j, at.twin)
                        for j in range(4)
                    ],
                    "far": [
                        send(to_far.at[i % RING, j], self.from_far.at[i, j], 4 + j, sides.far) for j in range(2)
                    ],
                    "kind": kind,
                    "near": (
                        send(to_near.at[i % RING], self.from_near.at[i], 6, sides.near)
                        if kind == 0
                        else send(to_near.at[i % RING, at.z], self.from_near.at[i, 3], 6, sides.near)
                    ),
                    "more": [
                        send(to_near.at[i % RING, at.others[k]], self.from_near.at[i, k], 10 + k, at.line[k])
                        for k in range(3 * kind)
                    ],
                    "own": [self.line(i, sides.order[j], at.c) for j in range(4)],
                    "line": [
                        send(to_line.at[i % RING, k], self.from_line.at[i, k], 7 + k, at.line[k])
                        for k in range(3)
                    ],
                    "store": pltpu.make_async_copy(
                        result.at[i % RING], out_ref.at[pack, :, pl.ds(cut * lanes, lanes)], self.stored.at[i]
                    ),
                }
            )

    def line(self, i, place, core):
        size = self.sums[3].shape[1]
        return self.grad.at[i, place[0], :, place[1], pl.ds(pl.multiple_of(core * size, 8), size)]

    def load(self, src, dst, k):
        copy = pltpu.make_async_copy(src, dst, self.loaded.at[k])
        copy.start()
        return copy

    def pushed(self, i):
        if i not in self.ready:
            self.ready.add(i)
            wait(self.pushes(i))

    def begin(self, i):
        self.pushed(i)
        for j in (1, 0, 2, 3):
            self.steps[i]["twin"][j].start()

    def first(self, i):
        step, to_far, temp, slot = self.steps[i], self.sums[0], self.temps[0], i % RING
        self.free(i, lambda old: old["far"])
        copies = []
        for j in (1, 0):
            own = self.load(step["own"][j], to_far.at[slot, j], 2 * j)
            step["twin"][j].wait_recv()
            copies.append((j, [own, self.load(self.from_twin.at[i, j], temp.at[j], 2 * j + 1)]))
        yield
        for j, pair in copies:
            wait(pair)

            def body(q, carry, j=j):
                to_far[slot, j, q] = (to_far[slot, j, q].astype(f32) + temp[j, q].astype(f32)).astype(bf16)
                return carry

            lax.fori_loop(0, 4, body, 0)
            step["far"][j].start()

    def second(self, i):
        step, to_near, temp, slot = self.steps[i], self.sums[1], self.temps[1], i % RING
        self.free(i, lambda old: [old["near"]] + old["more"])
        copies = [self.load(step["own"][2], to_near.at[slot], 4)]
        step["twin"][2].wait_recv()
        copies.append(self.load(self.from_twin.at[i, 2], temp.at[0], 5))
        step["far"][1].wait_recv()
        copies.append(self.load(self.from_far.at[i, 1], temp.at[1], 6))
        yield
        wait(copies)

        def body(q, carry):
            value = to_near[slot, q].astype(f32) + temp[0, q].astype(f32) + temp[1, q].astype(f32)
            to_near[slot, q] = value.astype(bf16)
            return carry

        lax.fori_loop(0, 4, body, 0)
        if step["kind"] == 0:
            step["near"].start()
        start(step["more"])

    def third(self, i):
        step, temp, slot = self.steps[i], self.temps[2], i % RING
        to_near, to_line, result = self.sums[1:]
        early = step["kind"] == 1
        self.free(i, lambda old: old["line"])
        if i >= RING:
            self.steps[slot]["store"].wait()
        copies = [self.load(step["own"][3], temp.at[0], 7)]
        step["twin"][3].wait_recv()
        copies.append(self.load(self.from_twin.at[i, 3], temp.at[1], 8))
        step["far"][0].wait_recv()
        copies.append(self.load(self.from_far.at[i, 0], temp.at[2], 9))
        if early:
            for copy in step["more"]:
                copy.wait_recv()
            copies.append(self.load(self.from_near.at[i, pl.ds(0, 3)], temp.at[3, pl.ds(0, 3)], 10))
        else:
            step["near"].wait_recv()
            copies.append(self.load(self.from_near.at[i], temp.at[3], 10))
        yield
        wait(copies)
        if early:
            value = to_near[slot, self.at.z].astype(f32)
            for k in range(3):
                value = value + temp[3, k].astype(f32)
            to_near[slot, self.at.z] = value.astype(bf16)
            step["near"].start()

        def total(q):
            value = (temp[0, q].astype(f32) + temp[1, q].astype(f32)) + temp[2, q].astype(f32)
            return value if early else value + temp[3, q].astype(f32)

        for k in range(3):
            to_line[slot, k] = total(self.at.others[k]).astype(bf16)
            step["line"][k].start()
        result[slot] = total(self.at.z)

    def fourth(self, i):
        step, temp, result, slot = self.steps[i], self.temps[3], self.sums[3], i % RING
        copies = []
        for k in range(3):
            step["line"][k].wait_recv()
            copies.append(self.load(self.from_line.at[i, k], temp.at[k], 11 + k))
        if step["kind"] == 1:
            step["near"].wait_recv()
            copies.append(self.load(self.from_near.at[i, 3], temp.at[3], 14))
        yield
        wait(copies)
        value = result[slot]
        for k in range(len(copies)):
            value = value + temp[k].astype(f32)
        result[slot] = value
        step["store"].start()

    def run(self, stages):
        names = {"1": self.first, "2": self.second, "3": self.third, "4": self.fourth}
        turn = []

        def flush():
            works = [names[name](i) for name, i in turn]
            for work in works:
                next(work)
            for work in works:
                next(work, None)
            turn.clear()

        for name, i in stages:
            if name == "B":
                self.begin(i)
            else:
                if any(name == held or (name > held and i == j) or i == j + RING for held, j in turn):
                    flush()
                turn.append((name, i))
        flush()

    def free(self, i, sends):
        if i >= RING:
            for copy in sends(self.steps[i - RING]):
                copy.wait_send()

    def finish(self):
        for i, step in enumerate(self.steps):
            for copy in step["twin"]:
                copy.wait_send()
            if i + RING >= len(self.steps):
                for copy in step["far"] + [step["near"]] + step["more"] + step["line"]:
                    copy.wait_send()
                step["store"].wait()


def flip_rows(src, dst):
    for tile in range(src.shape[1] // LANES):
        cols = pl.ds(tile * LANES, LANES)
        dst[cols, :] = src[:, cols].astype(f32).T.astype(bf16)


def backward_kernel(*refs):
    grad_out_ref, x_ref, gain_ref, cos_ref, sin_ref, first_ref, last_ref = refs[:7]
    full_refs, kept = refs[7:11], refs[11:20]
    gain_one_ref, gain_two_ref = gain_ref.at[pl.ds(0, 1)], gain_ref.at[pl.ds(1, 1)]
    attn_in_ref, y_ref, kv_ref, mix_ref, logs_ref, residual_ref, mlp_in_ref, acts_ref, hidden_ref = kept
    sum_ref, grad_in_ref, gain_sum_ref, grad_ref = refs[20:24]
    parts = refs[24:28]
    scratch = refs[28:]
    sums, temps = scratch[:4], scratch[4:8]
    staging, grad_res, branch, kv_out, kv_in, gains = scratch[8:14]
    sems, pulled, pushed, kv_sent, kv_came, gain_sent, gain_came = scratch[14:18], *scratch[18:24]
    at = Place()
    at.greet()
    dma = pltpu.SemaphoreType.DMA
    vmem = pltpu.VMEM
    tokens, width = grad_res.shape
    lanes = hidden_ref.shape[2]
    size = lanes // 2
    tiles = size // 256

    def pull(src, dst, k):
        return pltpu.make_async_copy(src, dst, pulled.at[k])

    def pull_cut(pack, cut, dst, k):
        return [
            pull(
                full_refs[pack].at[half].reshape(width, lanes).at[:, pl.ds(cut * size, size)],
                dst.at[:, pl.ds(half * size, size)],
                k + half,
            )
            for half in range(2)
        ]

    def push(i):
        slot = i % 2
        return [
            pltpu.make_async_copy(
                staging.at[slot, half], grad_ref.at[i, half].reshape(width, size), pushed.at[slot, half]
            )
            for half in range(2)
        ]

    scatter = Scatter(at, grad_ref, parts, sums, temps, sems, sum_ref, push)
    plain, looped = split_schedule(BACKWARD_ORDER)
    first_end, second_end, third_end = (plain.index(name) for name in ("norm", "mx", "in"))

    def follow(entries, work):
        moves = []
        for entry in entries:
            if isinstance(entry, tuple):
                moves.append(entry)
            else:
                scatter.run(moves)
                moves = []
                work[entry]()
        scatter.run(moves)

    def weight_grad(i, left, right):
        def body(k, carry):
            half, cols = k // tiles, pl.ds(pl.multiple_of((k % tiles) * 256, 256), 256)
            staging[i % 2, half, :, cols] = dot_nn(left[...], right[half, :, cols]).astype(bf16)
            return carry

        if i >= 2:
            scatter.pushed(i - 2)
        lax.fori_loop(0, 2 * tiles, body, 0)
        start(push(i))

    def feed_forward(weights, acts, hidden, grad_out, out_turned, in_turned, grad_acts):
        def pulls(cut):
            cols = pl.ds(cut * size, size)
            return {
                "hidden": [pull(hidden_ref.at[:, :, cols], hidden, 0)],
                "down": pull_cut(3, cut, weights.at[0], 1),
                "acts": [pull(acts_ref.at[:, :, :, cols], acts, 3)],
                "gate": pull_cut(1, cut, weights.at[1], 4) + pull_cut(2, cut, weights.at[2], 6),
            }

        cuts = [pulls(0), pulls(1)]
        given = [pull(grad_out_ref, grad_out, 8), pull(mlp_in_ref, branch, 9)]

        def load():
            copies = cuts[0]
            start(given + copies["hidden"] + copies["down"] + copies["acts"] + copies["gate"])
            wait(given)
            flip_rows(grad_out, out_turned)
            flip_rows(branch, in_turned)

        def down_grad(cut):
            wait(cuts[cut]["hidden"])
            weight_grad(3 * cut, out_turned, hidden)
            if cut == 0:
                start(cuts[1]["hidden"])

        def act_grad(cut):
            wait(cuts[cut]["down"] + cuts[cut]["acts"])

            def tile_of(k, carry):
                half, tile = k // tiles, k % tiles
                cols = pl.ds(pl.multiple_of(tile * 256, 256), 256)
                grad = dot_nn(grad_out[...], weights[0, :, pl.ds(pl.multiple_of(k * 256, 256), 256)])
                gate, up = acts[half, 0, :, cols], acts[half, 1, :, cols]
                sigmoid = jax.nn.sigmoid(gate)
                grad_acts[0, half, :, cols] = (
                    grad * up * sigmoid * (1.0 + gate * (1.0 - sigmoid))
                ).astype(bf16)
                grad_acts[1, half, :, cols] = (grad * gate * sigmoid).astype(bf16)
                return carry

            lax.fori_loop(0, 2 * tiles, tile_of, 0)
            if cut == 0:
                start(cuts[1]["down"] + cuts[1]["acts"])

        def input_grad(cut):
            wait(cuts[cut]["gate"])

            def rows_of(k, carry):
                rows = pl.ds(pl.multiple_of(k * 256, 256), 256)
                total = None if cut == 0 else grad_res[rows, :]
                for half in range(2):
                    for part in range(2):
                        term = dot_nt(
                            grad_acts[part, half, rows, :], weights[1 + part, :, pl.ds(half * size, size)]
                        )
                        total = term if total is None else total + term
                grad_res[rows, :] = total
                return carry

            lax.fori_loop(0, tokens // 256, rows_of, 0)
            if cut == 0:
                start(cuts[1]["gate"])

        work = {"ld": load}
        for cut in range(2):
            work["w" + str(3 * cut)] = lambda cut=cut: down_grad(cut)
            work["d" + str(cut)] = lambda cut=cut: act_grad(cut)
            work["w" + str(3 * cut + 1)] = lambda cut=cut: weight_grad(3 * cut + 1, in_turned, grad_acts.at[0])
            work["w" + str(3 * cut + 2)] = lambda cut=cut: weight_grad(3 * cut + 2, in_turned, grad_acts.at[1])
            work["m" + str(cut)] = lambda cut=cut: input_grad(cut)
        follow(plain[:first_end], work)

    pl.run_scoped(
        feed_forward,
        vmem((3, width, lanes), bf16),
        vmem((2, 2, tokens, size), f32),
        vmem((2, tokens, size), bf16),
        vmem((tokens, width), bf16),
        vmem((width, tokens), bf16),
        vmem((width, tokens), bf16),
        vmem((2, 2, tokens, size), bf16),
    )
    def second_norm(residual, grad_out):
        copies = [pull(residual_ref, residual, 0), pull(grad_out_ref, grad_out, 1)]
        start(copies)
        wait(copies)
        gain = gain_two_ref[...]

        def rows_of(k, carry):
            rows = pl.ds(pl.multiple_of(k * 128, 128), 128)
            value, grad = residual[rows, :], grad_res[rows, :]
            inverse = lax.rsqrt(jnp.mean(value * value, axis=1, keepdims=True) + eps)
            normed = value * inverse
            scaled = grad * gain
            inner = jnp.mean(scaled * normed, axis=1, keepdims=True)
            total = grad_out[rows, :].astype(f32) + inverse * (scaled - normed * inner)
            grad_res[rows, :] = total
            branch[rows, :] = total.astype(bf16)
            return carry + jnp.sum(grad * normed, axis=0, keepdims=True)

        gains[0, pl.ds(1, 1), :] = lax.fori_loop(0, tokens // 128, rows_of, jnp.zeros((1, width), f32))

    gains[0] = jnp.zeros(gains.shape[1:], f32)
    pl.run_scoped(second_norm, vmem((tokens, width), f32), vmem((tokens, width), bf16))
    follow(plain[first_end + 1 : second_end], {})

    def attention(weights, y, kv, dup, flip, acc, mix, grad_mix, grad_y, turned, logs, grad_kv, held):
        copies = [
            pull(full_refs[0].at[half].reshape(width, lanes), weights.at[half], half) for half in range(2)
        ] + [
            pull(y_ref, y, 2),
            pull(kv_ref, kv, 3),
            pull(mix_ref, mix, 4),
            pull(logs_ref, logs, 5),
            pull(attn_in_ref, held, 6),
        ]
        def mix_grad():
            start(copies)
            wait(copies[:2])

            def rows_of(k, carry):
                half, rows = k // 2, pl.ds(pl.multiple_of((k % 2) * 256, 256), 256)
                grad_mix[half, rows, :] = dot_nn(
                    branch[rows, :], weights[half, :, pl.ds(7 * LANES, 5 * LANES)]
                ).astype(bf16)
                return carry

            lax.fori_loop(0, 4, rows_of, 0)
            wait(copies[2:])

        mine = pl.ds(pl.multiple_of(at.x * tokens, tokens), tokens)
        other = pl.ds(pl.multiple_of((1 - at.x) * tokens, tokens), tokens)
        block = 256
        steps = tokens // block

        def send_kv(half):
            return remote(kv_out.at[half], kv_in.at[half], kv_sent.at[half], kv_came.at[half], at.cross)

        def attend_back_all():
            def rows_of(i, carry):
                half = i // steps

                @pl.when(i % steps == 0)
                def _():
                    load_groups(kv, half, dup, flip)
                    acc[...] = jnp.zeros_like(acc)

                attend_back_rows(
                    half, i % steps, block, y, dup, flip, first_ref, last_ref, logs, grad_mix, cos_ref, sin_ref, grad_y, acc
                )

                @pl.when(i % steps == steps - 1)
                def _():
                    join_groups(acc, grad_kv, half)
                    kv_out[half] = grad_kv[half, other, :].astype(bf16)

                for k in range(2):

                    @pl.when(i == (k + 1) * steps - 1)
                    def _(k=k):
                        send_kv(k).start()

                for k, part in enumerate(looped):
                    if part:

                        @pl.when(i == k * steps // 2)
                        def _(part=part):
                            scatter.run(part)

                return carry

            lax.fori_loop(0, 2 * steps, rows_of, 0)

        def late_part():
            scatter.pushed(4)
            flip_rows(held, turned.at[0])
            flip_rows(branch, turned.at[1])
            for half in range(2):
                tail = dot_nn(turned[0], grad_y[half, :, pl.ds(6 * LANES, 2 * LANES)])
                head = dot_nn(turned[1], mix[half, :, pl.ds(0, LANES)])
                staging[0, half, :, pl.ds(0, LANES)] = tail[:, :LANES].astype(bf16)
                staging[0, half, :, pl.ds(LANES, LANES)] = (tail[:, LANES:] + head).astype(bf16)
                for k in range(2):
                    staging[0, half, :, pl.ds((2 + 2 * k) * LANES, 2 * LANES)] = dot_nn(
                        turned[1], mix[half, :, pl.ds((1 + 2 * k) * LANES, 2 * LANES)]
                    ).astype(bf16)
            start(push(6))
            load_x.start()

        def join_keys():
            lane = lane_of((tokens, LANES))
            lower = lane % HEAD < HEAD // 2
            for half in range(2):
                send_kv(half).wait()
                for tile in range(3):
                    cols = pl.ds(tile * LANES, LANES)
                    total = grad_kv[half, mine, cols] + kv_in[half, :, cols].astype(f32)
                    if tile < 2:
                        back = turn_back(total, cos_ref[...], sin_ref[...], lower)
                        total = back if tile == 0 else jnp.where(lane < HEAD, back, total)
                    grad_y[half, :, cols] = total.astype(bf16)

        def input_rows():
            load_x.wait()
            gain = gain_one_ref[...]

            def rows_of(k, carry):
                rows = pl.ds(pl.multiple_of(k * 128, 128), 128)
                grad = dot_nt(grad_y[0, rows, :], weights[0, :, pl.ds(0, 8 * LANES)]) + dot_nt(
                    grad_y[1, rows, :], weights[1, :, pl.ds(0, 8 * LANES)]
                )
                value = held[rows, :].astype(f32)
                inverse = lax.rsqrt(jnp.mean(value * value, axis=1, keepdims=True) + eps)
                normed = value * inverse
                scaled = grad * gain
                inner = jnp.mean(scaled * normed, axis=1, keepdims=True)
                branch[rows, :] = (grad_res[rows, :] + inverse * (scaled - normed * inner)).astype(bf16)
                return carry + jnp.sum(grad * normed, axis=0, keepdims=True)

            gains[0, pl.ds(0, 1), :] = lax.fori_loop(0, tokens // 128, rows_of, jnp.zeros((1, width), f32))

        load_x = pull(x_ref, held, 6)
        follow(
            plain[second_end : third_end + 1],
            {
                "mx": mix_grad,
                "a": attend_back_all,
                "g1": late_part,
                "kvw": join_keys,
                "g0": lambda: weight_grad(7, turned.at[0], grad_y),
                "in": input_rows,
            },
        )

    keys = kv_ref.shape[1]
    pl.run_scoped(
        attention,
        vmem((2, width, lanes), bf16),
        vmem(y_ref.shape, bf16),
        vmem(kv_ref.shape, bf16),
        vmem((6, keys, LANES), bf16),
        vmem((6, LANES, keys), bf16),
        vmem((6, keys, LANES), f32),
        vmem(mix_ref.shape, bf16),
        vmem(mix_ref.shape, bf16),
        vmem(y_ref.shape, bf16),
        vmem((2, width, tokens), bf16),
        vmem(logs_ref.shape, f32),
        vmem((2, keys, 3 * LANES), f32),
        vmem((tokens, width), bf16),
    )
    out = pull(branch, grad_in_ref, 0)
    out.start()
    swap = remote(gains.at[0], gains.at[1], gain_sent.at[0], gain_came.at[0], at.twin)
    spot = 2 + 2 * at.x + at.y
    plane = [
        remote(gains.at[spot], gains.at[spot], gain_sent.at[1 + k], gain_came.at[1 + k], peer)
        for k, peer in enumerate([at.near, at.far, at.corner])
    ]
    everyone = [
        remote(gains.at[6 + at.z], gains.at[6 + at.z], gain_sent.at[4 + k], gain_came.at[4 + k], at.line[k])
        for k in range(3)
    ]
    rest = plain[third_end + 1 :]
    swap.start()
    follow(rest[:2], {})
    swap.wait()
    gains[spot] = gains[0] + gains[1]
    start(plane)
    follow(rest[2:7], {})
    wait(plane)
    gains[6 + at.z] = (gains[2] + gains[3]) + (gains[4] + gains[5])
    start(everyone)
    follow(rest[7:], {})
    wait(everyone)
    gain_sum_ref[...] = (gains[6] + gains[7]) + (gains[8] + gains[9])
    out.wait()
    scatter.finish()


def backward_special(grad_output, layer_input, gains, cosine, sine, first, last, packs, kept):
    tokens, width = layer_input.shape
    _, depth, lanes = packs[0].shape
    rows, size = depth // 16, lanes // 2
    count = len(SCATTER_PLAN)
    dma, vmem = pltpu.SemaphoreType.DMA, pltpu.VMEM
    anywhere = pl.BlockSpec(memory_space=pl.ANY)
    near = pl.BlockSpec(memory_space=pltpu.VMEM)
    shape = jax.ShapeDtypeStruct
    outs = pl.pallas_call(
        backward_kernel,
        out_shape=[
            shape((PACKS, rows, lanes), f32),
            shape((tokens, width), bf16),
            shape((8, width), f32),
            shape((count, 2, 4, 2, 2 * rows, size), bf16),
            shape((count, 4, 4, rows, size), bf16),
            shape((count, 2, 4, rows, size), bf16),
            shape((count, 4, rows, size), bf16),
            shape((count, 3, rows, size), bf16),
        ],
        in_specs=[anywhere] * 2 + [near] * 5 + [anywhere] * (PACKS + len(kept)),
        out_specs=[anywhere, anywhere, near] + [anywhere] * 5,
        scratch_shapes=[
            vmem((RING, 2, 4, rows, size), bf16),
            vmem((RING, 4, rows, size), bf16),
            vmem((RING, 3, rows, size), bf16),
            vmem((RING, rows, size), f32),
            vmem((2, 4, rows, size), bf16),
            vmem((2, 4, rows, size), bf16),
            vmem((4, 4, rows, size), bf16),
            vmem((4, rows, size), bf16),
            vmem((2, 2, width, size), bf16),
            vmem((tokens, width), f32),
            vmem((tokens, width), bf16),
            vmem((2, tokens, 3 * LANES), bf16),
            vmem((2, tokens, 3 * LANES), bf16),
            vmem((10, 8, width), f32),
            dma((count, 13)),
            dma((count, 13)),
            dma((15,)),
            dma((count,)),
            dma((10,)),
            dma((2, 2)),
            dma((2,)),
            dma((2,)),
            dma((7,)),
            dma((7,)),
        ],
        compiler_params=pltpu.CompilerParams(
            collective_id=2, has_side_effects=True, vmem_limit_bytes=VMEM_BYTES
        ),
        name="backward",
    )(
        grad_output,
        layer_input,
        gains,
        cosine,
        sine,
        first,
        last,
        *[pack.reshape(2, 4, 2, 2 * rows, lanes) for pack in packs],
        *kept,
    )
    sums, grad_input, gain_sums = outs[:3]
    kv = lanes // 8
    mixed = sums[0]
    return (
        grad_input,
        gain_sums[:2],
        (
            mixed[:, 2 * kv : 5 * kv],
            mixed[:, :kv],
            mixed[:, kv : 2 * kv],
            mixed[:, 5 * kv :].T,
            sums[1],
            sums[2],
            sums[3].T,
        ),
    )


def special():
    return (lax.axis_size("row"), lax.axis_size("col")) == (16, 2)


def lane_of(shape):
    return lax.broadcasted_iota(jnp.int32, shape, len(shape) - 1)


def turn(values, cosine, sine, lower):
    ahead = pltpu.roll(values, LANES - HEAD // 2, 1)
    behind = pltpu.roll(values, HEAD // 2, 1)
    return values * cosine + jnp.where(lower, -ahead, behind) * sine


def turn_back(values, cosine, sine, lower):
    scaled = values * sine
    ahead = pltpu.roll(scaled, LANES - HEAD // 2, 1)
    behind = pltpu.roll(scaled, HEAD // 2, 1)
    return values * cosine - jnp.where(lower, -ahead, behind)


def project_tiles(half, pairs, attn_in_ref, weight_ref, cos_ref, sin_ref, y_ref):
    cosine, sine = cos_ref[...], sin_ref[...]
    lane = lane_of(cosine.shape)
    lower = lane % HEAD < HEAD // 2
    for pair in pairs:
        two = dot_nn(attn_in_ref[...], weight_ref[half, :, pl.ds(pair * 2 * LANES, 2 * LANES)]).astype(bf16)
        for side in range(2):
            tile = 2 * pair + side
            raw = two[:, side * LANES : (side + 1) * LANES].astype(f32)
            if tile == 2:
                out = raw
            else:
                out = turn(raw, cosine, sine, lower)
                if tile == 1:
                    out = jnp.where(lane < HEAD, out, raw)
                elif tile > 2:
                    out = out * HEAD ** (-0.5)
            y_ref[half, :, pl.ds(tile * LANES, LANES)] = out.astype(bf16)


def project_kernel(x_ref, gain_ref, weight_ref, cos_ref, sin_ref, attn_in_ref, y_ref):
    values = x_ref[...].astype(f32)
    inverse = lax.rsqrt(jnp.mean(values * values, axis=1, keepdims=True) + eps)
    attn_in_ref[...] = (values * inverse * gain_ref[...]).astype(bf16)
    for half in range(2):
        project_tiles(half, range(4), attn_in_ref, weight_ref, cos_ref, sin_ref, y_ref)


def head_rows(values, side, lane):
    return jnp.where((lane < HEAD) if side == 0 else (lane >= HEAD), values, jnp.zeros_like(values))


def twice(tile, side, lane):
    values = tile.astype(f32)
    other = pltpu.roll(values, HEAD, 1)
    keep = (lane < HEAD) if side == 0 else (lane >= HEAD)
    return jnp.where(keep, values, other)


def load_groups(kv_ref, half, dup_ref, flip_ref):
    for slot in range(6):
        tile = kv_ref[half, :, pl.ds((slot // 2) * LANES, LANES)]
        both = twice(tile, slot % 2, lane_of(tile.shape))
        dup_ref[slot] = both.astype(bf16)
        flip_ref[slot] = both.T.astype(bf16)


def seen(first_ref, last_ref, rows, keys):
    index = lax.broadcasted_iota(jnp.int32, (keys, rows.size), 0)
    return (index >= first_ref[:, rows]) & (index <= last_ref[:, rows])


def attend_rows(half, step, block, y_ref, dup_ref, flip_ref, first_ref, last_ref, mix_ref, log_ref):
    keys = dup_ref.shape[1]
    lane = lane_of((block, LANES))
    rows = pl.ds(pl.multiple_of(step * block, block), block)
    allowed = seen(first_ref, last_ref, rows, keys)
    previous = jnp.zeros((block, LANES), f32)
    for head in range(9):
        group = head // 3
        query = head_rows(y_ref[half, rows, pl.ds((3 + head // 2) * LANES, LANES)], head % 2, lane)
        scores = jnp.where(allowed, dot_nt(dup_ref[group], query), neg_fill)
        top = jnp.max(scores, axis=0, keepdims=True)
        powers = jnp.exp(scores - top)
        total = jnp.sum(powers, axis=0, keepdims=True)
        probs = (powers * (1.0 / total)).astype(bf16)
        mixed = dot_nn(flip_ref[3 + group], probs).T
        log_ref[half, pl.ds(head, 1), rows] = top + jnp.log(total)
        if head % 2 == 0:
            tile = jnp.where(lane < HEAD, previous, mixed)
            mix_ref[half, rows, pl.ds((head // 2) * LANES, LANES)] = tile.astype(bf16)
        previous = mixed


def attend_kernel(block, y_ref, kv_ref, first_ref, last_ref, mix_ref, log_ref, dup_ref, flip_ref):
    load_groups(kv_ref, 0, dup_ref, flip_ref)

    def rows_of(step, carry):
        attend_rows(0, step, block, y_ref, dup_ref, flip_ref, first_ref, last_ref, mix_ref, log_ref)
        return carry

    lax.fori_loop(0, y_ref.shape[1] // block, rows_of, 0)


def attend_back_rows(
    half, step, block, y_ref, dup_ref, flip_ref, first_ref, last_ref, log_ref, grad_ref, cos_ref, sin_ref, out_ref, acc_ref
):
    keys = dup_ref.shape[1]
    lane = lane_of((block, LANES))
    lower = lane % HEAD < HEAD // 2
    rows = pl.ds(pl.multiple_of(step * block, block), block)
    allowed = seen(first_ref, last_ref, rows, keys)
    previous = None
    for head in range(9):
        group = head // 3
        query = head_rows(y_ref[half, rows, pl.ds((3 + head // 2) * LANES, LANES)], head % 2, lane)
        upstream = head_rows(
            grad_ref[half, rows, pl.ds(((head + 1) // 2) * LANES, LANES)], (head + 1) % 2, lane
        )
        scores = jnp.where(allowed, dot_nt(dup_ref[group], query), neg_fill)
        probs = jnp.exp(scores - log_ref[half, pl.ds(head, 1), rows])
        grad_probs = dot_nt(dup_ref[3 + group], upstream)
        inner = jnp.sum(probs * grad_probs, axis=0, keepdims=True)
        grad_scores = (probs * (grad_probs - inner)).astype(bf16)
        acc_ref[3 + group] += dot_nn(probs.astype(bf16), upstream)
        acc_ref[group] += dot_nn(grad_scores, query)
        grad_query = dot_nn(flip_ref[group], grad_scores).T
        if head % 2 == 1 or head == 8:
            if head == 8:
                tile = jnp.where(lane < HEAD, grad_query, 0.0)
            else:
                tile = jnp.where(lane < HEAD, previous, grad_query)
            tile = turn_back(tile * HEAD ** (-0.5), cos_ref[rows, :], sin_ref[rows, :], lower)
            out_ref[half, rows, pl.ds((3 + head // 2) * LANES, LANES)] = tile.astype(bf16)
        previous = grad_query


def join_groups(acc_ref, out_ref, half):
    lane = lane_of((acc_ref.shape[1], LANES))
    for tile in range(3):
        low, high = acc_ref[2 * tile], acc_ref[2 * tile + 1]
        low = low + pltpu.roll(low, HEAD, 1)
        high = high + pltpu.roll(high, HEAD, 1)
        out_ref[half, :, pl.ds(tile * LANES, LANES)] = jnp.where(lane < HEAD, low, high)


def attend_back_kernel(
    block, y_ref, kv_ref, first_ref, last_ref, log_ref, grad_ref, cos_ref, sin_ref, dq_ref, dkv_ref, dup_ref, flip_ref, acc_ref
):
    load_groups(kv_ref, 0, dup_ref, flip_ref)
    acc_ref[...] = jnp.zeros_like(acc_ref)

    def rows_of(step, carry):
        attend_back_rows(
            0, step, block, y_ref, dup_ref, flip_ref, first_ref, last_ref, log_ref, grad_ref, cos_ref, sin_ref, dq_ref, acc_ref
        )
        return carry

    lax.fori_loop(0, y_ref.shape[1] // block, rows_of, 0)
    join_groups(acc_ref, dkv_ref, 0)


def full_spec(shape):
    return pl.BlockSpec(shape, lambda i: (0,) * len(shape))


def half_spec(shape):
    return pl.BlockSpec((1,) + shape[1:], lambda i: (i,) + (0,) * (len(shape) - 1))


def params():
    return pltpu.CompilerParams(vmem_limit_bytes=VMEM_BYTES)


def project(layer_input, gain, first_pack, cosine, sine):
    tokens, width = layer_input.shape
    vm = pl.BlockSpec(memory_space=pltpu.VMEM)
    return pl.pallas_call(
        project_kernel,
        grid=(1,),
        out_shape=(
            jax.ShapeDtypeStruct((tokens, width), bf16),
            jax.ShapeDtypeStruct((2, tokens, 8 * LANES), bf16),
        ),
        in_specs=[
            full_spec((tokens, width)),
            full_spec((1, width)),
            full_spec((2, width, 8 * LANES)),
            full_spec((tokens, LANES)),
            full_spec((tokens, LANES)),
        ],
        out_specs=(full_spec((tokens, width)), full_spec((2, tokens, 8 * LANES))),
        compiler_params=params(),
        name="project",
    )(layer_input, gain, first_pack, cosine, sine)


def attend(y, kv, first, last):
    tokens, keys = y.shape[1], kv.shape[1]
    block = min(256, tokens)
    return pl.pallas_call(
        lambda *refs: attend_kernel(block, *refs),
        grid=(2,),
        out_shape=(
            jax.ShapeDtypeStruct((2, tokens, 5 * LANES), bf16),
            jax.ShapeDtypeStruct((2, 16, tokens), f32),
        ),
        in_specs=[half_spec(y.shape), half_spec(kv.shape), full_spec((1, tokens)), full_spec((1, tokens))],
        out_specs=(half_spec((2, tokens, 5 * LANES)), half_spec((2, 16, tokens))),
        scratch_shapes=[pltpu.VMEM((6, keys, LANES), bf16), pltpu.VMEM((6, LANES, keys), bf16)],
        compiler_params=params(),
        name="attend",
    )(y, kv, first, last)


def attend_back(y, kv, first, last, logs, grad, cosine, sine):
    tokens, keys = y.shape[1], kv.shape[1]
    block = min(256, tokens)
    return pl.pallas_call(
        lambda *refs: attend_back_kernel(block, *refs),
        grid=(2,),
        out_shape=(
            jax.ShapeDtypeStruct((2, tokens, 8 * LANES), bf16),
            jax.ShapeDtypeStruct((2, keys, 3 * LANES), f32),
        ),
        in_specs=[
            half_spec(y.shape),
            half_spec(kv.shape),
            full_spec((1, tokens)),
            full_spec((1, tokens)),
            half_spec(logs.shape),
            half_spec(grad.shape),
            full_spec((tokens, LANES)),
            full_spec((tokens, LANES)),
        ],
        out_specs=(half_spec((2, tokens, 8 * LANES)), half_spec((2, keys, 3 * LANES))),
        scratch_shapes=[
            pltpu.VMEM((6, keys, LANES), bf16),
            pltpu.VMEM((6, LANES, keys), bf16),
            pltpu.VMEM((6, keys, LANES), f32),
        ],
        compiler_params=params(),
        name="attend_back",
    )(y, kv, first, last, logs, grad, cosine, sine)


def rope_frequency():
    lane_index = (jnp.arange(LANES, dtype=jnp.int32) % (HEAD // 2)).astype(f32)
    return jnp.exp(lane_index * (-2.0 * math.log(rope_base) / HEAD))


def shards(
    layer_input,
    attn_gain,
    mlp_gain,
    query_weight,
    key_weight,
    value_weight,
    out_weight,
    gate_weight,
    up_weight,
    down_weight,
    seq_ids,
    block_ends,
    grad_output,
):
    tokens, width = layer_input.shape
    span = seq_ids.shape[0]
    start = lax.axis_index("col") * tokens
    gains = jnp.stack([attn_gain, mlp_gain]).astype(f32)
    weights = (query_weight, key_weight, value_weight, out_weight, gate_weight, up_weight, down_weight)
    if special():
        mine = jnp.concatenate([key_weight, value_weight, query_weight, out_weight.T], axis=1)
        packs, kept = forward_special(
            layer_input,
            gains,
            rope_frequency()[None, :],
            seq_ids[None, :],
            block_ends[None, :],
            (mine, gate_weight, up_weight, down_weight.T),
        )
        grad_input, gain_sums, weight_sums = backward_special(
            grad_output, layer_input, gains, *kept[10:], packs, kept[:9]
        )
        return (kept[9], grad_input, gain_sums[0], gain_sums[1]) + tuple(weight_sums)
    own = layer_input.astype(f32)
    gain_one, gain_two = gains[:1], gains[1:]
    index = start + jnp.arange(tokens, dtype=jnp.int32)
    length = jnp.sum(1 - (seq_ids & 1))
    own_first = jnp.where(index < length, 0, length)
    own_last = lax.dynamic_slice_in_dim(block_ends, start, tokens) - lax.axis_index("row") * span
    angles = (index - own_first).astype(f32)[:, None] * rope_frequency()[None, :]
    cosine, sine = jnp.cos(angles), jnp.sin(angles)
    own_first, own_last = own_first[None, :], own_last[None, :]
    pack_first, pack_gate, pack_up, pack_down = gather_any(weights)
    attn_in, y = project(layer_input, gain_one, pack_first, cosine, sine)
    kv = lax.all_gather(y[:, :, : 3 * LANES], "col", axis=1, tiled=True)
    mix, logs = attend(y, kv, own_first, own_last)
    pack_out = pack_first[:, :, 7 * LANES :]
    branch = jnp.einsum("htq,hdq->td", mix, pack_out, preferred_element_type=f32)
    residual = own + branch
    inv_two = lax.rsqrt(jnp.mean(residual * residual, axis=1, keepdims=True) + eps)
    normed_two = residual * inv_two
    mlp_in = (normed_two * gain_two).astype(bf16)
    gate_act = jnp.einsum("td,hdf->htf", mlp_in, pack_gate, preferred_element_type=f32)
    up_act = jnp.einsum("td,hdf->htf", mlp_in, pack_up, preferred_element_type=f32)
    hidden = (jax.nn.silu(gate_act) * up_act).astype(bf16)
    layer_output = (
        residual + jnp.einsum("htf,hdf->td", hidden, pack_down, preferred_element_type=f32)
    ).astype(bf16)
    grad_down = jnp.einsum("td,htf->hdf", grad_output, hidden, preferred_element_type=f32).astype(bf16)
    grad_hidden = jnp.einsum("td,hdf->htf", grad_output, pack_down, preferred_element_type=f32)
    sigmoid = jax.nn.sigmoid(gate_act)
    grad_gate_act = (grad_hidden * up_act * sigmoid * (1.0 + gate_act * (1.0 - sigmoid))).astype(bf16)
    grad_up_act = (grad_hidden * gate_act * sigmoid).astype(bf16)
    grad_gate = jnp.einsum("td,htf->hdf", mlp_in, grad_gate_act, preferred_element_type=f32).astype(bf16)
    grad_up = jnp.einsum("td,htf->hdf", mlp_in, grad_up_act, preferred_element_type=f32).astype(bf16)
    grad_mlp_in = jnp.einsum(
        "htf,hdf->td", grad_gate_act, pack_gate, preferred_element_type=f32
    ) + jnp.einsum("htf,hdf->td", grad_up_act, pack_up, preferred_element_type=f32)
    scaled_two = grad_mlp_in * gain_two
    inner_two = jnp.mean(scaled_two * normed_two, axis=1, keepdims=True)
    grad_residual = grad_output.astype(f32) + inv_two * (scaled_two - normed_two * inner_two)
    grad_mlp_gain = jnp.sum(grad_mlp_in * normed_two, axis=0)
    grad_branch = grad_residual.astype(bf16)
    grad_mixture = jnp.einsum("td,hdq->htq", grad_branch, pack_out, preferred_element_type=f32).astype(bf16)
    grad_q, grad_kv = attend_back(y, kv, own_first, own_last, logs, grad_mixture, cosine, sine)
    grad_kv = lax.psum_scatter(grad_kv, "col", scatter_dimension=1, tiled=True)
    key_cos, key_sin = jnp.tile(cosine, (1, 3)), jnp.tile(sine, (1, 3))
    lane = jnp.arange(3 * LANES, dtype=jnp.int32)
    is_key = lane < 3 * HEAD
    scaled = grad_kv * key_sin
    turned = jnp.where(
        lane % HEAD < HEAD // 2, -jnp.roll(scaled, -(HEAD // 2), axis=2), jnp.roll(scaled, HEAD // 2, axis=2)
    )
    grad_kv = jnp.where(is_key, grad_kv * key_cos - turned, grad_kv).astype(bf16)
    grad_y = jnp.concatenate([grad_kv, grad_q[:, :, 3 * LANES :]], axis=2)
    grad_proj = jnp.einsum("td,htf->hdf", attn_in, grad_y, preferred_element_type=f32)
    grad_out = jnp.einsum("td,htq->hdq", grad_branch, mix, preferred_element_type=f32)
    grad_first = jnp.concatenate(
        [
            grad_proj[:, :, : 7 * LANES],
            grad_proj[:, :, 7 * LANES :] + grad_out[:, :, :LANES],
            grad_out[:, :, LANES:],
        ],
        axis=2,
    ).astype(bf16)
    grad_attn_in = jnp.einsum(
        "htf,hdf->td", grad_y, pack_first[:, :, : 8 * LANES], preferred_element_type=f32
    )
    inv_one = lax.rsqrt(jnp.mean(own * own, axis=1, keepdims=True) + eps)
    normed_one = own * inv_one
    scaled_one = grad_attn_in * gain_one
    inner_one = jnp.mean(scaled_one * normed_one, axis=1, keepdims=True)
    grad_input = (grad_residual + inv_one * (scaled_one - normed_one * inner_one)).astype(bf16)
    grad_attn_gain = jnp.sum(grad_attn_in * normed_one, axis=0)
    gain_sums, weight_sums = scatter_any(
        (grad_first, grad_gate, grad_up, grad_down), jnp.stack([grad_attn_gain, grad_mlp_gain])
    )
    return (layer_output, grad_input, gain_sums[0], gain_sums[1]) + tuple(weight_sums)


def solution(mesh):
    tokens_spec = P(("row", "col"), None)
    in_specs = (
        tokens_spec,
        P(),
        P(),
        P("row", "col"),
        P("row", "col"),
        P("row", "col"),
        P("col", "row"),
        P("row", "col"),
        P("row", "col"),
        P("col", "row"),
        P("row"),
        P("row"),
        tokens_spec,
    )
    out_specs = (
        tokens_spec,
        tokens_spec,
        P(),
        P(),
        P("row", "col"),
        P("row", "col"),
        P("row", "col"),
        P("col", "row"),
        P("row", "col"),
        P("row", "col"),
        P("col", "row"),
    )
    return jax.shard_map(shards, mesh=mesh, in_specs=in_specs, out_specs=out_specs, check_vma=False)
```

```python
import math

import jax
import jax.numpy as jnp
from jax import lax
from jax.experimental import pallas as pl
from jax.experimental.pallas import tpu as pltpu
from jax.sharding import PartitionSpec as P

HEAD = 64
LANES = 128
eps = 1e-05
rope_base = 10000.0
neg_fill = -1e30
f32 = jnp.float32
bf16 = jnp.bfloat16
VMEM_BYTES = 62 * 1024 * 1024


def dot_nn(a, b):
    return lax.dot_general(a, b, (((1,), (0,)), ((), ())), preferred_element_type=f32)


def dot_nt(a, b):
    return lax.dot_general(a, b, (((1,), (1,)), ((), ())), preferred_element_type=f32)


def halves(values):
    rows, cols = values.shape
    return jnp.transpose(values.reshape(rows, 2, cols // 2), (1, 0, 2))


def whole(values):
    two, rows, cols = values.shape
    return jnp.transpose(values, (1, 0, 2)).reshape(rows, two * cols)


def gather_any(weights):
    query, key, value, out, gate, up, down = weights

    def both(weight, row_axis):
        part = lax.all_gather(weight, "row", axis=row_axis, tiled=True)
        return lax.all_gather(part, "col", axis=1 - row_axis, tiled=True)

    mix = [halves(both(key, 0)), halves(both(value, 0)), halves(both(query, 0)), halves(both(out, 1).T)]
    return [
        jnp.concatenate(mix, axis=2),
        halves(both(gate, 0)),
        halves(both(up, 0)),
        halves(both(down, 1).T),
    ]


def scatter_any(grads, gains):
    first, gate, up, down = [grad.astype(f32) for grad in grads]
    kv = first.shape[2] // 8
    key, value, query, out = (
        whole(first[:, :, :kv]),
        whole(first[:, :, kv : 2 * kv]),
        whole(first[:, :, 2 * kv : 5 * kv]),
        whole(first[:, :, 5 * kv :]).T,
    )

    def both(grad, row_axis):
        part = lax.psum_scatter(grad, "row", scatter_dimension=row_axis, tiled=True)
        return lax.psum_scatter(part, "col", scatter_dimension=1 - row_axis, tiled=True)

    return (
        lax.psum(gains, ("row", "col")),
        (
            both(query, 0),
            both(key, 0),
            both(value, 0),
            both(out, 1),
            both(whole(gate), 0),
            both(whole(up), 0),
            both(whole(down).T, 1),
        ),
    )


PACKS = 4
MESH = pl.DeviceIdType.MESH


class Sides:
    def __init__(self, at, core0, core1):
        if core0 == core1:
            along_x = twin_x = int(core0 == "x")
        else:
            along_x = at.c if core0 == "y" else 1 - at.c
            twin_x = 1 - along_x
        self.near_x, self.near_y, self.far_x, self.far_y = self.spots(at, along_x)
        self.near = at.device(self.near_x, at.z, self.near_y, at.c)
        self.far = at.device(self.far_x, at.z, self.far_y, at.c)
        twin = self.spots(at, twin_x)
        rest = (1 - at.x, 1 - at.y)
        self.order = [(self.far_x, self.far_y), rest, (self.near_x, self.near_y), (at.x, at.y)]
        self.twin_order = [twin[2:], rest, twin[:2], (at.x, at.y)]

    @staticmethod
    def spots(at, along_x):
        x, y = at.x, at.y
        near = (x + along_x * (1 - 2 * x), y + (1 - along_x) * (1 - 2 * y))
        far = (x + (1 - along_x) * (1 - 2 * x), y + along_x * (1 - 2 * y))
        return near + far


class Place:
    def __init__(self):
        row, x = lax.axis_index("row"), lax.axis_index("col")
        z, y, c = row // 4, (row // 2) % 2, row % 2
        self.x, self.z, self.y, self.c = x, z, y, c
        self.xa, self.ya = jnp.where(c == 0, 1 - x, x), jnp.where(c == 0, y, 1 - y)
        self.xb, self.yb = jnp.where(c == 0, x, 1 - x), jnp.where(c == 0, 1 - y, y)
        self.others = [(z + k) % 4 for k in (1, 2, 3)]
        self.line = [self.device(x, other, y, c) for other in self.others]
        self.near = self.device(self.xa, z, self.ya, c)
        self.far = self.device(self.xb, z, self.yb, c)
        self.twin = self.device(x, z, y, 1 - c)
        self.cross = self.device(1 - x, z, y, c)
        self.corner = self.device(1 - x, z, 1 - y, c)

    @staticmethod
    def device(x, z, y, c):
        return ((z * 2 + y) * 2 + c, x)

    def greet(self):
        barrier = pltpu.get_barrier_semaphore()
        peers = self.line + [self.near, self.far, self.corner, self.twin]
        for peer in peers:
            pl.semaphore_signal(barrier, inc=1, device_id=peer, device_id_type=MESH)
        pl.semaphore_wait(barrier, len(peers))


def remote(src, dst, send, recv, device):
    return pltpu.make_async_remote_copy(
        src_ref=src, dst_ref=dst, send_sem=send, recv_sem=recv, device_id=device, device_id_type=MESH
    )


GATHER_PLAN = [
    (0, 0, 512, 0, "x", "y"),
    (0, 512, 512, 0, "y", "x"),
    (0, 1024, 512, 0, "x", "x"),
    (1, 0, 768, 0, "y", "y"),
    (2, 0, 768, 1, "x", "x"),
    (1, 768, 768, 0, "y", "x"),
    (2, 768, 768, 0, "x", "y"),
    (3, 0, 768, 1, "x", "y"),
    (3, 768, 768, 1, "x", "y"),
]
FORWARD_ORDER = [
    ("B", 0), ("B", 1), "norm", ("F", 0), ("B", 2), ("F", 1), ("B", 3), ("S", 0), ("F", 2), ("B", 4),
    ("S", 1), ("T", 0), ("F", 3), ("B", 5), ("S", 2), ("T", 1), "kv", ("F", 4), ("B", 6), "q", ("T", 2),
    ("S", 3), ("F", 5), ("B", 7), "a0", ("S", 4), "a1", ("F", 6), ("B", 8), "a2", ("F", 7), ("S", 5),
    ("T", 3), ("T", 4), "a3", "br", ("S", 7), ("S", 6), ("F", 8), "h0", ("T", 5), ("S", 8), ("T", 6),
    ("T", 7), "h1", ("T", 8), "o0", "o1",
]
SCATTER_PLAN = [
    (3, 0, 1, "y", "x"),
    (1, 0, 0, "x", "y"),
    (2, 0, 0, "y", "x"),
    (3, 1, 1, "y", "x"),
    (1, 1, 0, "x", "x"),
    (2, 1, 0, "y", "y"),
    (0, 1, 0, "y", "x"),
    (0, 0, 0, "x", "y"),
]
BACKWARD_ORDER = [
    "ld", "w0", ("B", 0), "d0", "w1", ("B", 1), ("1", 0), "w2", "m0", ("1", 1), ("B", 2), "w3", ("B", 3),
    ("1", 2), "d1", "w4", "w5", ("B", 5), "m1", ("2", 1), ("1", 3), ("B", 4), "norm", ("1", 5), ("2", 0),
    "mx", "a0", ("1", 4), ("2", 3), ("3", 0), "a1", "a2", ("2", 2), ("3", 1), ("2", 5), "a3", ("3", 3), "g1",
    ("B", 6), ("4", 1), ("3", 2), ("3", 5), ("2", 4), ("1", 6), "kvw", "g0", "in", ("4", 0), ("B", 7),
    ("3", 4), ("2", 6), ("4", 3), ("1", 7), ("4", 2), ("3", 6), ("4", 4), ("2", 7), ("4", 5), ("3", 7),
    ("4", 6), ("4", 7),
]
RING = 6


class Gather:
    def __init__(self, at, plan, own_refs, out_refs, copied, sent, came):
        x, y, z = at.x, at.y, at.z
        self.plan, self.arrived = plan, set()
        size = own_refs[0].shape[0]
        rows = pl.ds(pl.multiple_of(at.c * size, 8), size)
        self.steps = []
        for i, (pack, lane, lanes, kind, *axes) in enumerate(plan):
            sides = Sides(at, *axes)
            cols = pl.ds(lane, lanes)
            own = own_refs[pack].at[:, cols]

            def one(xx, yy):
                return out_refs[pack].at[xx, z, yy, rows, cols]

            def line(xx, yy, slot, device):
                ref = out_refs[pack].at[xx, :, yy, rows, cols]
                return remote(ref, ref, sent.at[i, slot], came.at[i, slot], device)

            step = {"kind": kind, "keep": pltpu.make_async_copy(own, one(x, y), copied.at[i])}
            step["line"] = [remote(own, one(x, y), sent.at[i, k], came.at[i, k], at.line[k]) for k in range(3)]
            if kind == 0:
                step["near"] = line(x, y, 3, sides.near)
            else:
                step["near"] = remote(own, one(x, y), sent.at[i, 3], came.at[i, 3], sides.near)
                step["more"] = [
                    remote(
                        one(sides.near_x, sides.near_y),
                        one(sides.near_x, sides.near_y),
                        sent.at[i, 4 + k],
                        came.at[i, 4 + k],
                        at.line[k],
                    )
                    for k in range(3)
                ]
            step["far"] = [line(x, y, 7, sides.far), line(sides.near_x, sides.near_y, 8, sides.far)]
            step["twin"] = [
                line(xx, yy, 9 + j, at.twin)
                for j, (xx, yy) in enumerate(
                    [(x, y), (sides.near_x, sides.near_y), (sides.far_x, sides.far_y), (1 - x, 1 - y)]
                )
            ]
            self.steps.append(step)

    def begin(self, i):
        if 0 <= i < len(self.steps):
            self.steps[i]["keep"].start()
            for copy in self.steps[i]["line"]:
                copy.start()
            if self.steps[i]["kind"] == 1:
                self.steps[i]["near"].start()

    def first(self, i):
        if 0 <= i < len(self.steps):
            step = self.steps[i]
            if step["kind"] == 1:
                step["near"].wait_recv()
                for copy in step["more"]:
                    copy.start()
            for copy in step["line"]:
                copy.wait_recv()
            step["keep"].wait()
            if step["kind"] == 0:
                step["near"].start()
            step["far"][0].start()
            step["twin"][0].start()

    def second(self, i):
        if 0 <= i < len(self.steps):
            step = self.steps[i]
            for copy in [step["near"]] if step["kind"] == 0 else step["more"]:
                copy.wait_recv()
            step["far"][1].start()
            step["twin"][1].start()

    def third(self, i):
        if 0 <= i < len(self.steps):
            step = self.steps[i]
            for j in range(2):
                step["far"][j].wait_recv()
                step["twin"][2 + j].start()

    def arrive(self, *chunks):
        for i in chunks:
            if i not in self.arrived:
                self.arrived.add(i)
                for copy in self.steps[i]["twin"]:
                    copy.wait_recv()

    def arrive_lanes(self, pack, low, high):
        for i, (held, lane, lanes, *_) in enumerate(self.plan):
            if held == pack and lane < high and lane + lanes > low:
                self.arrive(i)

    def run(self, moves):
        for name, i in moves:
            {"B": self.begin, "F": self.first, "S": self.second, "T": self.third}[name](i)

    def finish(self):
        for step in self.steps:
            for copy in step["line"] + step.get("more", []) + [step["near"]] + step["far"] + step["twin"]:
                copy.wait_send()


def forward_kernel(plan, *refs):
    x_ref, gain_ref, frequency_ref, ids_ref, ends_ref = refs[:5]
    own_refs, full_refs = refs[5:9], refs[9:13]
    saved = refs[13:27]
    weights, attn_in, y, kv, dup, flip, mix, logs, residual, mlp_in, acts, hidden, output = refs[27:40]
    cos_ref, sin_ref, first_ref, last_ref = refs[40:44]
    copied, sent, came, loaded, stored, kv_sent, kv_came = refs[44:]
    gain_one_ref, gain_two_ref = gain_ref.at[pl.ds(0, 1)], gain_ref.at[pl.ds(1, 1)]
    at = Place()
    at.greet()
    gather = Gather(at, plan, own_refs, full_refs, copied, sent, came)
    tokens, width = x_ref.shape
    lanes = weights.shape[2]

    def load(pack, cut, slot, k):
        size = lanes // 2
        return [
            pltpu.make_async_copy(
                full_refs[pack].at[half].reshape(width, lanes).at[:, pl.ds(cut * size, size)],
                weights.at[slot, :, pl.ds(half * size, size)],
                loaded.at[k, half],
            )
            for half in range(2)
        ]

    def load_first(half, lane, size, k):
        part = pl.ds(lane, size)
        return pltpu.make_async_copy(
            full_refs[0].at[half].reshape(width, lanes).at[:, part], weights.at[half, :, part], loaded.at[k, half]
        )

    project_loads = [load_first(half, 0, 8 * LANES, 0) for half in range(2)]
    out_loads = [load_first(half, 8 * LANES, lanes - 8 * LANES, 1) for half in range(2)]
    gate_loads = [load(1, 0, 2, 2) + load(2, 0, 3, 3), load(1, 1, 0, 4) + load(2, 1, 1, 5)]
    down_loads = [load(3, 0, 2, 6), load(3, 1, 3, 7)]

    def save(k, ref):
        copy = pltpu.make_async_copy(ref, saved[k], stored.at[k])
        copy.start()
        return copy

    mine = pl.ds(pl.multiple_of(at.x * tokens, tokens), tokens)
    exchanges = [
        remote(kv.at[half, mine, :], kv.at[half, mine, :], kv_sent.at[half], kv_came.at[half], at.cross)
        for half in range(2)
    ]
    block = 256
    steps = tokens // block
    span = pl.ds(7 * LANES, 5 * LANES)
    size = lanes // 2
    saves = {}

    def norm():
        length = jnp.sum(1 - (ids_ref[...] & 1), axis=1, keepdims=True)
        index = at.x * tokens + lax.broadcasted_iota(jnp.int32, (1, tokens), 1)
        first_ref[...] = jnp.where(index < length, 0, length)
        row_start = lax.axis_index("row") * ids_ref.shape[1]
        last_ref[...] = ends_ref[:, pl.ds(pl.multiple_of(at.x * tokens, LANES), tokens)] - row_start
        index = at.x * tokens + lax.broadcasted_iota(jnp.int32, (tokens, LANES), 0)
        position = (index - jnp.where(index < length, 0, length)).astype(f32)
        angles = position * frequency_ref[...]
        cos_ref[...] = jnp.cos(angles)
        sin_ref[...] = jnp.sin(angles)
        for k, ref in enumerate((cos_ref, sin_ref, first_ref, last_ref)):
            saves[10 + k] = save(10 + k, ref)
        values = x_ref[...].astype(f32)
        inverse = lax.rsqrt(jnp.mean(values * values, axis=1, keepdims=True) + eps)
        attn_in[...] = (values * inverse * gain_one_ref[...]).astype(bf16)
        saves[0] = save(0, attn_in)

    def keys():
        gather.arrive_lanes(0, 0, 8 * LANES)
        start(project_loads)
        for half in range(2):
            project_loads[half].wait()
            project_tiles(half, range(2), attn_in, weights, cos_ref, sin_ref, y)
            kv[half, mine, :] = y[half, :, : 3 * LANES]
            exchanges[half].start()

    def queries():
        for half in range(2):
            project_tiles(half, range(2, 4), attn_in, weights, cos_ref, sin_ref, y)
        saves[1] = save(1, y)

    def attend_all(moves):
        def rows_of(i, carry):
            half = i // steps
            for k in range(2):

                @pl.when(i == k * steps)
                def _(k=k):
                    exchanges[k].wait()

            @pl.when(i % steps == 0)
            def _():
                load_groups(kv, half, dup, flip)

            attend_rows(half, i % steps, block, y, dup, flip, first_ref, last_ref, mix, logs)
            for k, part in enumerate(moves):
                if part:

                    @pl.when(i == k * steps // 2)
                    def _(part=part):
                        gather.run(part)

            return carry

        lax.fori_loop(0, 2 * steps, rows_of, 0)
        saves[2], saves[3], saves[4] = save(2, kv), save(3, mix), save(4, logs)

    def branch():
        gather.arrive_lanes(0, 8 * LANES, lanes)
        start(out_loads)
        wait(out_loads)

        def rows_of(i, carry):
            rows = pl.ds(pl.multiple_of(i * 256, 256), 256)
            total = x_ref[rows, :].astype(f32)
            for half in range(2):
                total = total + dot_nt(mix[half, rows, :], weights[half, :, span])
            residual[rows, :] = total
            inverse = lax.rsqrt(jnp.mean(total * total, axis=1, keepdims=True) + eps)
            mlp_in[rows, :] = (total * inverse * gain_two_ref[...]).astype(bf16)
            return carry

        lax.fori_loop(0, tokens // 256, rows_of, 0)
        saves[5], saves[6] = save(5, residual), save(6, mlp_in)

    def hide(cut):
        gather.arrive_lanes(1, cut * size, (cut + 1) * size)
        gather.arrive_lanes(2, cut * size, (cut + 1) * size)
        start(gate_loads[cut])
        wait(gate_loads[cut])
        slot = 2 - 2 * cut

        def tile_of(i, carry):
            half, tile = i // (size // 256), i % (size // 256)
            cols = pl.ds(pl.multiple_of(i * 256, 256), 256)
            into = pl.ds(pl.multiple_of(cut * size + tile * 256, 256), 256)
            gate = dot_nn(mlp_in[...], weights[slot, :, cols])
            up = dot_nn(mlp_in[...], weights[slot + 1, :, cols])
            acts[half, 0, :, into] = gate
            acts[half, 1, :, into] = up
            hidden[half, :, into] = (gate * jax.nn.sigmoid(gate) * up).astype(bf16)
            return carry

        lax.fori_loop(0, lanes // 256, tile_of, 0)
        if cut == 1:
            saves[7], saves[8] = save(7, acts), save(8, hidden)

    def finish_rows(cut):
        gather.arrive_lanes(3, cut * size, (cut + 1) * size)
        start(down_loads[cut])
        wait(down_loads[cut])
        if cut == 0:
            saves.pop(5).wait()

        def rows_of(i, carry):
            rows = pl.ds(pl.multiple_of(i * 256, 256), 256)
            total = residual[rows, :]
            for half in range(2):
                total = total + dot_nt(
                    hidden[half, rows, pl.ds(cut * size, size)], weights[2 + cut, :, pl.ds(half * size, size)]
                )
            if cut == 0:
                residual[rows, :] = total
            else:
                output[rows, :] = total.astype(bf16)
            return carry

        lax.fori_loop(0, tokens // 256, rows_of, 0)
        if cut == 1:
            saves[9] = save(9, output)

    work = {
        "norm": norm,
        "kv": keys,
        "q": queries,
        "br": branch,
        "h0": lambda: hide(0),
        "h1": lambda: hide(1),
        "o0": lambda: finish_rows(0),
        "o1": lambda: finish_rows(1),
    }
    plain, looped = split_schedule(FORWARD_ORDER)
    for entry in plain:
        if isinstance(entry, tuple):
            gather.run([entry])
        elif entry == "a":
            attend_all(looped)
        else:
            work[entry]()
    gather.finish()
    for copy in saves.values():
        copy.wait()


def forward_special(layer_input, gains, frequency, ids, ends, packs):
    plan = GATHER_PLAN
    tokens, width = layer_input.shape
    rows, lanes = packs[0].shape
    keys = 2 * tokens
    dma, vmem = pltpu.SemaphoreType.DMA, pltpu.VMEM
    anywhere = pl.BlockSpec(memory_space=pl.ANY)
    near = pl.BlockSpec(memory_space=pltpu.VMEM)
    saved = [
        ((tokens, width), bf16),
        ((2, tokens, 8 * LANES), bf16),
        ((2, keys, 3 * LANES), bf16),
        ((2, tokens, 5 * LANES), bf16),
        ((2, 16, tokens), f32),
        ((tokens, width), f32),
        ((tokens, width), bf16),
        ((2, 2, tokens, lanes), f32),
        ((2, tokens, lanes), bf16),
        ((tokens, width), bf16),
        ((tokens, LANES), f32),
        ((tokens, LANES), f32),
        ((1, tokens), jnp.int32),
        ((1, tokens), jnp.int32),
    ]
    full = [((2, 4, 2, 2 * rows, lanes), bf16)] * PACKS
    count = len(plan)
    outs = pl.pallas_call(
        lambda *refs: forward_kernel(plan, *refs),
        out_shape=[jax.ShapeDtypeStruct(*shape) for shape in full + saved],
        in_specs=[near] * 5 + [anywhere] * PACKS,
        out_specs=[anywhere] * (PACKS + len(saved)),
        scratch_shapes=[
            vmem((4, width, lanes), bf16),
            vmem(*saved[0]),
            vmem(*saved[1]),
            vmem(*saved[2]),
            vmem((6, keys, LANES), bf16),
            vmem((6, LANES, keys), bf16),
            vmem(*saved[3]),
            vmem(*saved[4]),
            vmem(*saved[5]),
            vmem(*saved[6]),
            vmem(*saved[7]),
            vmem(*saved[8]),
            vmem(*saved[9]),
            vmem(*saved[10]),
            vmem(*saved[11]),
            vmem(*saved[12]),
            vmem(*saved[13]),
            dma((count,)),
            dma((count, 13)),
            dma((count, 13)),
            dma((8, 2)),
            dma((len(saved),)),
            dma((2,)),
            dma((2,)),
        ],
        compiler_params=pltpu.CompilerParams(
            collective_id=1, has_side_effects=True, vmem_limit_bytes=VMEM_BYTES
        ),
        name="forward",
    )(layer_input, gains, frequency, ids, ends, *packs)
    return [part.reshape(2, 16 * rows, lanes) for part in outs[:PACKS]], outs[PACKS:]


def split_schedule(order):
    plain, looped, part = [], [[] for _ in range(4)], None
    for entry in order:
        if isinstance(entry, str) and entry[0] == "a":
            part = int(entry[1])
            if part == 0:
                plain.append("a")
        elif isinstance(entry, tuple) and part is not None and part < 4:
            looped[part].append(entry)
        else:
            part = None
            plain.append(entry)
    return plain, looped


def start(copies):
    for copy in copies:
        copy.start()


def wait(copies):
    for copy in copies:
        copy.wait()


class Scatter:
    def __init__(self, at, grad_ref, parts, sums, temps, sems, out_ref, pushes):
        self.pushes, self.ready = pushes, set()
        self.at, self.grad, self.sums, self.temps = at, grad_ref, sums, temps
        self.from_twin, self.from_far, self.from_near, self.from_line = parts
        self.sent, self.came, self.loaded, self.stored = sems
        self.out_ref = out_ref
        to_far, to_near, to_line, result = sums
        self.steps = []
        for i, (pack, cut, kind, *axes) in enumerate(SCATTER_PLAN):
            sides = Sides(at, *axes)
            lanes = result.shape[2]

            def send(src, dst, slot, device, i=i):
                return remote(src, dst, self.sent.at[i, slot], self.came.at[i, slot], device)

            self.steps.append(
                {
                    "twin": [
                        send(self.line(i, sides.twin_order[j], 1 - at.c), self.from_twin.at[i, j], j, at.twin)
                        for j in range(4)
                    ],
                    "far": [
                        send(to_far.at[i % RING, j], self.from_far.at[i, j], 4 + j, sides.far) for j in range(2)
                    ],
                    "kind": kind,
                    "near": (
                        send(to_near.at[i % RING], self.from_near.at[i], 6, sides.near)
                        if kind == 0
                        else send(to_near.at[i % RING, at.z], self.from_near.at[i, 3], 6, sides.near)
                    ),
                    "more": [
                        send(to_near.at[i % RING, at.others[k]], self.from_near.at[i, k], 10 + k, at.line[k])
                        for k in range(3 * kind)
                    ],
                    "own": [self.line(i, sides.order[j], at.c) for j in range(4)],
                    "line": [
                        send(to_line.at[i % RING, k], self.from_line.at[i, k], 7 + k, at.line[k])
                        for k in range(3)
                    ],
                    "store": pltpu.make_async_copy(
                        result.at[i % RING], out_ref.at[pack, :, pl.ds(cut * lanes, lanes)], self.stored.at[i]
                    ),
                }
            )

    def line(self, i, place, core):
        size = self.sums[3].shape[1]
        return self.grad.at[i, place[0], :, place[1], pl.ds(pl.multiple_of(core * size, 8), size)]

    def load(self, src, dst, k):
        copy = pltpu.make_async_copy(src, dst, self.loaded.at[k])
        copy.start()
        return copy

    def pushed(self, i):
        if i not in self.ready:
            self.ready.add(i)
            wait(self.pushes(i))

    def begin(self, i):
        self.pushed(i)
        for j in (1, 0, 2, 3):
            self.steps[i]["twin"][j].start()

    def first(self, i):
        step, to_far, temp, slot = self.steps[i], self.sums[0], self.temps[0], i % RING
        self.free(i, lambda old: old["far"])
        copies = []
        for j in (1, 0):
            own = self.load(step["own"][j], to_far.at[slot, j], 2 * j)
            step["twin"][j].wait_recv()
            copies.append((j, [own, self.load(self.from_twin.at[i, j], temp.at[j], 2 * j + 1)]))
        yield
        for j, pair in copies:
            wait(pair)

            def body(q, carry, j=j):
                to_far[slot, j, q] = (to_far[slot, j, q].astype(f32) + temp[j, q].astype(f32)).astype(bf16)
                return carry

            lax.fori_loop(0, 4, body, 0)
            step["far"][j].start()

    def second(self, i):
        step, to_near, temp, slot = self.steps[i], self.sums[1], self.temps[1], i % RING
        self.free(i, lambda old: [old["near"]] + old["more"])
        copies = [self.load(step["own"][2], to_near.at[slot], 4)]
        step["twin"][2].wait_recv()
        copies.append(self.load(self.from_twin.at[i, 2], temp.at[0], 5))
        step["far"][1].wait_recv()
        copies.append(self.load(self.from_far.at[i, 1], temp.at[1], 6))
        yield
        wait(copies)

        def body(q, carry):
            value = to_near[slot, q].astype(f32) + temp[0, q].astype(f32) + temp[1, q].astype(f32)
            to_near[slot, q] = value.astype(bf16)
            return carry

        lax.fori_loop(0, 4, body, 0)
        if step["kind"] == 0:
            step["near"].start()
        start(step["more"])

    def third(self, i):
        step, temp, slot = self.steps[i], self.temps[2], i % RING
        to_near, to_line, result = self.sums[1:]
        early = step["kind"] == 1
        self.free(i, lambda old: old["line"])
        if i >= RING:
            self.steps[slot]["store"].wait()
        copies = [self.load(step["own"][3], temp.at[0], 7)]
        step["twin"][3].wait_recv()
        copies.append(self.load(self.from_twin.at[i, 3], temp.at[1], 8))
        step["far"][0].wait_recv()
        copies.append(self.load(self.from_far.at[i, 0], temp.at[2], 9))
        if early:
            for copy in step["more"]:
                copy.wait_recv()
            copies.append(self.load(self.from_near.at[i, pl.ds(0, 3)], temp.at[3, pl.ds(0, 3)], 10))
        else:
            step["near"].wait_recv()
            copies.append(self.load(self.from_near.at[i], temp.at[3], 10))
        yield
        wait(copies)
        if early:
            value = to_near[slot, self.at.z].astype(f32)
            for k in range(3):
                value = value + temp[3, k].astype(f32)
            to_near[slot, self.at.z] = value.astype(bf16)
            step["near"].start()

        def total(q):
            value = (temp[0, q].astype(f32) + temp[1, q].astype(f32)) + temp[2, q].astype(f32)
            return value if early else value + temp[3, q].astype(f32)

        for k in range(3):
            to_line[slot, k] = total(self.at.others[k]).astype(bf16)
            step["line"][k].start()
        result[slot] = total(self.at.z)

    def fourth(self, i):
        step, temp, result, slot = self.steps[i], self.temps[3], self.sums[3], i % RING
        copies = []
        for k in range(3):
            step["line"][k].wait_recv()
            copies.append(self.load(self.from_line.at[i, k], temp.at[k], 11 + k))
        if step["kind"] == 1:
            step["near"].wait_recv()
            copies.append(self.load(self.from_near.at[i, 3], temp.at[3], 14))
        yield
        wait(copies)
        value = result[slot]
        for k in range(len(copies)):
            value = value + temp[k].astype(f32)
        result[slot] = value
        step["store"].start()

    def run(self, stages):
        names = {"1": self.first, "2": self.second, "3": self.third, "4": self.fourth}
        turn = []

        def flush():
            works = [names[name](i) for name, i in turn]
            for work in works:
                next(work)
            for work in works:
                next(work, None)
            turn.clear()

        for name, i in stages:
            if name == "B":
                self.begin(i)
            else:
                if any(name == held or (name > held and i == j) or i == j + RING for held, j in turn):
                    flush()
                turn.append((name, i))
        flush()

    def free(self, i, sends):
        if i >= RING:
            for copy in sends(self.steps[i - RING]):
                copy.wait_send()

    def finish(self):
        for i, step in enumerate(self.steps):
            for copy in step["twin"]:
                copy.wait_send()
            if i + RING >= len(self.steps):
                for copy in step["far"] + [step["near"]] + step["more"] + step["line"]:
                    copy.wait_send()
                step["store"].wait()


def flip_rows(src, dst):
    for tile in range(src.shape[1] // LANES):
        cols = pl.ds(tile * LANES, LANES)
        dst[cols, :] = src[:, cols].astype(f32).T.astype(bf16)


def backward_kernel(*refs):
    grad_out_ref, x_ref, gain_ref, cos_ref, sin_ref, first_ref, last_ref = refs[:7]
    full_refs, kept = refs[7:11], refs[11:20]
    gain_one_ref, gain_two_ref = gain_ref.at[pl.ds(0, 1)], gain_ref.at[pl.ds(1, 1)]
    attn_in_ref, y_ref, kv_ref, mix_ref, logs_ref, residual_ref, mlp_in_ref, acts_ref, hidden_ref = kept
    sum_ref, grad_in_ref, gain_sum_ref, grad_ref = refs[20:24]
    parts = refs[24:28]
    scratch = refs[28:]
    sums, temps = scratch[:4], scratch[4:8]
    staging, grad_res, branch, kv_out, kv_in, gains = scratch[8:14]
    sems, pulled, pushed, kv_sent, kv_came, gain_sent, gain_came = scratch[14:18], *scratch[18:24]
    at = Place()
    at.greet()
    dma = pltpu.SemaphoreType.DMA
    vmem = pltpu.VMEM
    tokens, width = grad_res.shape
    lanes = hidden_ref.shape[2]
    size = lanes // 2
    tiles = size // 256

    def pull(src, dst, k):
        return pltpu.make_async_copy(src, dst, pulled.at[k])

    def pull_cut(pack, cut, dst, k):
        return [
            pull(
                full_refs[pack].at[half].reshape(width, lanes).at[:, pl.ds(cut * size, size)],
                dst.at[:, pl.ds(half * size, size)],
                k + half,
            )
            for half in range(2)
        ]

    def push(i):
        slot = i % 2
        return [
            pltpu.make_async_copy(
                staging.at[slot, half], grad_ref.at[i, half].reshape(width, size), pushed.at[slot, half]
            )
            for half in range(2)
        ]

    scatter = Scatter(at, grad_ref, parts, sums, temps, sems, sum_ref, push)
    plain, looped = split_schedule(BACKWARD_ORDER)
    first_end, second_end, third_end = (plain.index(name) for name in ("norm", "mx", "in"))

    def follow(entries, work):
        moves = []
        for entry in entries:
            if isinstance(entry, tuple):
                moves.append(entry)
            else:
                scatter.run(moves)
                moves = []
                work[entry]()
        scatter.run(moves)

    def weight_grad(i, left, right):
        def body(k, carry):
            half, cols = k // tiles, pl.ds(pl.multiple_of((k % tiles) * 256, 256), 256)
            staging[i % 2, half, :, cols] = dot_nn(left[...], right[half, :, cols]).astype(bf16)
            return carry

        if i >= 2:
            scatter.pushed(i - 2)
        lax.fori_loop(0, 2 * tiles, body, 0)
        start(push(i))

    def feed_forward(weights, acts, hidden, grad_out, out_turned, in_turned, grad_acts):
        def pulls(cut):
            cols = pl.ds(cut * size, size)
            return {
                "hidden": [pull(hidden_ref.at[:, :, cols], hidden, 0)],
                "down": pull_cut(3, cut, weights.at[0], 1),
                "acts": [pull(acts_ref.at[:, :, :, cols], acts, 3)],
                "gate": pull_cut(1, cut, weights.at[1], 4) + pull_cut(2, cut, weights.at[2], 6),
            }

        cuts = [pulls(0), pulls(1)]
        given = [pull(grad_out_ref, grad_out, 8), pull(mlp_in_ref, branch, 9)]

        def load():
            copies = cuts[0]
            start(given + copies["hidden"] + copies["down"] + copies["acts"] + copies["gate"])
            wait(given)
            flip_rows(grad_out, out_turned)
            flip_rows(branch, in_turned)

        def down_grad(cut):
            wait(cuts[cut]["hidden"])
            weight_grad(3 * cut, out_turned, hidden)
            if cut == 0:
                start(cuts[1]["hidden"])

        def act_grad(cut):
            wait(cuts[cut]["down"] + cuts[cut]["acts"])

            def tile_of(k, carry):
                half, tile = k // tiles, k % tiles
                cols = pl.ds(pl.multiple_of(tile * 256, 256), 256)
                grad = dot_nn(grad_out[...], weights[0, :, pl.ds(pl.multiple_of(k * 256, 256), 256)])
                gate, up = acts[half, 0, :, cols], acts[half, 1, :, cols]
                sigmoid = jax.nn.sigmoid(gate)
                grad_acts[0, half, :, cols] = (
                    grad * up * sigmoid * (1.0 + gate * (1.0 - sigmoid))
                ).astype(bf16)
                grad_acts[1, half, :, cols] = (grad * gate * sigmoid).astype(bf16)
                return carry

            lax.fori_loop(0, 2 * tiles, tile_of, 0)
            if cut == 0:
                start(cuts[1]["down"] + cuts[1]["acts"])

        def input_grad(cut):
            wait(cuts[cut]["gate"])

            def rows_of(k, carry):
                rows = pl.ds(pl.multiple_of(k * 256, 256), 256)
                total = None if cut == 0 else grad_res[rows, :]
                for half in range(2):
                    for part in range(2):
                        term = dot_nt(
                            grad_acts[part, half, rows, :], weights[1 + part, :, pl.ds(half * size, size)]
                        )
                        total = term if total is None else total + term
                grad_res[rows, :] = total
                return carry

            lax.fori_loop(0, tokens // 256, rows_of, 0)
            if cut == 0:
                start(cuts[1]["gate"])

        work = {"ld": load}
        for cut in range(2):
            work["w" + str(3 * cut)] = lambda cut=cut: down_grad(cut)
            work["d" + str(cut)] = lambda cut=cut: act_grad(cut)
            work["w" + str(3 * cut + 1)] = lambda cut=cut: weight_grad(3 * cut + 1, in_turned, grad_acts.at[0])
            work["w" + str(3 * cut + 2)] = lambda cut=cut: weight_grad(3 * cut + 2, in_turned, grad_acts.at[1])
            work["m" + str(cut)] = lambda cut=cut: input_grad(cut)
        follow(plain[:first_end], work)

    pl.run_scoped(
        feed_forward,
        vmem((3, width, lanes), bf16),
        vmem((2, 2, tokens, size), f32),
        vmem((2, tokens, size), bf16),
        vmem((tokens, width), bf16),
        vmem((width, tokens), bf16),
        vmem((width, tokens), bf16),
        vmem((2, 2, tokens, size), bf16),
    )
    def second_norm(residual, grad_out):
        copies = [pull(residual_ref, residual, 0), pull(grad_out_ref, grad_out, 1)]
        start(copies)
        wait(copies)
        gain = gain_two_ref[...]

        def rows_of(k, carry):
            rows = pl.ds(pl.multiple_of(k * 128, 128), 128)
            value, grad = residual[rows, :], grad_res[rows, :]
            inverse = lax.rsqrt(jnp.mean(value * value, axis=1, keepdims=True) + eps)
            normed = value * inverse
            scaled = grad * gain
            inner = jnp.mean(scaled * normed, axis=1, keepdims=True)
            total = grad_out[rows, :].astype(f32) + inverse * (scaled - normed * inner)
            grad_res[rows, :] = total
            branch[rows, :] = total.astype(bf16)
            return carry + jnp.sum(grad * normed, axis=0, keepdims=True)

        gains[0, pl.ds(1, 1), :] = lax.fori_loop(0, tokens // 128, rows_of, jnp.zeros((1, width), f32))

    gains[0] = jnp.zeros(gains.shape[1:], f32)
    pl.run_scoped(second_norm, vmem((tokens, width), f32), vmem((tokens, width), bf16))
    follow(plain[first_end + 1 : second_end], {})

    def attention(weights, y, kv, dup, flip, acc, mix, grad_mix, grad_y, turned, logs, grad_kv, held):
        copies = [
            pull(full_refs[0].at[half].reshape(width, lanes), weights.at[half], half) for half in range(2)
        ] + [
            pull(y_ref, y, 2),
            pull(kv_ref, kv, 3),
            pull(mix_ref, mix, 4),
            pull(logs_ref, logs, 5),
            pull(attn_in_ref, held, 6),
        ]
        def mix_grad():
            start(copies)
            wait(copies[:2])

            def rows_of(k, carry):
                half, rows = k // 2, pl.ds(pl.multiple_of((k % 2) * 256, 256), 256)
                grad_mix[half, rows, :] = dot_nn(
                    branch[rows, :], weights[half, :, pl.ds(7 * LANES, 5 * LANES)]
                ).astype(bf16)
                return carry

            lax.fori_loop(0, 4, rows_of, 0)
            wait(copies[2:])

        mine = pl.ds(pl.multiple_of(at.x * tokens, tokens), tokens)
        other = pl.ds(pl.multiple_of((1 - at.x) * tokens, tokens), tokens)
        block = 256
        steps = tokens // block

        def send_kv(half):
            return remote(kv_out.at[half], kv_in.at[half], kv_sent.at[half], kv_came.at[half], at.cross)

        def attend_back_all():
            def rows_of(i, carry):
                half = i // steps

                @pl.when(i % steps == 0)
                def _():
                    load_groups(kv, half, dup, flip)
                    acc[...] = jnp.zeros_like(acc)

                attend_back_rows(
                    half, i % steps, block, y, dup, flip, first_ref, last_ref, logs, grad_mix, cos_ref, sin_ref, grad_y, acc
                )

                @pl.when(i % steps == steps - 1)
                def _():
                    join_groups(acc, grad_kv, half)
                    kv_out[half] = grad_kv[half, other, :].astype(bf16)

                for k in range(2):

                    @pl.when(i == (k + 1) * steps - 1)
                    def _(k=k):
                        send_kv(k).start()

                for k, part in enumerate(looped):
                    if part:

                        @pl.when(i == k * steps // 2)
                        def _(part=part):
                            scatter.run(part)

                return carry

            lax.fori_loop(0, 2 * steps, rows_of, 0)

        def late_part():
            scatter.pushed(4)
            flip_rows(held, turned.at[0])
            flip_rows(branch, turned.at[1])
            for half in range(2):
                tail = dot_nn(turned[0], grad_y[half, :, pl.ds(6 * LANES, 2 * LANES)])
                head = dot_nn(turned[1], mix[half, :, pl.ds(0, LANES)])
                staging[0, half, :, pl.ds(0, LANES)] = tail[:, :LANES].astype(bf16)
                staging[0, half, :, pl.ds(LANES, LANES)] = (tail[:, LANES:] + head).astype(bf16)
                for k in range(2):
                    staging[0, half, :, pl.ds((2 + 2 * k) * LANES, 2 * LANES)] = dot_nn(
                        turned[1], mix[half, :, pl.ds((1 + 2 * k) * LANES, 2 * LANES)]
                    ).astype(bf16)
            start(push(6))
            load_x.start()

        def join_keys():
            lane = lane_of((tokens, LANES))
            lower = lane % HEAD < HEAD // 2
            for half in range(2):
                send_kv(half).wait()
                for tile in range(3):
                    cols = pl.ds(tile * LANES, LANES)
                    total = grad_kv[half, mine, cols] + kv_in[half, :, cols].astype(f32)
                    if tile < 2:
                        back = turn_back(total, cos_ref[...], sin_ref[...], lower)
                        total = back if tile == 0 else jnp.where(lane < HEAD, back, total)
                    grad_y[half, :, cols] = total.astype(bf16)

        def input_rows():
            load_x.wait()
            gain = gain_one_ref[...]

            def rows_of(k, carry):
                rows = pl.ds(pl.multiple_of(k * 128, 128), 128)
                grad = dot_nt(grad_y[0, rows, :], weights[0, :, pl.ds(0, 8 * LANES)]) + dot_nt(
                    grad_y[1, rows, :], weights[1, :, pl.ds(0, 8 * LANES)]
                )
                value = held[rows, :].astype(f32)
                inverse = lax.rsqrt(jnp.mean(value * value, axis=1, keepdims=True) + eps)
                normed = value * inverse
                scaled = grad * gain
                inner = jnp.mean(scaled * normed, axis=1, keepdims=True)
                branch[rows, :] = (grad_res[rows, :] + inverse * (scaled - normed * inner)).astype(bf16)
                return carry + jnp.sum(grad * normed, axis=0, keepdims=True)

            gains[0, pl.ds(0, 1), :] = lax.fori_loop(0, tokens // 128, rows_of, jnp.zeros((1, width), f32))

        load_x = pull(x_ref, held, 6)
        follow(
            plain[second_end : third_end + 1],
            {
                "mx": mix_grad,
                "a": attend_back_all,
                "g1": late_part,
                "kvw": join_keys,
                "g0": lambda: weight_grad(7, turned.at[0], grad_y),
                "in": input_rows,
            },
        )

    keys = kv_ref.shape[1]
    pl.run_scoped(
        attention,
        vmem((2, width, lanes), bf16),
        vmem(y_ref.shape, bf16),
        vmem(kv_ref.shape, bf16),
        vmem((6, keys, LANES), bf16),
        vmem((6, LANES, keys), bf16),
        vmem((6, keys, LANES), f32),
        vmem(mix_ref.shape, bf16),
        vmem(mix_ref.shape, bf16),
        vmem(y_ref.shape, bf16),
        vmem((2, width, tokens), bf16),
        vmem(logs_ref.shape, f32),
        vmem((2, keys, 3 * LANES), f32),
        vmem((tokens, width), bf16),
    )
    out = pull(branch, grad_in_ref, 0)
    out.start()
    swap = remote(gains.at[0], gains.at[1], gain_sent.at[0], gain_came.at[0], at.twin)
    spot = 2 + 2 * at.x + at.y
    plane = [
        remote(gains.at[spot], gains.at[spot], gain_sent.at[1 + k], gain_came.at[1 + k], peer)
        for k, peer in enumerate([at.near, at.far, at.corner])
    ]
    everyone = [
        remote(gains.at[6 + at.z], gains.at[6 + at.z], gain_sent.at[4 + k], gain_came.at[4 + k], at.line[k])
        for k in range(3)
    ]
    rest = plain[third_end + 1 :]
    swap.start()
    follow(rest[:2], {})
    swap.wait()
    gains[spot] = gains[0] + gains[1]
    start(plane)
    follow(rest[2:10], {})
    wait(plane)
    gains[6 + at.z] = (gains[2] + gains[3]) + (gains[4] + gains[5])
    start(everyone)
    follow(rest[10:], {})
    wait(everyone)
    gain_sum_ref[...] = (gains[6] + gains[7]) + (gains[8] + gains[9])
    out.wait()
    scatter.finish()


def backward_special(grad_output, layer_input, gains, cosine, sine, first, last, packs, kept):
    tokens, width = layer_input.shape
    _, depth, lanes = packs[0].shape
    rows, size = depth // 16, lanes // 2
    count = len(SCATTER_PLAN)
    dma, vmem = pltpu.SemaphoreType.DMA, pltpu.VMEM
    anywhere = pl.BlockSpec(memory_space=pl.ANY)
    near = pl.BlockSpec(memory_space=pltpu.VMEM)
    shape = jax.ShapeDtypeStruct
    outs = pl.pallas_call(
        backward_kernel,
        out_shape=[
            shape((PACKS, rows, lanes), f32),
            shape((tokens, width), bf16),
            shape((8, width), f32),
            shape((count, 2, 4, 2, 2 * rows, size), bf16),
            shape((count, 4, 4, rows, size), bf16),
            shape((count, 2, 4, rows, size), bf16),
            shape((count, 4, rows, size), bf16),
            shape((count, 3, rows, size), bf16),
        ],
        in_specs=[anywhere] * 2 + [near] * 5 + [anywhere] * (PACKS + len(kept)),
        out_specs=[anywhere, anywhere, near] + [anywhere] * 5,
        scratch_shapes=[
            vmem((RING, 2, 4, rows, size), bf16),
            vmem((RING, 4, rows, size), bf16),
            vmem((RING, 3, rows, size), bf16),
            vmem((RING, rows, size), f32),
            vmem((2, 4, rows, size), bf16),
            vmem((2, 4, rows, size), bf16),
            vmem((4, 4, rows, size), bf16),
            vmem((4, rows, size), bf16),
            vmem((2, 2, width, size), bf16),
            vmem((tokens, width), f32),
            vmem((tokens, width), bf16),
            vmem((2, tokens, 3 * LANES), bf16),
            vmem((2, tokens, 3 * LANES), bf16),
            vmem((10, 8, width), f32),
            dma((count, 13)),
            dma((count, 13)),
            dma((15,)),
            dma((count,)),
            dma((10,)),
            dma((2, 2)),
            dma((2,)),
            dma((2,)),
            dma((7,)),
            dma((7,)),
        ],
        compiler_params=pltpu.CompilerParams(
            collective_id=2, has_side_effects=True, vmem_limit_bytes=VMEM_BYTES
        ),
        name="backward",
    )(
        grad_output,
        layer_input,
        gains,
        cosine,
        sine,
        first,
        last,
        *[pack.reshape(2, 4, 2, 2 * rows, lanes) for pack in packs],
        *kept,
    )
    sums, grad_input, gain_sums = outs[:3]
    kv = lanes // 8
    mixed = sums[0]
    return (
        grad_input,
        gain_sums[:2],
        (
            mixed[:, 2 * kv : 5 * kv],
            mixed[:, :kv],
            mixed[:, kv : 2 * kv],
            mixed[:, 5 * kv :].T,
            sums[1],
            sums[2],
            sums[3].T,
        ),
    )


def special():
    return (lax.axis_size("row"), lax.axis_size("col")) == (16, 2)


def lane_of(shape):
    return lax.broadcasted_iota(jnp.int32, shape, len(shape) - 1)


def turn(values, cosine, sine, lower):
    ahead = pltpu.roll(values, LANES - HEAD // 2, 1)
    behind = pltpu.roll(values, HEAD // 2, 1)
    return values * cosine + jnp.where(lower, -ahead, behind) * sine


def turn_back(values, cosine, sine, lower):
    scaled = values * sine
    ahead = pltpu.roll(scaled, LANES - HEAD // 2, 1)
    behind = pltpu.roll(scaled, HEAD // 2, 1)
    return values * cosine - jnp.where(lower, -ahead, behind)


def project_tiles(half, pairs, attn_in_ref, weight_ref, cos_ref, sin_ref, y_ref):
    cosine, sine = cos_ref[...], sin_ref[...]
    lane = lane_of(cosine.shape)
    lower = lane % HEAD < HEAD // 2
    for pair in pairs:
        two = dot_nn(attn_in_ref[...], weight_ref[half, :, pl.ds(pair * 2 * LANES, 2 * LANES)]).astype(bf16)
        for side in range(2):
            tile = 2 * pair + side
            raw = two[:, side * LANES : (side + 1) * LANES].astype(f32)
            if tile == 2:
                out = raw
            else:
                out = turn(raw, cosine, sine, lower)
                if tile == 1:
                    out = jnp.where(lane < HEAD, out, raw)
                elif tile > 2:
                    out = out * HEAD ** (-0.5)
            y_ref[half, :, pl.ds(tile * LANES, LANES)] = out.astype(bf16)


def project_kernel(x_ref, gain_ref, weight_ref, cos_ref, sin_ref, attn_in_ref, y_ref):
    values = x_ref[...].astype(f32)
    inverse = lax.rsqrt(jnp.mean(values * values, axis=1, keepdims=True) + eps)
    attn_in_ref[...] = (values * inverse * gain_ref[...]).astype(bf16)
    for half in range(2):
        project_tiles(half, range(4), attn_in_ref, weight_ref, cos_ref, sin_ref, y_ref)


def head_rows(values, side, lane):
    return jnp.where((lane < HEAD) if side == 0 else (lane >= HEAD), values, jnp.zeros_like(values))


def twice(tile, side, lane):
    values = tile.astype(f32)
    other = pltpu.roll(values, HEAD, 1)
    keep = (lane < HEAD) if side == 0 else (lane >= HEAD)
    return jnp.where(keep, values, other)


def load_groups(kv_ref, half, dup_ref, flip_ref):
    for slot in range(6):
        tile = kv_ref[half, :, pl.ds((slot // 2) * LANES, LANES)]
        both = twice(tile, slot % 2, lane_of(tile.shape))
        dup_ref[slot] = both.astype(bf16)
        flip_ref[slot] = both.T.astype(bf16)


def seen(first_ref, last_ref, rows, keys):
    index = lax.broadcasted_iota(jnp.int32, (keys, rows.size), 0)
    return (index >= first_ref[:, rows]) & (index <= last_ref[:, rows])


def attend_rows(half, step, block, y_ref, dup_ref, flip_ref, first_ref, last_ref, mix_ref, log_ref):
    keys = dup_ref.shape[1]
    lane = lane_of((block, LANES))
    rows = pl.ds(pl.multiple_of(step * block, block), block)
    allowed = seen(first_ref, last_ref, rows, keys)
    previous = jnp.zeros((block, LANES), f32)
    for head in range(9):
        group = head // 3
        query = head_rows(y_ref[half, rows, pl.ds((3 + head // 2) * LANES, LANES)], head % 2, lane)
        scores = jnp.where(allowed, dot_nt(dup_ref[group], query), neg_fill)
        top = jnp.max(scores, axis=0, keepdims=True)
        powers = jnp.exp(scores - top)
        total = jnp.sum(powers, axis=0, keepdims=True)
        probs = (powers * (1.0 / total)).astype(bf16)
        mixed = dot_nn(flip_ref[3 + group], probs).T
        log_ref[half, pl.ds(head, 1), rows] = top + jnp.log(total)
        if head % 2 == 0:
            tile = jnp.where(lane < HEAD, previous, mixed)
            mix_ref[half, rows, pl.ds((head // 2) * LANES, LANES)] = tile.astype(bf16)
        previous = mixed


def attend_kernel(block, y_ref, kv_ref, first_ref, last_ref, mix_ref, log_ref, dup_ref, flip_ref):
    load_groups(kv_ref, 0, dup_ref, flip_ref)

    def rows_of(step, carry):
        attend_rows(0, step, block, y_ref, dup_ref, flip_ref, first_ref, last_ref, mix_ref, log_ref)
        return carry

    lax.fori_loop(0, y_ref.shape[1] // block, rows_of, 0)


def attend_back_rows(
    half, step, block, y_ref, dup_ref, flip_ref, first_ref, last_ref, log_ref, grad_ref, cos_ref, sin_ref, out_ref, acc_ref
):
    keys = dup_ref.shape[1]
    lane = lane_of((block, LANES))
    lower = lane % HEAD < HEAD // 2
    rows = pl.ds(pl.multiple_of(step * block, block), block)
    allowed = seen(first_ref, last_ref, rows, keys)
    previous = None
    for head in range(9):
        group = head // 3
        query = head_rows(y_ref[half, rows, pl.ds((3 + head // 2) * LANES, LANES)], head % 2, lane)
        upstream = head_rows(
            grad_ref[half, rows, pl.ds(((head + 1) // 2) * LANES, LANES)], (head + 1) % 2, lane
        )
        scores = jnp.where(allowed, dot_nt(dup_ref[group], query), neg_fill)
        probs = jnp.exp(scores - log_ref[half, pl.ds(head, 1), rows])
        grad_probs = dot_nt(dup_ref[3 + group], upstream)
        inner = jnp.sum(probs * grad_probs, axis=0, keepdims=True)
        grad_scores = (probs * (grad_probs - inner)).astype(bf16)
        acc_ref[3 + group] += dot_nn(probs.astype(bf16), upstream)
        acc_ref[group] += dot_nn(grad_scores, query)
        grad_query = dot_nn(flip_ref[group], grad_scores).T
        if head % 2 == 1 or head == 8:
            if head == 8:
                tile = jnp.where(lane < HEAD, grad_query, 0.0)
            else:
                tile = jnp.where(lane < HEAD, previous, grad_query)
            tile = turn_back(tile * HEAD ** (-0.5), cos_ref[rows, :], sin_ref[rows, :], lower)
            out_ref[half, rows, pl.ds((3 + head // 2) * LANES, LANES)] = tile.astype(bf16)
        previous = grad_query


def join_groups(acc_ref, out_ref, half):
    lane = lane_of((acc_ref.shape[1], LANES))
    for tile in range(3):
        low, high = acc_ref[2 * tile], acc_ref[2 * tile + 1]
        low = low + pltpu.roll(low, HEAD, 1)
        high = high + pltpu.roll(high, HEAD, 1)
        out_ref[half, :, pl.ds(tile * LANES, LANES)] = jnp.where(lane < HEAD, low, high)


def attend_back_kernel(
    block, y_ref, kv_ref, first_ref, last_ref, log_ref, grad_ref, cos_ref, sin_ref, dq_ref, dkv_ref, dup_ref, flip_ref, acc_ref
):
    load_groups(kv_ref, 0, dup_ref, flip_ref)
    acc_ref[...] = jnp.zeros_like(acc_ref)

    def rows_of(step, carry):
        attend_back_rows(
            0, step, block, y_ref, dup_ref, flip_ref, first_ref, last_ref, log_ref, grad_ref, cos_ref, sin_ref, dq_ref, acc_ref
        )
        return carry

    lax.fori_loop(0, y_ref.shape[1] // block, rows_of, 0)
    join_groups(acc_ref, dkv_ref, 0)


def full_spec(shape):
    return pl.BlockSpec(shape, lambda i: (0,) * len(shape))


def half_spec(shape):
    return pl.BlockSpec((1,) + shape[1:], lambda i: (i,) + (0,) * (len(shape) - 1))


def params():
    return pltpu.CompilerParams(vmem_limit_bytes=VMEM_BYTES)


def project(layer_input, gain, first_pack, cosine, sine):
    tokens, width = layer_input.shape
    vm = pl.BlockSpec(memory_space=pltpu.VMEM)
    return pl.pallas_call(
        project_kernel,
        grid=(1,),
        out_shape=(
            jax.ShapeDtypeStruct((tokens, width), bf16),
            jax.ShapeDtypeStruct((2, tokens, 8 * LANES), bf16),
        ),
        in_specs=[
            full_spec((tokens, width)),
            full_spec((1, width)),
            full_spec((2, width, 8 * LANES)),
            full_spec((tokens, LANES)),
            full_spec((tokens, LANES)),
        ],
        out_specs=(full_spec((tokens, width)), full_spec((2, tokens, 8 * LANES))),
        compiler_params=params(),
        name="project",
    )(layer_input, gain, first_pack, cosine, sine)


def attend(y, kv, first, last):
    tokens, keys = y.shape[1], kv.shape[1]
    block = min(256, tokens)
    return pl.pallas_call(
        lambda *refs: attend_kernel(block, *refs),
        grid=(2,),
        out_shape=(
            jax.ShapeDtypeStruct((2, tokens, 5 * LANES), bf16),
            jax.ShapeDtypeStruct((2, 16, tokens), f32),
        ),
        in_specs=[half_spec(y.shape), half_spec(kv.shape), full_spec((1, tokens)), full_spec((1, tokens))],
        out_specs=(half_spec((2, tokens, 5 * LANES)), half_spec((2, 16, tokens))),
        scratch_shapes=[pltpu.VMEM((6, keys, LANES), bf16), pltpu.VMEM((6, LANES, keys), bf16)],
        compiler_params=params(),
        name="attend",
    )(y, kv, first, last)


def attend_back(y, kv, first, last, logs, grad, cosine, sine):
    tokens, keys = y.shape[1], kv.shape[1]
    block = min(256, tokens)
    return pl.pallas_call(
        lambda *refs: attend_back_kernel(block, *refs),
        grid=(2,),
        out_shape=(
            jax.ShapeDtypeStruct((2, tokens, 8 * LANES), bf16),
            jax.ShapeDtypeStruct((2, keys, 3 * LANES), f32),
        ),
        in_specs=[
            half_spec(y.shape),
            half_spec(kv.shape),
            full_spec((1, tokens)),
            full_spec((1, tokens)),
            half_spec(logs.shape),
            half_spec(grad.shape),
            full_spec((tokens, LANES)),
            full_spec((tokens, LANES)),
        ],
        out_specs=(half_spec((2, tokens, 8 * LANES)), half_spec((2, keys, 3 * LANES))),
        scratch_shapes=[
            pltpu.VMEM((6, keys, LANES), bf16),
            pltpu.VMEM((6, LANES, keys), bf16),
            pltpu.VMEM((6, keys, LANES), f32),
        ],
        compiler_params=params(),
        name="attend_back",
    )(y, kv, first, last, logs, grad, cosine, sine)


def rope_frequency():
    lane_index = (jnp.arange(LANES, dtype=jnp.int32) % (HEAD // 2)).astype(f32)
    return jnp.exp(lane_index * (-2.0 * math.log(rope_base) / HEAD))


def shards(
    layer_input,
    attn_gain,
    mlp_gain,
    query_weight,
    key_weight,
    value_weight,
    out_weight,
    gate_weight,
    up_weight,
    down_weight,
    seq_ids,
    block_ends,
    grad_output,
):
    tokens, width = layer_input.shape
    span = seq_ids.shape[0]
    start = lax.axis_index("col") * tokens
    gains = jnp.stack([attn_gain, mlp_gain]).astype(f32)
    weights = (query_weight, key_weight, value_weight, out_weight, gate_weight, up_weight, down_weight)
    if special():
        mine = jnp.concatenate([key_weight, value_weight, query_weight, out_weight.T], axis=1)
        packs, kept = forward_special(
            layer_input,
            gains,
            rope_frequency()[None, :],
            seq_ids[None, :],
            block_ends[None, :],
            (mine, gate_weight, up_weight, down_weight.T),
        )
        grad_input, gain_sums, weight_sums = backward_special(
            grad_output, layer_input, gains, *kept[10:], packs, kept[:9]
        )
        return (kept[9], grad_input, gain_sums[0], gain_sums[1]) + tuple(weight_sums)
    own = layer_input.astype(f32)
    gain_one, gain_two = gains[:1], gains[1:]
    index = start + jnp.arange(tokens, dtype=jnp.int32)
    length = jnp.sum(1 - (seq_ids & 1))
    own_first = jnp.where(index < length, 0, length)
    own_last = lax.dynamic_slice_in_dim(block_ends, start, tokens) - lax.axis_index("row") * span
    angles = (index - own_first).astype(f32)[:, None] * rope_frequency()[None, :]
    cosine, sine = jnp.cos(angles), jnp.sin(angles)
    own_first, own_last = own_first[None, :], own_last[None, :]
    pack_first, pack_gate, pack_up, pack_down = gather_any(weights)
    attn_in, y = project(layer_input, gain_one, pack_first, cosine, sine)
    kv = lax.all_gather(y[:, :, : 3 * LANES], "col", axis=1, tiled=True)
    mix, logs = attend(y, kv, own_first, own_last)
    pack_out = pack_first[:, :, 7 * LANES :]
    branch = jnp.einsum("htq,hdq->td", mix, pack_out, preferred_element_type=f32)
    residual = own + branch
    inv_two = lax.rsqrt(jnp.mean(residual * residual, axis=1, keepdims=True) + eps)
    normed_two = residual * inv_two
    mlp_in = (normed_two * gain_two).astype(bf16)
    gate_act = jnp.einsum("td,hdf->htf", mlp_in, pack_gate, preferred_element_type=f32)
    up_act = jnp.einsum("td,hdf->htf", mlp_in, pack_up, preferred_element_type=f32)
    hidden = (jax.nn.silu(gate_act) * up_act).astype(bf16)
    layer_output = (
        residual + jnp.einsum("htf,hdf->td", hidden, pack_down, preferred_element_type=f32)
    ).astype(bf16)
    grad_down = jnp.einsum("td,htf->hdf", grad_output, hidden, preferred_element_type=f32).astype(bf16)
    grad_hidden = jnp.einsum("td,hdf->htf", grad_output, pack_down, preferred_element_type=f32)
    sigmoid = jax.nn.sigmoid(gate_act)
    grad_gate_act = (grad_hidden * up_act * sigmoid * (1.0 + gate_act * (1.0 - sigmoid))).astype(bf16)
    grad_up_act = (grad_hidden * gate_act * sigmoid).astype(bf16)
    grad_gate = jnp.einsum("td,htf->hdf", mlp_in, grad_gate_act, preferred_element_type=f32).astype(bf16)
    grad_up = jnp.einsum("td,htf->hdf", mlp_in, grad_up_act, preferred_element_type=f32).astype(bf16)
    grad_mlp_in = jnp.einsum(
        "htf,hdf->td", grad_gate_act, pack_gate, preferred_element_type=f32
    ) + jnp.einsum("htf,hdf->td", grad_up_act, pack_up, preferred_element_type=f32)
    scaled_two = grad_mlp_in * gain_two
    inner_two = jnp.mean(scaled_two * normed_two, axis=1, keepdims=True)
    grad_residual = grad_output.astype(f32) + inv_two * (scaled_two - normed_two * inner_two)
    grad_mlp_gain = jnp.sum(grad_mlp_in * normed_two, axis=0)
    grad_branch = grad_residual.astype(bf16)
    grad_mixture = jnp.einsum("td,hdq->htq", grad_branch, pack_out, preferred_element_type=f32).astype(bf16)
    grad_q, grad_kv = attend_back(y, kv, own_first, own_last, logs, grad_mixture, cosine, sine)
    grad_kv = lax.psum_scatter(grad_kv, "col", scatter_dimension=1, tiled=True)
    key_cos, key_sin = jnp.tile(cosine, (1, 3)), jnp.tile(sine, (1, 3))
    lane = jnp.arange(3 * LANES, dtype=jnp.int32)
    is_key = lane < 3 * HEAD
    scaled = grad_kv * key_sin
    turned = jnp.where(
        lane % HEAD < HEAD // 2, -jnp.roll(scaled, -(HEAD // 2), axis=2), jnp.roll(scaled, HEAD // 2, axis=2)
    )
    grad_kv = jnp.where(is_key, grad_kv * key_cos - turned, grad_kv).astype(bf16)
    grad_y = jnp.concatenate([grad_kv, grad_q[:, :, 3 * LANES :]], axis=2)
    grad_proj = jnp.einsum("td,htf->hdf", attn_in, grad_y, preferred_element_type=f32)
    grad_out = jnp.einsum("td,htq->hdq", grad_branch, mix, preferred_element_type=f32)
    grad_first = jnp.concatenate(
        [
            grad_proj[:, :, : 7 * LANES],
            grad_proj[:, :, 7 * LANES :] + grad_out[:, :, :LANES],
            grad_out[:, :, LANES:],
        ],
        axis=2,
    ).astype(bf16)
    grad_attn_in = jnp.einsum(
        "htf,hdf->td", grad_y, pack_first[:, :, : 8 * LANES], preferred_element_type=f32
    )
    inv_one = lax.rsqrt(jnp.mean(own * own, axis=1, keepdims=True) + eps)
    normed_one = own * inv_one
    scaled_one = grad_attn_in * gain_one
    inner_one = jnp.mean(scaled_one * normed_one, axis=1, keepdims=True)
    grad_input = (grad_residual + inv_one * (scaled_one - normed_one * inner_one)).astype(bf16)
    grad_attn_gain = jnp.sum(grad_attn_in * normed_one, axis=0)
    gain_sums, weight_sums = scatter_any(
        (grad_first, grad_gate, grad_up, grad_down), jnp.stack([grad_attn_gain, grad_mlp_gain])
    )
    return (layer_output, grad_input, gain_sums[0], gain_sums[1]) + tuple(weight_sums)


def solution(mesh):
    tokens_spec = P(("row", "col"), None)
    in_specs = (
        tokens_spec,
        P(),
        P(),
        P("row", "col"),
        P("row", "col"),
        P("row", "col"),
        P("col", "row"),
        P("row", "col"),
        P("row", "col"),
        P("col", "row"),
        P("row"),
        P("row"),
        tokens_spec,
    )
    out_specs = (
        tokens_spec,
        tokens_spec,
        P(),
        P(),
        P("row", "col"),
        P("row", "col"),
        P("row", "col"),
        P("col", "row"),
        P("row", "col"),
        P("row", "col"),
        P("col", "row"),
    )
    return jax.shard_map(shards, mesh=mesh, in_specs=in_specs, out_specs=out_specs, check_vma=False)
```
